32 devices in a mesh: dp: 32 (over z, y, x, core).
Axes of the slice: x: 2, y: 2, z: 4, core: 2. Of those that a mesh axis runs over, the one named last changes fastest.
Arguments:
- tokens: bfloat16 [2, 4096, 896], P(None, 'dp'), may hold values from -6 to 6
- positions: int32 [2, 4096], P(None, 'dp'), may hold values from 0 to 127, as said below
- cotangent: bfloat16 [2, 4096, 896], P(None, 'dp'), may hold values from -6 to 6
- norm_attn: bfloat16 [896], P('dp'), may hold values from 0.099609375 to 1.8984375
- w_query: bfloat16 [802816], P('dp'), may hold values from -0.1875 to 0.1875
- b_query: bfloat16 [896], P('dp'), may hold values from -3 to 3
- w_key: bfloat16 [114688], P('dp'), may hold values from -0.1875 to 0.1875
- b_key: bfloat16 [128], replicated, may hold values from -3 to 3
- w_value: bfloat16 [114688], P('dp'), may hold values from -0.1875 to 0.1875
- b_value: bfloat16 [128], P('dp'), may hold values from -3 to 3
- w_out: bfloat16 [802816], P('dp'), may hold values from -1.5 to 1.5
- norm_ffn: bfloat16 [896], P('dp'), may hold values from 0.099609375 to 1.8984375
- w_gate: bfloat16 [4358144], P('dp'), may hold values from -0.1875 to 0.1875
- w_up: bfloat16 [4358144], P('dp'), may hold values from -0.1875 to 0.1875
- w_down: bfloat16 [4358144], P('dp'), may hold values from -0.078125 to 0.078125
Outputs:
- block_out: bfloat16 [2, 4096, 896], P(None, 'dp')
- grad_input: bfloat16 [2, 4096, 896], P(None, 'dp')
- grad_norm_attn: float32 [896], P('dp')
- grad_query: float32 [802816], P('dp')
- grad_bquery: float32 [896], P('dp')
- grad_key: float32 [114688], P('dp')
- grad_bkey: float32 [128], replicated
- grad_value: float32 [114688], P('dp')
- grad_bvalue: float32 [128], P('dp')
- grad_out: float32 [802816], P('dp')
- grad_norm_ffn: float32 [896], P('dp')
- grad_gate: float32 [4358144], P('dp')
- grad_up: float32 [4358144], P('dp')
- grad_down: float32 [4358144], P('dp')
The draws below stay inside these ranges and needn't reach their ends.
Inputs may be any that keep to these rules, and one draw needn't show every extreme that they name: `positions`: within each block of 128 tokens of one micro-batch the first position is 0; from token to token a position either rises by one (same sequence) or is 0 (a new sequence begins).
All inputs are finite; a program needn't handle non-finite values.
Results may differ from the reference program's by a relative error of at most 0.023.
Values may be sent and summed in bfloat16 or wider, within the bound.
A program may use at most 256 MiB of HBM per device.

```python
import jax
import jax.numpy as jnp
from jax import lax

D = 896
FF = 4864
HEADS = 14
KV_HEADS = 2
HEAD_DIM = 64
SLOTS = 128
MICRO = 2
TOKENS = 4096


def draw_positions(key, part):
    blocks = MICRO * (TOKENS // SLOTS)
    rate_bits = jax.random.randint(jax.random.fold_in(key, 31), (blocks, 1), 6, 10)
    spacing = jnp.left_shift(jnp.ones_like(rate_bits), rate_bits)
    raw_bits = jax.random.randint(jax.random.fold_in(key, 32), (blocks, SLOTS), 0, 1 << 20)
    column = jnp.arange(SLOTS, dtype=jnp.int32)
    row_number = jnp.arange(blocks, dtype=jnp.int32)
    restart = (raw_bits % spacing == 0) & (column[None, :] > 0) & (row_number[:, None] % 4 != 0)
    seq_start = lax.cummax(jnp.where(restart, column[None, :], 0), axis=1)
    return (column[None, :] - seq_start).reshape(MICRO, TOKENS).astype(jnp.int32)


def spiked(values, stream_key, source, target, shards_of, factor):
    def block_of(position):
        return (jnp.arange(values.shape[position]) // (values.shape[position] // shards_of)).reshape((-1,) + (1,) * (values.ndim - 1 - position))

    first = jax.random.permutation(stream_key, shards_of)[block_of(target)]
    other_side = (block_of(target) + shards_of // 2) % shards_of
    return jnp.where((block_of(source) == first) | (block_of(source) == other_side), factor * values, values)


def level_of(own_key, extent, cuts, smallest, top_value):
    def one(dim, shards_of):
        draws = jax.random.uniform(jax.random.fold_in(jax.random.fold_in(own_key, 6), dim), (shards_of,), jnp.float32, smallest / len(cuts), top_value / len(cuts))
        return jnp.repeat(jnp.exp(draws), extent[dim] // shards_of).reshape((-1,) + (1,) * (len(extent) - dim - 1))

    loudness = one(*cuts[0])
    for cut in cuts[1:]:
        loudness = loudness * one(*cut)
    return loudness


def centred(stream_key, extent, deviation, reach, cuts=(), kind=jnp.bfloat16):
    values = deviation * jax.random.normal(stream_key, extent, jnp.float32)
    if cuts:
        values = values * level_of(stream_key, extent, cuts, -0.22, 0.18)
    return jnp.clip(values, -reach, reach).astype(kind)


def gaussian_with(stream_key, dims, width, most, cuts, heavy, kind=jnp.bfloat16):
    values = width * jax.random.normal(stream_key, dims, jnp.float32)
    if cuts:
        values = values * level_of(stream_key, dims, cuts, -0.22, 0.18)
    return jnp.clip(spiked(values, jax.random.fold_in(stream_key, 3), *heavy), -most, most).astype(kind)


def setup_inputs(seed: int = 0) -> dict:
    key_of = jax.random.split(jax.random.key(seed), 16)
    tokens = gaussian_with(key_of[0], (MICRO, TOKENS, D), 1.0, 6.0, ((1, 32),), (1, 2, 32, 2.75))
    positions = draw_positions(jax.random.fold_in(key_of[15], 71), 0)
    cotangent = centred(key_of[2], (MICRO, TOKENS, D), 1.0, 6.0, ((1, 32),))
    norm_attn = jnp.clip(1.0 + 0.18 * jax.random.normal(key_of[3], (D,), jnp.float32), 0.099609375, 1.8984375).astype(jnp.bfloat16)
    w_query = centred(key_of[4], (D * HEADS * HEAD_DIM,), D ** -0.5, 0.1875, ((0, 32),))
    b_query = centred(key_of[5], (HEADS * HEAD_DIM,), 0.5, 3.0, ((0, 32),))
    w_key = centred(key_of[6], (D * KV_HEADS * HEAD_DIM,), D ** -0.5, 0.1875, ((0, 32),))
    b_key = centred(key_of[7], (KV_HEADS * HEAD_DIM,), 0.5, 3.0)
    w_value = centred(key_of[8], (D * KV_HEADS * HEAD_DIM,), D ** -0.5, 0.1875, ((0, 32),))
    b_value = centred(key_of[9], (KV_HEADS * HEAD_DIM,), 0.5, 3.0, ((0, 32),))
    w_out = centred(key_of[10], (HEADS * HEAD_DIM * D,), (HEADS * HEAD_DIM // 64) ** -0.5, 1.5, ((0, 32),))
    norm_ffn = jnp.clip(1.0 + 0.18 * jax.random.normal(key_of[11], (D,), jnp.float32), 0.099609375, 1.8984375).astype(jnp.bfloat16)
    w_gate = centred(key_of[12], (D * FF,), D ** -0.5, 0.1875, ((0, 32),))
    w_up = centred(key_of[13], (D * FF,), D ** -0.5, 0.1875, ((0, 32),))
    w_down = centred(key_of[14], (FF * D,), FF ** -0.5, 0.078125, ((0, 32),))
    return {"tokens": tokens, "positions": positions, "cotangent": cotangent, "norm_attn": norm_attn, "w_query": w_query, "b_query": b_query, "w_key": w_key, "b_key": b_key, "w_value": w_value, "b_value": b_value, "w_out": w_out, "norm_ffn": norm_ffn, "w_gate": w_gate, "w_up": w_up, "w_down": w_down}


@jax.custom_vjp
def low(v):
    return lax.optimization_barrier(v.astype(jnp.bfloat16)).astype(jnp.float32)

@jax.custom_vjp
def low_back(v):
    return v

def low_keep(v):
    return (low(v), None)

def low_pass(kept, grad):
    return (grad,)

def back_keep(v):
    return (v, None)

def back_low(kept, grad):
    return (low(grad),)
low.defvjp(low_keep, low_pass)
low_back.defvjp(back_keep, back_low)

def rms_scale(field):
    return lax.rsqrt(lax.optimization_barrier(jnp.mean(field * field, axis=-1, keepdims=True)) + 1e-06)

def matmul(left, right):
    return jnp.dot(left, right, precision=lax.Precision.HIGHEST)

def rope_tables(positions):
    half_dim = HEAD_DIM // 2
    inv_freq = 1000000.0 ** (-(jnp.arange(half_dim).astype(jnp.float32) * 2.0 / HEAD_DIM))
    angles = positions.astype(jnp.float32)[:, None] * inv_freq[None, :]
    angles = jnp.concatenate([angles, angles], axis=-1)
    return (jnp.cos(angles)[:, None, :], jnp.sin(angles)[:, None, :])

def rotate(field, cosine, sine_table):
    half_dim = HEAD_DIM // 2
    turned = jnp.concatenate([-field[..., half_dim:], field[..., :half_dim]], axis=-1)
    return field * cosine + turned * sine_table

def attention_mask(positions):
    row_index = jnp.arange(SLOTS, dtype=jnp.int32)
    seq_start = row_index - positions.astype(jnp.int32)
    return (seq_start[:, None] == seq_start[None, :]) & (row_index[:, None] >= row_index[None, :])

def block_forward(params, block_in, positions):
    norm_attn, w_query, b_query, w_key, b_key, w_value, b_value, w_out, norm_ffn, w_gate, w_up, w_down = params
    w_query = w_query.reshape(D, HEADS * HEAD_DIM)
    w_key = w_key.reshape(D, KV_HEADS * HEAD_DIM)
    w_value = w_value.reshape(D, KV_HEADS * HEAD_DIM)
    w_out = w_out.reshape(HEADS * HEAD_DIM, D)
    w_gate = w_gate.reshape(D, FF)
    w_up = w_up.reshape(D, FF)
    w_down = w_down.reshape(FF, D)
    group_size = HEADS // KV_HEADS
    normed = low(block_in * rms_scale(block_in) * norm_attn)
    query_lin = low_back(matmul(normed, w_query) + b_query)
    key_lin = low_back(matmul(normed, w_key) + b_key)
    value_lin = low_back(matmul(normed, w_value) + b_value)
    cosine, sine_table = rope_tables(positions)
    query = low(rotate(query_lin.reshape(SLOTS, HEADS, HEAD_DIM), cosine, sine_table))
    key_rot = low(rotate(key_lin.reshape(SLOTS, KV_HEADS, HEAD_DIM), cosine, sine_table))
    values = low(value_lin.reshape(SLOTS, KV_HEADS, HEAD_DIM))
    query = query.reshape(SLOTS, KV_HEADS, group_size, HEAD_DIM)
    scores = low_back(jnp.einsum('qhgd,khd->hgqk', query, key_rot, precision=lax.Precision.HIGHEST) * 0.125)
    allowed = attention_mask(positions)
    scores = jnp.where(allowed[None, None], scores, -1e+30)
    row_max = lax.optimization_barrier(jnp.max(scores, axis=-1, keepdims=True))
    expo = jnp.exp(scores - row_max)
    row_sum = lax.optimization_barrier(jnp.sum(expo, axis=-1, keepdims=True))
    attn_probs = low(expo / row_sum)
    mixed = jnp.einsum('hgqk,khd->qhgd', attn_probs, values, precision=lax.Precision.HIGHEST)
    mixed = low(low_back(mixed.reshape(SLOTS, HEADS * HEAD_DIM)))
    hidden = block_in + low_back(matmul(mixed, w_out))
    normed_ffn = low(hidden * rms_scale(hidden) * norm_ffn)
    gate_pre = low_back(matmul(normed_ffn, w_gate))
    up_pre = low_back(matmul(normed_ffn, w_up))
    hidden_act = low(jax.nn.silu(gate_pre) * up_pre)
    return hidden + low_back(matmul(hidden_act, w_down))

def reference(tokens, positions, cotangent, norm_attn, w_query, b_query, w_key, b_key, w_value, b_value, w_out, norm_ffn, w_gate, w_up, w_down):
    params = jax.tree.map(lambda weight: weight.astype(jnp.float32), (norm_attn, w_query, b_query, w_key, b_key, w_value, b_value, w_out, norm_ffn, w_gate, w_up, w_down))
    count = MICRO * (TOKENS // SLOTS)
    inputs = tokens.astype(jnp.float32).reshape(count, SLOTS, D)
    spots = positions.reshape(count, SLOTS)
    grads_in = cotangent.astype(jnp.float32).reshape(count, SLOTS, D)

    def one_block(running, pieces):
        block_in, block_pos, block_grad = pieces
        result, pullback = jax.vjp(lambda weights, field: block_forward(weights, field, block_pos), params, block_in)
        weight_grads, input_grad = pullback(block_grad)
        running = jax.tree.map(jnp.add, running, weight_grads)
        return (running, (result, input_grad))
    zeros = jax.tree.map(jnp.zeros_like, params)
    sums, (outputs, input_grads) = lax.scan(one_block, zeros, (inputs, spots, grads_in))
    outputs = outputs.reshape(MICRO, TOKENS, D).astype(jnp.bfloat16)
    input_grads = input_grads.reshape(MICRO, TOKENS, D).astype(jnp.bfloat16)
    return (outputs, input_grads, sums[0], sums[1], sums[2], sums[3], sums[4], sums[5], sums[6], sums[7], sums[8], sums[9], sums[10], sums[11])
```

```python
import functools

import jax
import jax.numpy as jnp
from jax import lax
from jax.experimental import pallas as pl
from jax.experimental.pallas import tpu as pltpu
from jax.sharding import PartitionSpec as P

HEADS = 14
KV_HEADS = 2
HEAD_DIM = 64
GROUP = HEADS // KV_HEADS
PLANE = 8
CHIPS = 4
LANES = 128
FIELD = 32
MESH = pl.DeviceIdType.MESH
F32 = jnp.float32
BF16 = jnp.bfloat16


def up(value, step):
    return -(-value // step) * step


def mm(left, right, dims=((1,), (0,))):
    return lax.dot_general(left, right, (dims, ((), ())), preferred_element_type=F32)


def mm_nt(left, right):
    return mm(left, right, ((1,), (1,)))


def mm_tn(left, right):
    return mm(left, right, ((0,), (0,)))


def split_mm(left, right, nt=False):
    high = left.astype(BF16)
    low = (left - high.astype(F32)).astype(BF16)
    dot = mm_nt if nt else mm
    return dot(high, right) + dot(low, right)


def iota(shape, dim):
    return lax.broadcasted_iota(jnp.int32, shape, dim)


class Dims:
    def __init__(self, n, d, ff, slots, micro):
        self.n, self.d, self.ff = n, d, ff
        self.planes = n // PLANE
        self.rows = d // n
        self.rp = 8
        while self.rp < self.rows + 1:
            self.rp *= 2
        self.dp = n * self.rp
        self.rf = ff // n
        self.ffr = up(ff // PLANE, LANES)
        self.rfp = self.ffr // self.planes
        self.slots, self.micro = slots, micro
        self.tok = slots * micro
        self.heads = HEADS * HEAD_DIM
        self.kv = KV_HEADS * HEAD_DIM
        self.qkv = self.heads + 2 * self.kv
        self.wide = self.qkv + d
        self.rv = self.kv // n


def spread_matrix(dm):
    shape = (dm.d, dm.dp)
    row, col = iota(shape, 0), iota(shape, 1)
    inner = col & (dm.rp - 1)
    hit = (row == (col // dm.rp) * dm.rows + inner) & (inner < dm.rows)
    return jnp.where(hit, 1.0, 0.0).astype(BF16)


def field_matrix(dm, offset):
    shape = (LANES, dm.dp)
    row, col = iota(shape, 0), iota(shape, 1)
    inner = col & (dm.rp - 1)
    return jnp.where((row == offset + inner) & (inner < dm.rows), 1.0, 0.0).astype(BF16)


def own_block(dm):
    shape = (dm.n, dm.dp)
    return iota(shape, 1) // dm.rp == iota(shape, 0)


def spare_rows(dm):
    shape = (dm.n, dm.dp)
    return jnp.where(iota(shape, 1) == iota(shape, 0) * dm.rp + dm.rows, 1.0, 0.0).astype(BF16)


def value_field(dm):
    shape = (LANES, LANES)
    return jnp.where(
        iota(shape, 0) == 3 * FIELD + (iota(shape, 1) & (dm.rv - 1)), 1.0, 0.0
    ).astype(BF16)


def value_block(dm):
    shape = (dm.n, LANES)
    return iota(shape, 1) // dm.rv == iota(shape, 0)


def half_turn(field):
    width = field.shape[-1]
    first = (iota(field.shape, 1) & (HEAD_DIM - 1)) < HEAD_DIM // 2
    ahead = pltpu.roll(field, width - HEAD_DIM // 2, 1)
    behind = pltpu.roll(field, HEAD_DIM // 2, 1)
    return first, ahead, behind


def twice(field):
    low = iota(field.shape, 1) < HEAD_DIM
    turned = pltpu.roll(field, HEAD_DIM, 1)
    return jnp.where(low, field, turned), jnp.where(low, turned, field)


class Refs:
    def __init__(self, names, refs):
        self.__dict__.update(zip(names, refs, strict=True))


def layer_kernel(dm, names, *refs):
    b = Refs(names, refs)
    n, planes = dm.n, dm.planes
    me = lax.axis_index("dp")
    r, p = me // PLANE, me % PLANE
    q, c = p // 2, p % 2
    other = 1 - c
    partner = r * PLANE + q * 2 + other

    def dev(plane, place):
        return (plane * PLANE + place,)

    barrier = pltpu.get_barrier_semaphore()
    peers = [dev(r, (p + k) % PLANE) for k in range(1, PLANE)]
    peers += [dev((r + k) % planes, p) for k in range(1, planes)]
    for peer in peers:
        pl.semaphore_signal(barrier, inc=1, device_id=peer, device_id_type=MESH)
    pl.semaphore_wait(barrier, len(peers))

    pending = []
    count = [0]

    def send(src, dst, arrive, to):
        copy = pltpu.make_async_remote_copy(
            src_ref=src,
            dst_ref=dst,
            send_sem=b.ssem.at[count[0]],
            recv_sem=arrive,
            device_id=to,
            device_id_type=MESH,
        )
        copy.start()
        count[0] += 1
        pending.append(copy)

    def drain():
        for copy in pending:
            copy.wait_send()
        pending.clear()

    def arrived(dst, arrive):
        pltpu.make_async_remote_copy(
            src_ref=dst,
            dst_ref=dst,
            send_sem=b.ssem.at[0],
            recv_sem=arrive,
            device_id=(partner,),
            device_id_type=MESH,
        ).wait_recv()

    def block(ref, index):
        return ref.at[index // 2, index % 2]

    def plane_rows(ref, plane):
        return ref.at[pl.ds(plane * PLANE, PLANE)]

    keep = [
        pltpu.make_async_copy(b.ap, block(b.W, me), b.csem.at[0]),
        pltpu.make_async_copy(b.gus.at[p], b.GU.at[me], b.csem.at[1]),
        pltpu.make_async_copy(b.g, b.gA.at[p], b.csem.at[2]),
    ]
    for copy in keep:
        copy.start()

    for k in range(1, planes):
        send(b.ap, block(b.W, me), b.rA.at[me], dev((r + k) % planes, p))

    def fan(index, src, k_list=(1, 2, 3)):
        for k in k_list:
            send(src, block(b.W, index), b.rA.at[index], dev(r, ((q + k) % CHIPS) * 2 + c))

    fan(me, b.ap)
    send(b.ap, block(b.W, me), b.rA.at[me], (partner,))
    for k in range(1, PLANE):
        send(b.gus.at[(p + k) % PLANE], b.GU.at[me], b.rGU.at[p], dev(r, (p + k) % PLANE))
    for k in range(1, planes):
        send(b.wds, b.WDz.at[r], b.rWZ.at[r], dev((r + k) % planes, p))

    tok = dm.tok
    xf = b.x[...].astype(F32)
    scale1 = lax.rsqrt(jnp.mean(xf * xf, axis=-1, keepdims=True) + 1e-06)
    angle = b.posc[...].astype(F32) * b.freq[...]
    b.tabs[0] = jnp.cos(angle)
    b.tabs[1] = jnp.sin(angle)
    b.spr[...] = spread_matrix(dm)

    for k in range(1, planes):
        index = ((r + planes - k) % planes) * PLANE + p
        arrived(block(b.W, index), b.rA.at[index])
        fan(index, block(b.W, index))
        send(block(b.W, index), block(b.W, index), b.rA.at[index], (partner,))
    for k in range(1, PLANE):
        origin = (p + PLANE - k) % PLANE
        arrived(b.GU.at[r * PLANE + origin], b.rGU.at[origin])
    keep[1].wait()
    for k in range(1, planes):
        send(
            plane_rows(b.GU, r),
            plane_rows(b.GU, r),
            b.rGZ.at[r],
            dev((r + k) % planes, p),
        )
    for k in range(1, CHIPS):
        for shift in range(planes):
            index = ((r + planes - shift) % planes) * PLANE + ((q + CHIPS - k) % CHIPS) * 2 + c
            arrived(block(b.W, index), b.rA.at[index])
            send(block(b.W, index), block(b.W, index), b.rA.at[index], (partner,))
    for k in range(1, CHIPS):
        send(b.g, b.gA.at[p], b.rG.at[p], dev(r, ((q + k) % CHIPS) * 2 + c))
    send(b.g, b.gA.at[p], b.rG.at[p], (partner,))

    def down_route(shift):
        origin = (r + planes - shift) % planes
        whole = origin * PLANE + p
        src = b.wds if shift == 0 else b.WDz.at[origin]
        return origin, whole // planes, whole % planes, src

    def down_copy(shift):
        origin, rank, slot, src = down_route(shift)
        return pltpu.make_async_remote_copy(
            src_ref=src,
            dst_ref=b.WD.at[slot],
            send_sem=b.wsem.at[shift],
            recv_sem=b.rWD.at[slot],
            device_id=dev(r, rank),
            device_id_type=MESH,
        )

    for shift in range(planes):
        origin, rank, slot, src = down_route(shift)
        if shift:
            arrived(b.WDz.at[origin], b.rWZ.at[origin])

        @pl.when(rank == p)
        def _():
            pltpu.make_async_copy(src, b.WD.at[slot], b.rWD.at[slot]).start()

        @pl.when(rank != p)
        def _():
            down_copy(shift).start()

    keep[0].wait()
    for k in range(CHIPS):
        for shift in range(planes):
            index = ((r + planes - shift) % planes) * PLANE + ((q + CHIPS - k) % CHIPS) * 2 + other
            arrived(block(b.W, index), b.rA.at[index])

    W = b.W.reshape(dm.dp, dm.wide)
    small = mm(spare_rows(dm), W[:, :LANES]).astype(BF16)
    mine = own_block(dm)
    rows8 = iota((8, dm.dp), 0)
    padded = jnp.zeros((8, dm.dp), F32)
    for i in range(3):
        piece = mm(small, field_matrix(dm, i * FIELD))
        piece = jnp.sum(jnp.where(mine, piece, 0.0), axis=0, keepdims=True)
        padded = jnp.where(rows8 == i, piece, padded)
    b.vec[...] = mm_nt(padded.astype(BF16), b.spr[...])
    gain1, bias_q, gain2 = b.vec[0:1], b.vec[1:2], b.vec[2:3]
    bias_v = jnp.sum(
        jnp.where(value_block(dm), mm(small, value_field(dm)), 0.0), axis=0, keepdims=True
    )
    bias_k = b.bkey[...].astype(F32)

    normed = (xf * scale1 * gain1).astype(BF16)
    b.npad[...] = mm(normed, b.spr[...]).astype(BF16)
    lin = mm(b.npad[...], W[:, : dm.qkv])
    turn_in = jnp.concatenate([lin[:, : dm.heads] + bias_q, lin[:, dm.heads : dm.heads + dm.kv] + bias_k], axis=1)
    reps = (dm.heads + dm.kv) // LANES
    cosine = jnp.concatenate([b.tabs[0]] * reps, axis=1)
    sine = jnp.concatenate([b.tabs[1]] * reps, axis=1)
    first, ahead, behind = half_turn(turn_in)
    turned = turn_in * cosine + jnp.where(first, -ahead, behind) * sine
    values = lin[:, dm.heads + dm.kv :] + bias_v
    for i, piece in enumerate(twice(turned[:, dm.heads :])):
        b.kd[i] = piece.astype(BF16)
    for i, piece in enumerate(twice(values)):
        b.vd[i] = piece.astype(BF16)
    low = iota((dm.slots, LANES), 1) < HEAD_DIM

    def stack_heads(field, store):
        for h in range(HEADS):
            part = field[:, LANES * (h // 2) : LANES * (h // 2) + LANES]
            part = jnp.where(low if h % 2 == 0 else ~low, part, 0.0)
            store[h * dm.slots : (h + 1) * dm.slots, :] = part.astype(BF16)

    span = GROUP * dm.slots
    for m in range(dm.micro):
        here = slice(m * dm.slots, (m + 1) * dm.slots)
        stack_heads(turned[here, : dm.heads], b.QS.at[m])
        grid = (dm.slots, dm.slots)
        start_row = iota((dm.slots, 1), 0) - b.posc[here]
        start_col = iota((1, dm.slots), 1) - b.posr[m : m + 1]
        allowed = (start_row == start_col) & (iota(grid, 1) <= iota(grid, 0))
        for kv in range(KV_HEADS):
            rows = slice(kv * span, (kv + 1) * span)
            score = mm_nt(b.QS[m, rows], b.kd[kv, here]) * 0.125
            score = jnp.where(allowed[None], score.reshape(GROUP, *grid), -1e30)
            top = jnp.max(score, axis=-1, keepdims=True)
            expo = jnp.exp(score - top)
            prob = expo / jnp.sum(expo, axis=-1, keepdims=True)
            prob = prob.reshape(span, dm.slots)
            b.PF[m, rows] = prob
            b.DMS[rows] = mm(prob.astype(BF16), b.vd[kv, here]).astype(BF16)
        for t in range(HEADS // 2):
            even = b.DMS[2 * t * dm.slots : (2 * t + 1) * dm.slots]
            odd = b.DMS[(2 * t + 1) * dm.slots : (2 * t + 2) * dm.slots]
            b.mix[here, t * LANES : (t + 1) * LANES] = jnp.where(low, even, odd)
    b.mpad[...] = mm(b.mix[...], b.spr[...]).astype(BF16)
    hidden = xf + mm(b.mpad[...], W[:, dm.qkv :])
    b.hid[...] = hidden
    scale2 = lax.rsqrt(jnp.mean(hidden * hidden, axis=-1, keepdims=True) + 1e-06)
    nf = (hidden * scale2 * gain2).astype(BF16)
    b.nfA[p] = mm(nf, b.spr[...]).astype(BF16)

    for k in range(1, CHIPS):
        send(b.nfA.at[p], b.nfA.at[p], b.rNF.at[p], dev(r, ((q + k) % CHIPS) * 2 + c))
    send(b.nfA.at[p], b.nfA.at[p], b.rNF.at[p], (partner,))
    for k in range(1, CHIPS):
        place = ((q + CHIPS - k) % CHIPS) * 2 + c
        arrived(b.gA.at[place], b.rG.at[place])
        send(b.gA.at[place], b.gA.at[place], b.rG.at[place], (partner,))
    for k in range(1, CHIPS):
        place = ((q + CHIPS - k) % CHIPS) * 2 + c
        arrived(b.nfA.at[place], b.rNF.at[place])
        send(b.nfA.at[place], b.nfA.at[place], b.rNF.at[place], (partner,))
    for k in range(1, planes):
        origin = (r + planes - k) % planes
        arrived(plane_rows(b.GU, origin), b.rGZ.at[origin])
    for slot in range(planes):
        arrived(b.WD.at[slot], b.rWD.at[slot])
    keep[2].wait()
    for k in range(CHIPS):
        place = ((q + CHIPS - k) % CHIPS) * 2 + other
        arrived(b.gA.at[place], b.rG.at[place])
        arrived(b.nfA.at[place], b.rNF.at[place])

    GU = b.GU.reshape(dm.dp, 2 * dm.ffr)
    WD = b.WD.reshape(dm.ffr, dm.d)
    BIG = b.BIG.reshape(dm.dp, 4 * dm.ffr)
    half = PLANE // 2

    def feed(place_q, place_c, slot):
        place = place_q * 2 + place_c
        nf_t, g_t = b.nfA[place], b.gA[place]
        pre = mm(nf_t, GU[...])
        gate, upper = pre[:, : dm.ffr], pre[:, dm.ffr :]
        sigma = jax.nn.sigmoid(gate)
        silu = gate * sigma
        act = (silu * upper).astype(BF16)
        b.act[pl.ds(pl.multiple_of(place * tok, tok), tok), :] = act
        b.oP[place_q, place_c] = mm(act, WD[...]).astype(BF16)
        d_act = mm_nt(g_t, WD[...])
        d_gate = (d_act * upper * (sigma + silu * (1.0 - sigma))).astype(BF16)
        d_up = (d_act * silu).astype(BF16)
        d_both = jnp.concatenate([d_gate, d_up], axis=1)
        rows = pl.ds(pl.multiple_of((place % half) * tok, tok), tok)
        cols = pl.ds(pl.multiple_of((place // half) * 2 * dm.ffr, LANES), 2 * dm.ffr)
        BIG[rows, cols] = d_both
        b.dP[place_q, place_c] = mm_nt(d_both, GU[...]).astype(BF16)

    def first_copy(where, part, landing, sems, arrive):
        return pltpu.make_async_remote_copy(
            src_ref=part.at[where, other],
            dst_ref=landing.at[where],
            send_sem=sems.at[where],
            recv_sem=arrive.at[where],
            device_id=(partner,),
            device_id_type=MESH,
        )

    @pl.loop(0, CHIPS)
    def _(step):
        where = (q + step) % CHIPS

        @pl.loop(0, 2)
        def _(turn):
            feed(where, (other + turn) % 2, step)

            @pl.when(turn == 0)
            def _():
                first_copy(where, b.oP, b.oR1, b.osem, b.rO1).start()
                first_copy(where, b.dP, b.dR1, b.dsem, b.rD1).start()

    for k in (1, 2, 3, 0):
        where = (q + k) % CHIPS
        arrived(b.oR1.at[where], b.rO1.at[where])
        b.oP[where, c] = (b.oP[where, c].astype(F32) + b.oR1[where].astype(F32)).astype(BF16)
        arrived(b.dR1.at[where], b.rD1.at[where])
        b.dP[where, c] = (b.dP[where, c].astype(F32) + b.dR1[where].astype(F32)).astype(BF16)
        if k:
            send(b.dP.at[where, c], b.dR2.at[k - 1], b.rD2.at[k - 1], dev(r, where * 2 + c))
            send(b.oP.at[where, c], b.oR2.at[k - 1], b.rO2.at[k - 1], dev(r, where * 2 + c))

    for shift in range(planes):
        origin, rank, slot, src = down_route(shift)

        @pl.when(rank != p)
        def _():
            down_copy(shift).wait_send()

    drain()
    nf_all = b.nfA.reshape(PLANE * tok, dm.dp)
    g_all = b.gA.reshape(PLANE * tok, dm.d)
    wide_rows = dm.dp
    chunk = dm.dp // 4

    @pl.loop(0, 4)
    def _(i):
        cols = pl.ds(pl.multiple_of(i * chunk, chunk), chunk)
        total = mm_tn(nf_all[:wide_rows, cols], BIG[:, : 2 * dm.ffr])
        total = total + mm_tn(nf_all[wide_rows:, cols], BIG[:, 2 * dm.ffr :])
        GU[cols, :] = total.astype(BF16)

    for k in range(1, planes):
        to = (r + k) % planes
        send(plane_rows(b.GU, to), b.zR.at[k - 1], b.rZ.at[k - 1], dev(to, p))
    WD[...] = mm_tn(b.act[...], g_all[...]).astype(BF16)

    def down_back(slot):
        whole = p * planes + slot
        return whole // PLANE, whole % PLANE

    def down_back_copy(slot):
        plane_to, place_to = down_back(slot)
        return pltpu.make_async_remote_copy(
            src_ref=b.WD.at[slot],
            dst_ref=b.dWDz.at[plane_to],
            send_sem=b.vsem.at[slot],
            recv_sem=b.rW1.at[plane_to],
            device_id=dev(r, place_to),
            device_id_type=MESH,
        )

    for slot in range(planes):
        plane_to, place_to = down_back(slot)

        @pl.when(place_to == p)
        def _():
            pltpu.make_async_copy(b.WD.at[slot], b.dWDz.at[plane_to], b.rW1.at[plane_to]).start()

        @pl.when(place_to != p)
        def _():
            down_back_copy(slot).start()

    d_nf = b.dP[q, c].astype(F32)
    total = b.oP[q, c].astype(F32)
    for k in range(1, CHIPS):
        arrived(b.dR2.at[k - 1], b.rD2.at[k - 1])
        d_nf = d_nf + b.dR2[k - 1].astype(F32)
    for k in range(1, CHIPS):
        arrived(b.oR2.at[k - 1], b.rO2.at[k - 1])
        total = total + b.oR2[k - 1].astype(F32)
    hidden = b.hid[...]
    b.out[...] = (hidden + total).astype(BF16)
    d_nf = split_mm(d_nf, b.spr[...], nt=True)
    scale2 = lax.rsqrt(jnp.mean(hidden * hidden, axis=-1, keepdims=True) + 1e-06)

    def norm_back(grad, field, scale, gain):
        weighted = grad * gain
        d_gain = jnp.sum(grad * field * scale, axis=0, keepdims=True)
        d_field = weighted * scale - field * (scale * scale * scale) * jnp.mean(
            weighted * field, axis=-1, keepdims=True
        )
        return d_gain, d_field

    d_gain2, d_part = norm_back(d_nf, hidden, scale2, b.vec[2:3])
    d_hidden = b.g[...].astype(F32) + d_part
    b.hid[...] = d_hidden
    d_attn = d_hidden.astype(BF16)
    for k in range(1, planes):
        to = (r + k) % planes
        arrived(b.dWDz.at[to], b.rW1.at[to])
        send(b.dWDz.at[to], b.dWDr.at[k - 1], b.rW2.at[k - 1], dev(to, p))

    BIG[:, dm.qkv : dm.wide] = mm_tn(b.mpad[...], d_attn).astype(BF16)
    d_mixed = mm_nt(d_attn, W[:, dm.qkv :]).astype(BF16)
    d_mixed = mm_nt(d_mixed, b.spr[...])
    d_values = []
    for m in range(dm.micro):
        here = slice(m * dm.slots, (m + 1) * dm.slots)
        stack_heads(d_mixed[here], b.DMS)
        d_v, d_k = [], []
        for kv in range(KV_HEADS):
            rows = slice(kv * span, (kv + 1) * span)
            dms, prob, qs = b.DMS[rows], b.PF[m, rows], b.QS[m, rows]
            d_v.append(mm_tn(prob.astype(BF16), dms))
            d_prob = mm_nt(dms, b.vd[kv, here])
            delta = jnp.sum(d_prob * prob, axis=-1, keepdims=True)
            d_score = (prob * (d_prob - delta)).astype(BF16)
            d_k.append(0.125 * mm_tn(d_score, qs))
            b.PF[m, rows] = 0.125 * mm(d_score, b.kd[kv, here])
        for t in range(HEADS // 2):
            even = b.PF[m, 2 * t * dm.slots : (2 * t + 1) * dm.slots]
            odd = b.PF[m, (2 * t + 1) * dm.slots : (2 * t + 2) * dm.slots]
            b.FQ[here, t * LANES : (t + 1) * LANES] = jnp.where(low, even, odd)

        def joined(pair):
            zero, one = (piece + pltpu.roll(piece, HEAD_DIM, 1) for piece in pair)
            return jnp.where(low, zero, one)

        b.FQ[here, dm.heads : dm.heads + dm.kv] = joined(d_k)
        d_values.append(joined(d_v))
    d_turned = b.FQ[...]
    cosine = jnp.concatenate([b.tabs[0]] * reps, axis=1)
    sine = jnp.concatenate([b.tabs[1]] * reps, axis=1)
    first, ahead, behind = half_turn(d_turned * sine)
    d_lin = (d_turned * cosine + jnp.where(first, ahead, -behind)).astype(BF16)
    d_lin = jnp.concatenate([d_lin, jnp.concatenate(d_values, axis=0).astype(BF16)], axis=1)
    BIG[:, : dm.qkv] = mm_tn(b.npad[...], d_lin).astype(BF16)
    d_bias = jnp.sum(d_lin.astype(F32), axis=0, keepdims=True)
    d_normed = split_mm(mm_nt(d_lin, W[:, : dm.qkv]), b.spr[...], nt=True)
    xf = b.x[...].astype(F32)
    scale1 = lax.rsqrt(jnp.mean(xf * xf, axis=-1, keepdims=True) + 1e-06)
    d_gain1, d_part = norm_back(d_normed, xf, scale1, b.vec[0:1])
    b.gin[...] = (b.hid[...] + d_part).astype(BF16)

    rows8 = iota((8, dm.d), 0)
    packed = jnp.zeros((8, dm.d), F32)
    for i, piece in enumerate((d_gain1, d_bias[:, : dm.heads], d_gain2)):
        packed = jnp.where(rows8 == i, piece, packed)
    packed = split_mm(packed, b.spr[...])
    mine = own_block(dm)
    spare = jnp.zeros((n, LANES), F32)
    for i in range(3):
        piece = jnp.where(mine, packed[i : i + 1], 0.0).astype(BF16)
        spare = spare + mm_nt(piece, field_matrix(dm, i * FIELD))
    piece = jnp.where(value_block(dm), d_bias[:, dm.heads + dm.kv :], 0.0).astype(BF16)
    spare = spare + mm_nt(piece, value_field(dm))
    key_bias = jnp.broadcast_to(d_bias[:, dm.heads : dm.heads + dm.kv], (n, LANES))
    spare = jnp.concatenate([spare, key_bias], axis=1).astype(BF16)
    BIG[:, : 2 * LANES] = (
        BIG[:, : 2 * LANES].astype(F32) + mm_tn(spare_rows(dm), spare)
    ).astype(BF16)

    cols = pl.ds(0, dm.wide)

    def quad(plane):
        return pl.ds(plane * CHIPS, CHIPS)

    for k in (*range(1, planes), 0):
        to = (r + k) % planes
        send(b.BIG.at[quad(to), other, :, cols], b.aR1.at[quad(to)], b.rA1.at[to], (partner,))
    for k in (*range(1, planes), 0):
        to = (r + k) % planes
        arrived(b.aR1.at[quad(to)], b.rA1.at[to])
        mine_now = b.BIG[quad(to), c, :, cols].astype(F32) + b.aR1[quad(to)].astype(F32)
        b.aR1[quad(to)] = mine_now.astype(BF16)
        for j in range(1, CHIPS):
            where = (q + j) % CHIPS
            send(
                b.aR1.at[to * CHIPS + where],
                b.aR2.at[j - 1, to],
                b.rA2.at[j - 1, to],
                dev(r, where * 2 + c),
            )
    mine_gu = plane_rows(b.GU, r)
    total = mine_gu[...].astype(F32)
    for k in range(1, planes):
        arrived(b.zR.at[k - 1], b.rZ.at[k - 1])
        total = total + b.zR[k - 1].astype(F32)
    mine_gu[...] = total.astype(BF16)
    for k in range(1, PLANE):
        to = (p + k) % PLANE
        send(b.GU.at[r * PLANE + to], b.fgu.at[p], b.rF.at[p], dev(r, to))
    b.fgu[p] = b.GU[me]
    for k in (*range(1, planes), 0):
        to = (r + k) % planes
        total = b.aR1[to * CHIPS + q].astype(F32)
        for j in range(1, CHIPS):
            arrived(b.aR2.at[j - 1, to], b.rA2.at[j - 1, to])
            total = total + b.aR2[j - 1, to].astype(F32)
        if k:
            b.aR2[0, to] = total.astype(BF16)
            send(b.aR2.at[0, to], b.aR3.at[k - 1], b.rA3.at[k - 1], dev(to, p))
    arrived(b.dWDz.at[r], b.rW1.at[r])
    down = b.dWDz[r].astype(F32)
    for k in range(1, planes):
        arrived(b.dWDr.at[k - 1], b.rW2.at[k - 1])
        down = down + b.dWDr[k - 1].astype(F32)
    b.fwd[...] = down
    for k in range(1, planes):
        arrived(b.aR3.at[k - 1], b.rA3.at[k - 1])
        total = total + b.aR3[k - 1].astype(F32)
    b.fa[...] = total
    for k in range(1, PLANE):
        origin = (p + PLANE - k) % PLANE
        arrived(b.fgu.at[origin], b.rF.at[origin])
    for slot in range(planes):
        plane_to, place_to = down_back(slot)

        @pl.when(place_to != p)
        def _():
            down_back_copy(slot).wait_send()

    for where in range(CHIPS):
        first_copy(where, b.oP, b.oR1, b.osem, b.rO1).wait_send()
        first_copy(where, b.dP, b.dR1, b.dsem, b.rD1).wait_send()
    drain()


def run_layer(dm, operands):
    n, planes, rp, tok = dm.n, dm.planes, dm.rp, dm.tok
    vm = pltpu.VMEM
    sem = pltpu.SemaphoreType.DMA
    quads = planes * CHIPS
    pairs = dm.heads + dm.kv
    outs = {
        "out": jax.ShapeDtypeStruct((tok, dm.d), BF16),
        "gin": jax.ShapeDtypeStruct((tok, dm.d), BF16),
        "fa": jax.ShapeDtypeStruct((rp, dm.wide), F32),
        "fgu": jax.ShapeDtypeStruct((PLANE, rp, 2 * dm.ffr), BF16),
        "fwd": jax.ShapeDtypeStruct((dm.rfp, dm.d), F32),
    }
    n_sends = 1 + (planes - 1) * 5 + 8 * PLANE + 8 * quads + 64
    scratch = {
        "W": vm((quads, 2, rp, dm.wide), BF16),
        "GU": vm((n, rp, 2 * dm.ffr), BF16),
        "WDz": vm((planes, dm.rfp, dm.d), BF16),
        "WD": vm((planes, dm.rfp, dm.d), BF16),
        "nfA": vm((PLANE, tok, dm.dp), BF16),
        "gA": vm((PLANE, tok, dm.d), BF16),
        "act": vm((PLANE * tok, dm.ffr), BF16),
        "BIG": vm((quads, 2, rp, 4 * dm.ffr), BF16),
        "oP": vm((CHIPS, 2, tok, dm.d), BF16),
        "dP": vm((CHIPS, 2, tok, dm.dp), BF16),
        "oR1": vm((CHIPS, tok, dm.d), BF16),
        "dR1": vm((CHIPS, tok, dm.dp), BF16),
        "oR2": vm((CHIPS - 1, tok, dm.d), BF16),
        "dR2": vm((CHIPS - 1, tok, dm.dp), BF16),
        "zR": vm((planes - 1, PLANE, rp, 2 * dm.ffr), BF16),
        "dWDz": vm((planes, dm.rfp, dm.d), BF16),
        "dWDr": vm((planes - 1, dm.rfp, dm.d), BF16),
        "aR1": vm((quads, rp, dm.wide), BF16),
        "aR2": vm((CHIPS - 1, planes, rp, dm.wide), BF16),
        "aR3": vm((planes - 1, rp, dm.wide), BF16),
        "QS": vm((dm.micro, HEADS * dm.slots, LANES), BF16),
        "PF": vm((dm.micro, HEADS * dm.slots, dm.slots), F32),
        "DMS": vm((HEADS * dm.slots, LANES), BF16),
        "hid": vm((tok, dm.d), F32),
        "npad": vm((tok, dm.dp), BF16),
        "mpad": vm((tok, dm.dp), BF16),
        "spr": vm((dm.d, dm.dp), BF16),
        "kd": vm((KV_HEADS, tok, LANES), BF16),
        "vd": vm((KV_HEADS, tok, LANES), BF16),
        "FQ": vm((tok, pairs), F32),
        "mix": vm((tok, dm.d), BF16),
        "tabs": vm((2, tok, LANES), F32),
        "vec": vm((8, dm.d), F32),
        "ssem": sem((n_sends,)),
        "csem": sem((3,)),
        "osem": sem((CHIPS,)),
        "dsem": sem((CHIPS,)),
        "wsem": sem((planes,)),
        "vsem": sem((planes,)),
        "rA": sem((n,)),
        "rGU": sem((PLANE,)),
        "rGZ": sem((planes,)),
        "rG": sem((PLANE,)),
        "rWZ": sem((planes,)),
        "rWD": sem((planes,)),
        "rNF": sem((PLANE,)),
        "rO1": sem((CHIPS,)),
        "rD1": sem((CHIPS,)),
        "rO2": sem((CHIPS - 1,)),
        "rD2": sem((CHIPS - 1,)),
        "rZ": sem((planes - 1,)),
        "rF": sem((PLANE,)),
        "rW1": sem((planes,)),
        "rW2": sem((planes - 1,)),
        "rA1": sem((planes,)),
        "rA2": sem((CHIPS - 1, planes)),
        "rA3": sem((planes - 1,)),
    }
    return pl.pallas_call(
        functools.partial(layer_kernel, dm, (*operands, *outs, *scratch)),
        name="layer",
        out_shape=list(outs.values()),
        in_specs=[pl.BlockSpec(memory_space=pltpu.VMEM)] * len(operands),
        out_specs=[pl.BlockSpec(memory_space=pltpu.VMEM)] * len(outs),
        scratch_shapes=list(scratch.values()),
        compiler_params=pltpu.CompilerParams(
            collective_id=0, has_side_effects=True, vmem_limit_bytes=67043328
        ),
    )(*operands.values())


def per_device(n, *args):
    (
        tokens,
        positions,
        cotangent,
        norm_attn,
        w_query,
        b_query,
        w_key,
        b_key,
        w_value,
        b_value,
        w_out,
        norm_ffn,
        w_gate,
        w_up,
        w_down,
    ) = args
    micro, slots, d = tokens.shape
    dm = Dims(n, d, w_gate.shape[0] * n // d, slots, micro)
    rows, rp = dm.rows, dm.rp

    def lanes(vector):
        return jnp.pad(vector, (0, FIELD - vector.shape[0]))

    spare = jnp.concatenate([lanes(v) for v in (norm_attn, b_query, norm_ffn, b_value)])
    spare = jnp.pad(spare, (0, dm.wide - spare.shape[0]))
    pack = jnp.concatenate(
        [w.reshape(rows, -1) for w in (w_query, w_key, w_value, w_out)], axis=1
    )
    pack = jnp.concatenate([pack, spare[None]], axis=0)
    pack = jnp.pad(pack, ((0, rp - rows - 1), (0, 0)))

    def columns(weight):
        weight = weight.reshape(rows, PLANE, dm.planes, dm.rf)
        weight = jnp.pad(weight, ((0, rp - rows), (0, 0), (0, 0), (0, dm.rfp - dm.rf)))
        return weight.reshape(rp, PLANE, dm.ffr)

    both = jnp.concatenate([columns(w_gate), columns(w_up)], axis=2)
    both = both.transpose(1, 0, 2)
    down = jnp.pad(w_down.reshape(dm.rf, d), ((0, dm.rfp - dm.rf), (0, 0)))
    half_dim = HEAD_DIM // 2
    freq = 1000000.0 ** (-(jnp.arange(half_dim).astype(F32) * 2.0 / HEAD_DIM))
    freq = jnp.tile(freq, LANES // half_dim)[None]
    operands = {
        "x": tokens.reshape(dm.tok, d),
        "g": cotangent.reshape(dm.tok, d),
        "posc": positions.reshape(dm.tok, 1),
        "posr": positions,
        "freq": freq,
        "bkey": b_key[None],
        "ap": pack,
        "gus": both,
        "wds": down,
    }
    out, gin, fa, fgu, fwd = run_layer(dm, operands)

    def field(i, size):
        return fa[rows, i * FIELD : i * FIELD + size]

    def flat(start, stop):
        return fa[:rows, start:stop].reshape(-1)

    def gate_part(start):
        part = fgu[:, :rows, start : start + dm.ffr].astype(F32)
        part = part.reshape(PLANE, rows, dm.planes, dm.rfp)[..., : dm.rf]
        return part.transpose(1, 0, 2, 3).reshape(-1)

    h, kv = dm.heads, dm.kv
    return (
        out.reshape(micro, slots, d),
        gin.reshape(micro, slots, d),
        field(0, rows),
        flat(0, h),
        field(1, rows),
        flat(h, h + kv),
        fa[rows, LANES : LANES + kv],
        flat(h + kv, h + 2 * kv),
        field(3, dm.rv),
        flat(h + 2 * kv, dm.wide),
        field(2, rows),
        gate_part(0),
        gate_part(dm.ffr),
        fwd[: dm.rf].reshape(-1),
    )


def solution(mesh):
    n = mesh.shape["dp"]
    split, row = P("dp"), P(None, "dp", None)
    in_specs = (row, P(None, "dp"), row, *[split] * 4, P(), *[split] * 7)
    out_specs = (row, row, *[split] * 4, P(), *[split] * 7)
    return jax.shard_map(
        functools.partial(per_device, n),
        mesh=mesh,
        in_specs=in_specs,
        out_specs=out_specs,
        check_vma=False,
    )
```

```python
import functools

import jax
import jax.numpy as jnp
from jax import lax
from jax.experimental import pallas as pl
from jax.experimental.pallas import tpu as pltpu
from jax.sharding import PartitionSpec as P

HEADS = 14
KV_HEADS = 2
HEAD_DIM = 64
GROUP = HEADS // KV_HEADS
PLANE = 8
CHIPS = 4
LANES = 128
FIELD = 32
MESH = pl.DeviceIdType.MESH
F32 = jnp.float32
BF16 = jnp.bfloat16


def up(value, step):
    return -(-value // step) * step


def mm(left, right, dims=((1,), (0,))):
    return lax.dot_general(left, right, (dims, ((), ())), preferred_element_type=F32)


def mm_nt(left, right):
    return mm(left, right, ((1,), (1,)))


def mm_tn(left, right):
    return mm(left, right, ((0,), (0,)))


def split_mm(left, right, nt=False):
    high = left.astype(BF16)
    low = (left - high.astype(F32)).astype(BF16)
    dot = mm_nt if nt else mm
    return dot(high, right) + dot(low, right)


def iota(shape, dim):
    return lax.broadcasted_iota(jnp.int32, shape, dim)


class Dims:
    def __init__(self, n, d, ff, slots, micro):
        self.n, self.d, self.ff = n, d, ff
        self.planes = n // PLANE
        self.rows = d // n
        self.rp = 8
        while self.rp < self.rows + 1:
            self.rp *= 2
        self.dp = n * self.rp
        self.rf = ff // n
        self.ffr = up(ff // PLANE, LANES)
        self.rfp = self.ffr // self.planes
        self.slots, self.micro = slots, micro
        self.tok = slots * micro
        self.heads = HEADS * HEAD_DIM
        self.kv = KV_HEADS * HEAD_DIM
        self.qkv = self.heads + 2 * self.kv
        self.wide = self.qkv + d
        self.rv = self.kv // n
        self.unit = PLANE * self.rows
        self.gs = 16 if self.unit % 16 == 0 else 8
        self.groups = self.unit // self.gs


def spread_matrix(dm):
    shape = (dm.d, dm.dp)
    row, col = iota(shape, 0), iota(shape, 1)
    inner = col & (dm.rp - 1)
    hit = (row == (col // dm.rp) * dm.rows + inner) & (inner < dm.rows)
    return jnp.where(hit, 1.0, 0.0).astype(BF16)


def field_matrix(dm, offset):
    shape = (LANES, dm.dp)
    row, col = iota(shape, 0), iota(shape, 1)
    inner = col & (dm.rp - 1)
    return jnp.where((row == offset + inner) & (inner < dm.rows), 1.0, 0.0).astype(BF16)


def own_block(dm):
    shape = (dm.n, dm.dp)
    return iota(shape, 1) // dm.rp == iota(shape, 0)


def spare_rows(dm):
    shape = (dm.n, dm.dp)
    return jnp.where(iota(shape, 1) == iota(shape, 0) * dm.rp + dm.rows, 1.0, 0.0).astype(BF16)


def value_field(dm):
    shape = (LANES, LANES)
    return jnp.where(
        iota(shape, 0) == 3 * FIELD + (iota(shape, 1) & (dm.rv - 1)), 1.0, 0.0
    ).astype(BF16)


def value_block(dm):
    shape = (dm.n, LANES)
    return iota(shape, 1) // dm.rv == iota(shape, 0)


def half_turn(field):
    width = field.shape[-1]
    first = (iota(field.shape, 1) & (HEAD_DIM - 1)) < HEAD_DIM // 2
    ahead = pltpu.roll(field, width - HEAD_DIM // 2, 1)
    behind = pltpu.roll(field, HEAD_DIM // 2, 1)
    return first, ahead, behind


def twice(field):
    low = iota(field.shape, 1) < HEAD_DIM
    turned = pltpu.roll(field, HEAD_DIM, 1)
    return jnp.where(low, field, turned), jnp.where(low, turned, field)


class Refs:
    def __init__(self, names, refs):
        self.__dict__.update(zip(names, refs, strict=True))


def layer_kernel(dm, names, *refs):
    b = Refs(names, refs)
    n, planes, rp = dm.n, dm.planes, dm.rp
    me = lax.axis_index("dp")
    r, p = me // PLANE, me % PLANE
    q, c = p // 2, p % 2
    other = 1 - c
    partner = r * PLANE + q * 2 + other

    def dev(plane, place):
        return (plane * PLANE + place,)

    barrier = pltpu.get_barrier_semaphore()
    peers = [dev(r, (p + k) % PLANE) for k in range(1, PLANE)]
    peers += [dev((r + k) % planes, p) for k in range(1, planes)]
    for peer in peers:
        pl.semaphore_signal(barrier, inc=1, device_id=peer, device_id_type=MESH)
    pl.semaphore_wait(barrier, len(peers))

    pending = []
    count = [0]

    def send(src, dst, arrive, to, cond=None):
        copy = pltpu.make_async_remote_copy(
            src_ref=src,
            dst_ref=dst,
            send_sem=b.ssem.at[count[0]],
            recv_sem=arrive,
            device_id=to,
            device_id_type=MESH,
        )
        count[0] += 1
        pending.append((copy, cond))
        if cond is None:
            copy.start()
        else:
            pl.when(cond)(copy.start)

    def drain(left=0):
        for copy, cond in pending[: len(pending) - left]:
            if cond is None:
                copy.wait_send()
            else:
                pl.when(cond)(copy.wait_send)
        del pending[: len(pending) - left]

    upper = r // max(planes // 2, 1)
    mirror = r + upper * (planes - 1 - 2 * r)

    def origin_of(k):
        spot = k - (mirror + planes - k) // planes
        return spot + upper * (planes - 1 - 2 * spot)

    def relay(src, dst, arrive, origin=None):
        if origin is None:
            send(src, dst, arrive, dev(r + 1, p), r + 1 < planes)
            send(src, dst, arrive, dev(r - 1, p), r >= 1)
        else:
            to = r - 1 + 2 * ((r - origin - 1 + planes) // planes)
            send(src, dst, arrive, dev(to, p), (to >= 0) & (to < planes))

    def arrived(dst, arrive):
        pltpu.make_async_remote_copy(
            src_ref=dst,
            dst_ref=dst,
            send_sem=b.ssem.at[0],
            recv_sem=arrive,
            device_id=(partner,),
            device_id_type=MESH,
        ).wait_recv()

    def block(ref, index):
        return ref.at[index // 2, index % 2]

    def plane_rows(ref, plane):
        return ref.at[pl.ds(plane * dm.groups, dm.groups)]

    keep = [
        pltpu.make_async_copy(b.ap, block(b.W, me), b.csem.at[0]),
        pltpu.make_async_copy(b.gus.at[p], b.fgu.at[p], b.csem.at[1]),
        pltpu.make_async_copy(b.g, b.gA.at[p], b.csem.at[2]),
        pltpu.make_async_copy(b.wds, b.WD.at[r], b.csem.at[3]),
    ]
    for copy in keep:
        copy.start()

    relay(b.ap, block(b.W, me), b.rA.at[me])

    def fan(index, src, k_list=(1, 2, 3)):
        for k in k_list:
            send(src, block(b.W, index), b.rA.at[index], dev(r, ((q + k) % CHIPS) * 2 + c))

    fan(me, b.ap)
    send(b.ap, block(b.W, me), b.rA.at[me], (partner,))
    for k in range(1, PLANE):
        send(b.gus.at[(p + k) % PLANE], b.fgu.at[p], b.rGU.at[p], dev(r, (p + k) % PLANE))
    relay(b.wds, b.WD.at[r], b.rWD.at[r])

    tok = dm.tok
    xf = b.x[...].astype(F32)
    scale1 = lax.rsqrt(jnp.mean(xf * xf, axis=-1, keepdims=True) + 1e-06)
    angle = b.posc[...].astype(F32) * b.freq[...]
    b.tabs[0] = jnp.cos(angle)
    b.tabs[1] = jnp.sin(angle)
    b.spr[...] = spread_matrix(dm)

    for k in range(1, planes):
        origin = origin_of(k)
        index = origin * PLANE + p
        arrived(block(b.W, index), b.rA.at[index])
        relay(block(b.W, index), block(b.W, index), b.rA.at[index], origin)
        fan(index, block(b.W, index))
        send(block(b.W, index), block(b.W, index), b.rA.at[index], (partner,))
    for k in range(1, PLANE):
        origin = (p + PLANE - k) % PLANE
        arrived(b.fgu.at[origin], b.rGU.at[origin])
    keep[1].wait()
    GU = b.GU.reshape(dm.d, 2 * dm.ffr)
    my_rows = pl.ds(pl.multiple_of(r * dm.unit, dm.gs), dm.unit)
    squeeze = b.spr[: dm.unit, : PLANE * rp]
    for i in range(2):
        piece = b.fgu[:, i].reshape(PLANE * rp, dm.ffr)
        GU[my_rows, i * dm.ffr : (i + 1) * dm.ffr] = mm(squeeze, piece).astype(BF16)
    relay(plane_rows(b.GU, r), plane_rows(b.GU, r), b.rGZ.at[r])

    def relay_down(k):
        origin = origin_of(k)
        arrived(b.WD.at[origin], b.rWD.at[origin])
        relay(b.WD.at[origin], b.WD.at[origin], b.rWD.at[origin], origin)

    def relay_gate(k):
        origin = origin_of(k)
        arrived(plane_rows(b.GU, origin), b.rGZ.at[origin])
        relay(plane_rows(b.GU, origin), plane_rows(b.GU, origin), b.rGZ.at[origin], origin)

    relay_down(1)
    for k in range(1, CHIPS):
        for shift in range(planes):
            index = ((r + planes - shift) % planes) * PLANE + ((q + CHIPS - k) % CHIPS) * 2 + c
            arrived(block(b.W, index), b.rA.at[index])
            send(block(b.W, index), block(b.W, index), b.rA.at[index], (partner,))
    for k in range(1, CHIPS):
        send(b.g, b.gA.at[p], b.rG.at[p], dev(r, ((q + k) % CHIPS) * 2 + c))
    send(b.g, b.gA.at[p], b.rG.at[p], (partner,))

    for k in range(2, min(planes, 3)):
        relay_down(k)

    keep[0].wait()
    for k in range(CHIPS):
        for shift in range(planes):
            index = ((r + planes - shift) % planes) * PLANE + ((q + CHIPS - k) % CHIPS) * 2 + other
            arrived(block(b.W, index), b.rA.at[index])

    W = b.W.reshape(dm.dp, dm.wide)
    small = mm(spare_rows(dm), W[:, :LANES]).astype(BF16)
    mine = own_block(dm)
    rows8 = iota((8, dm.dp), 0)
    padded = jnp.zeros((8, dm.dp), F32)
    for i in range(3):
        piece = mm(small, field_matrix(dm, i * FIELD))
        piece = jnp.sum(jnp.where(mine, piece, 0.0), axis=0, keepdims=True)
        padded = jnp.where(rows8 == i, piece, padded)
    b.vec[...] = mm_nt(padded.astype(BF16), b.spr[...])
    gain1, bias_q, gain2 = b.vec[0:1], b.vec[1:2], b.vec[2:3]
    bias_v = jnp.sum(
        jnp.where(value_block(dm), mm(small, value_field(dm)), 0.0), axis=0, keepdims=True
    )
    bias_k = b.bkey[...].astype(F32)

    normed = (xf * scale1 * gain1).astype(BF16)
    b.npad[...] = mm(normed, b.spr[...]).astype(BF16)
    lin = mm(b.npad[...], W[:, : dm.qkv])
    turn_in = jnp.concatenate([lin[:, : dm.heads] + bias_q, lin[:, dm.heads : dm.heads + dm.kv] + bias_k], axis=1)
    reps = (dm.heads + dm.kv) // LANES
    cosine = jnp.concatenate([b.tabs[0]] * reps, axis=1)
    sine = jnp.concatenate([b.tabs[1]] * reps, axis=1)
    first, ahead, behind = half_turn(turn_in)
    turned = turn_in * cosine + jnp.where(first, -ahead, behind) * sine
    values = lin[:, dm.heads + dm.kv :] + bias_v
    for i, piece in enumerate(twice(turned[:, dm.heads :])):
        b.kd[i] = piece.astype(BF16)
    for i, piece in enumerate(twice(values)):
        b.vd[i] = piece.astype(BF16)
    low = iota((dm.slots, LANES), 1) < HEAD_DIM

    def stack_heads(field, store):
        for h in range(HEADS):
            part = field[:, LANES * (h // 2) : LANES * (h // 2) + LANES]
            part = jnp.where(low if h % 2 == 0 else ~low, part, 0.0)
            store(h)[...] = part.astype(BF16)

    span = GROUP * dm.slots
    mix = b.oP.at[0, 0]
    BIG = b.BIG.reshape(dm.dp, 4 * dm.ffr)
    dms = [BIG.at[:span, dm.wide + kv * LANES : dm.wide + (kv + 1) * LANES] for kv in range(KV_HEADS)]

    def head_rows(h):
        return dms[h // GROUP].at[(h % GROUP) * dm.slots : (h % GROUP + 1) * dm.slots]

    for m in range(dm.micro):
        here = slice(m * dm.slots, (m + 1) * dm.slots)
        stack_heads(turned[here, : dm.heads], lambda h: b.QS.at[m, h * dm.slots : (h + 1) * dm.slots])
        grid = (dm.slots, dm.slots)
        start_row = iota((dm.slots, 1), 0) - b.posc[here]
        start_col = iota((1, dm.slots), 1) - b.posr[m : m + 1]
        allowed = (start_row == start_col) & (iota(grid, 1) <= iota(grid, 0))
        for kv in range(KV_HEADS):
            rows = slice(kv * span, (kv + 1) * span)
            score = mm_nt(b.QS[m, rows], b.kd[kv, here]) * 0.125
            score = jnp.where(allowed[None], score.reshape(GROUP, *grid), -1e30)
            top = jnp.max(score, axis=-1, keepdims=True)
            expo = jnp.exp(score - top)
            prob = expo / jnp.sum(expo, axis=-1, keepdims=True)
            prob = prob.reshape(span, dm.slots)
            b.PF[m, rows] = prob
            dms[kv][...] = mm(prob.astype(BF16), b.vd[kv, here]).astype(BF16)
        for t in range(HEADS // 2):
            even, odd = head_rows(2 * t)[...], head_rows(2 * t + 1)[...]
            mix[here, t * LANES : (t + 1) * LANES] = jnp.where(low, even, odd)
    b.mpad[...] = mm(mix[...], b.spr[...]).astype(BF16)
    hidden = xf + mm(b.mpad[...], W[:, dm.qkv :])
    b.hid[...] = hidden
    scale2 = lax.rsqrt(jnp.mean(hidden * hidden, axis=-1, keepdims=True) + 1e-06)
    nf = (hidden * scale2 * gain2).astype(BF16)
    b.nfA[p] = nf

    for k in range(1, CHIPS):
        send(b.nfA.at[p], b.nfA.at[p], b.rNF.at[p], dev(r, ((q + k) % CHIPS) * 2 + c))
    send(b.nfA.at[p], b.nfA.at[p], b.rNF.at[p], (partner,))
    relay_gate(1)
    for k in range(1, CHIPS):
        place = ((q + CHIPS - k) % CHIPS) * 2 + c
        arrived(b.gA.at[place], b.rG.at[place])
        send(b.gA.at[place], b.gA.at[place], b.rG.at[place], (partner,))
    for k in range(2, planes):
        if k > 2:
            relay_down(k)
        relay_gate(k)
    for k in range(1, CHIPS):
        place = ((q + CHIPS - k) % CHIPS) * 2 + c
        arrived(b.nfA.at[place], b.rNF.at[place])
        send(b.nfA.at[place], b.nfA.at[place], b.rNF.at[place], (partner,))
    keep[2].wait()
    keep[3].wait()
    for k in range(CHIPS):
        place = ((q + CHIPS - k) % CHIPS) * 2 + other
        arrived(b.gA.at[place], b.rG.at[place])
        arrived(b.nfA.at[place], b.rNF.at[place])

    ACT = b.act.reshape(PLANE * tok, dm.ffr)
    WD = b.WD.reshape(dm.ffr, dm.d)
    half = PLANE // 2

    def feed(place_q, place_c):
        place = place_q * 2 + place_c
        nf_t, g_t = b.nfA[place], b.gA[place]
        pre = mm(nf_t, GU[...])
        gate, upper = pre[:, : dm.ffr], pre[:, dm.ffr :]
        sigma = jax.nn.sigmoid(gate)
        silu = gate * sigma
        act = (silu * upper).astype(BF16)
        ACT[pl.ds(pl.multiple_of(place * tok, tok), tok), :] = act
        b.oP[place_q, place_c] = mm(act, WD[...]).astype(BF16)
        d_act = mm_nt(g_t, WD[...])
        d_gate = (d_act * upper * (sigma + silu * (1.0 - sigma))).astype(BF16)
        d_up = (d_act * silu).astype(BF16)
        d_both = jnp.concatenate([d_gate, d_up], axis=1)
        rows = pl.ds(pl.multiple_of((place % half) * tok, tok), tok)
        cols = pl.ds(pl.multiple_of((place // half) * 2 * dm.ffr, LANES), 2 * dm.ffr)
        BIG[rows, cols] = d_both
        b.dP[place_q, place_c] = mm_nt(d_both, GU[...]).astype(BF16)

    def first_copy(where, part, landing, sems, arrive):
        return pltpu.make_async_remote_copy(
            src_ref=part.at[where, other],
            dst_ref=landing.at[where],
            send_sem=sems.at[where],
            recv_sem=arrive.at[where],
            device_id=(partner,),
            device_id_type=MESH,
        )

    def second_copy(k, part, landing, sems, arrive):
        where = (q + k) % CHIPS
        return pltpu.make_async_remote_copy(
            src_ref=part.at[where, c],
            dst_ref=landing.at[k - 1],
            send_sem=sems.at[k - 1],
            recv_sem=arrive.at[k - 1],
            device_id=dev(r, where * 2 + c),
            device_id_type=MESH,
        )

    def join(where):
        for part, one, arrive in ((b.dP, b.dR1, b.rD1), (b.oP, b.oR1, b.rO1)):
            arrived(one.at[where], arrive.at[where])
            part[where, c] = (part[where, c].astype(F32) + one[where].astype(F32)).astype(BF16)

    @pl.loop(0, CHIPS)
    def _(step):
        where = (q + 1 + step) % CHIPS

        @pl.loop(0, 2)
        def _(turn):
            feed(where, (other + turn) % 2)

            @pl.when(turn == 0)
            def _():
                first_copy(where, b.dP, b.dR1, b.dsem, b.rD1).start()
                first_copy(where, b.oP, b.oR1, b.osem, b.rO1).start()

        @pl.when(step > 0)
        def _():
            join((q + step) % CHIPS)
            second_copy(step, b.dP, b.dR2, b.dsem2, b.rD2).start()
            second_copy(step, b.oP, b.oR2, b.osem2, b.rO2).start()

    drain()
    join(q)

    nf_all = b.nfA.reshape(PLANE * tok, dm.d)
    g_all = b.gA.reshape(PLANE * tok, dm.d)
    wide_rows = half * tok
    chunk = 2 * LANES

    def hop(part, landing, arrive, to, cond):
        ahead = (to - r - 1 + planes) // planes
        beyond = r - to - 1 + 2 * planes * ahead
        last = 1 - (beyond + 4 * planes - 1) // (4 * planes)
        slot = to + (planes - to) * last
        send(part(to), landing.at[slot], arrive.at[slot], dev(r - 1 + 2 * ahead, p), cond)

    def behind_of(to):
        ahead = (to - r - 1 + planes) // planes
        follows = r + 1 - 2 * ahead
        return (follows >= 0) & (follows < planes)

    far = [origin_of(planes - k) for k in range(1, planes)]

    def chain_start(part, landing, arrive):
        for to in far:
            hop(part, landing, arrive, to, jnp.logical_not(behind_of(to)))

    def chain_step(part, landing, arrive, k):
        to = far[k]
        has = behind_of(to)

        @pl.when(has)
        def _():
            arrived(landing.at[to], arrive.at[to])
            mine = part(to)
            mine[...] = (mine[...].astype(F32) + landing[to].astype(F32)).astype(BF16)

        hop(part, landing, arrive, to, has)

    def chain_end(total, landing, arrive):
        for slot, cond in ((r, r >= 1), (planes, r + 1 < planes)):

            @pl.when(cond)
            def _():
                arrived(landing.at[slot], arrive.at[slot])
                total[...] = (total[...].astype(F32) + landing[slot].astype(F32)).astype(total.dtype)

    def gate_part(plane):
        return plane_rows(b.GU, plane)

    def down_part(plane):
        return b.WD.at[plane]

    def attn_part(plane):
        return b.aR2.at[0, plane]

    WD[...] = mm_tn(ACT[...], g_all[...]).astype(BF16)
    chain_start(down_part, b.zD, b.rW)

    def gate_grad(start, width):
        cols = pl.ds(start, width)
        total = mm_tn(nf_all[:wide_rows, cols], BIG[:, : 2 * dm.ffr])
        total = total + mm_tn(nf_all[wide_rows:, cols], BIG[:, 2 * dm.ffr :])
        GU[cols, :] = total.astype(BF16)

    @pl.loop(0, dm.d // chunk)
    def _(i):
        gate_grad(pl.multiple_of(i * chunk, chunk), chunk)

    if dm.d % chunk:
        gate_grad(dm.d - dm.d % chunk, dm.d % chunk)

    chain_start(gate_part, b.zR, b.rZ)
    d_nf = b.dP[q, c].astype(F32)
    for k in range(1, CHIPS):
        arrived(b.dR2.at[k - 1], b.rD2.at[k - 1])
        d_nf = d_nf + b.dR2[k - 1].astype(F32)
    hidden = b.hid[...]
    scale2 = lax.rsqrt(jnp.mean(hidden * hidden, axis=-1, keepdims=True) + 1e-06)

    def norm_back(grad, field, scale, gain):
        weighted = grad * gain
        d_gain = jnp.sum(grad * field * scale, axis=0, keepdims=True)
        d_field = weighted * scale - field * (scale * scale * scale) * jnp.mean(
            weighted * field, axis=-1, keepdims=True
        )
        return d_gain, d_field

    d_gain2, d_part = norm_back(d_nf, hidden, scale2, b.vec[2:3])
    d_hidden = b.g[...].astype(F32) + d_part
    b.dhid[...] = d_hidden
    d_attn = d_hidden.astype(BF16)
    BIG[:, dm.qkv : dm.wide] = mm_tn(b.mpad[...], d_attn).astype(BF16)
    d_mixed = mm_nt(d_attn, W[:, dm.qkv :]).astype(BF16)
    d_mixed = mm_nt(d_mixed, b.spr[...])
    d_values = []
    for m in range(dm.micro):
        here = slice(m * dm.slots, (m + 1) * dm.slots)
        stack_heads(d_mixed[here], head_rows)
        d_v, d_k = [], []
        for kv in range(KV_HEADS):
            rows = slice(kv * span, (kv + 1) * span)
            d_mix, prob, qs = dms[kv][...], b.PF[m, rows], b.QS[m, rows]
            d_v.append(mm_tn(prob.astype(BF16), d_mix))
            d_prob = mm_nt(d_mix, b.vd[kv, here])
            delta = jnp.sum(d_prob * prob, axis=-1, keepdims=True)
            d_score = (prob * (d_prob - delta)).astype(BF16)
            d_k.append(0.125 * mm_tn(d_score, qs))
            b.PF[m, rows] = 0.125 * mm(d_score, b.kd[kv, here])
        for t in range(HEADS // 2):
            even = b.PF[m, 2 * t * dm.slots : (2 * t + 1) * dm.slots]
            odd = b.PF[m, (2 * t + 1) * dm.slots : (2 * t + 2) * dm.slots]
            b.FQ[here, t * LANES : (t + 1) * LANES] = jnp.where(low, even, odd)

        def joined(pair):
            zero, one = (piece + pltpu.roll(piece, HEAD_DIM, 1) for piece in pair)
            return jnp.where(low, zero, one)

        b.FQ[here, dm.heads : dm.heads + dm.kv] = joined(d_k)
        d_values.append(joined(d_v))
    d_turned = b.FQ[...]
    cosine = jnp.concatenate([b.tabs[0]] * reps, axis=1)
    sine = jnp.concatenate([b.tabs[1]] * reps, axis=1)
    first, ahead, behind = half_turn(d_turned * sine)
    d_lin = (d_turned * cosine + jnp.where(first, ahead, -behind)).astype(BF16)
    d_lin = jnp.concatenate([d_lin, jnp.concatenate(d_values, axis=0).astype(BF16)], axis=1)
    BIG[:, : dm.qkv] = mm_tn(b.npad[...], d_lin).astype(BF16)
    d_bias = jnp.sum(d_lin.astype(F32), axis=0, keepdims=True)
    d_normed = split_mm(mm_nt(d_lin, W[:, : dm.qkv]), b.spr[...], nt=True)
    xf = b.x[...].astype(F32)
    scale1 = lax.rsqrt(jnp.mean(xf * xf, axis=-1, keepdims=True) + 1e-06)
    d_gain1, d_part = norm_back(d_normed, xf, scale1, b.vec[0:1])
    b.gin[...] = (b.dhid[...] + d_part).astype(BF16)

    rows8 = iota((8, dm.d), 0)
    packed = jnp.zeros((8, dm.d), F32)
    for i, piece in enumerate((d_gain1, d_bias[:, : dm.heads], d_gain2)):
        packed = jnp.where(rows8 == i, piece, packed)
    packed = split_mm(packed, b.spr[...])
    mine = own_block(dm)
    spare = jnp.zeros((n, LANES), F32)
    for i in range(3):
        piece = jnp.where(mine, packed[i : i + 1], 0.0).astype(BF16)
        spare = spare + mm_nt(piece, field_matrix(dm, i * FIELD))
    piece = jnp.where(value_block(dm), d_bias[:, dm.heads + dm.kv :], 0.0).astype(BF16)
    spare = spare + mm_nt(piece, value_field(dm))
    key_bias = jnp.broadcast_to(d_bias[:, dm.heads : dm.heads + dm.kv], (n, LANES))
    spare = jnp.concatenate([spare, key_bias], axis=1).astype(BF16)
    BIG[:, : 2 * LANES] = (
        BIG[:, : 2 * LANES].astype(F32) + mm_tn(spare_rows(dm), spare)
    ).astype(BF16)

    cols = pl.ds(0, dm.wide)

    def quad(plane):
        return pl.ds(plane * CHIPS, CHIPS)

    for to in (*far, r):
        send(b.BIG.at[quad(to), other, :, cols], b.aR1.at[quad(to)], b.rA1.at[to], (partner,))
    for to in (*far, r):
        arrived(b.aR1.at[quad(to)], b.rA1.at[to])
        mine_now = b.BIG[quad(to), c, :, cols].astype(F32) + b.aR1[quad(to)].astype(F32)
        b.aR1[quad(to)] = mine_now.astype(BF16)
        for j in range(1, CHIPS):
            where = (q + j) % CHIPS
            send(
                b.aR1.at[to * CHIPS + where],
                b.aR2.at[j - 1, to],
                b.rA2.at[j - 1, to],
                dev(r, where * 2 + c),
            )
    total = b.hid[...] + b.oP[q, c].astype(F32)
    for k in range(1, CHIPS):
        arrived(b.oR2.at[k - 1], b.rO2.at[k - 1])
        total = total + b.oR2[k - 1].astype(F32)
    b.out[...] = total.astype(BF16)
    for k in range(planes - 1):
        chain_step(down_part, b.zD, b.rW, k)
    for k in range(planes - 2):
        chain_step(gate_part, b.zR, b.rZ, k)
    for to in (*far, r):
        total = b.aR1[to * CHIPS + q].astype(F32)
        for j in range(1, CHIPS):
            arrived(b.aR2.at[j - 1, to], b.rA2.at[j - 1, to])
            total = total + b.aR2[j - 1, to].astype(F32)
        b.aR2[0, to] = total.astype(BF16)
    chain_start(attn_part, b.aR3, b.rA3)
    chain_step(gate_part, b.zR, b.rZ, planes - 2)
    chain_end(gate_part(r), b.zR, b.rZ)
    squeeze = b.spr[: dm.unit, : PLANE * rp]
    for i in range(2):
        piece = mm_tn(squeeze, GU[my_rows, i * dm.ffr : (i + 1) * dm.ffr]).astype(BF16)
        piece = piece.reshape(PLANE, rp, dm.ffr)
        for place in range(PLANE):
            b.act[2 * place + i] = piece[place]
    for k in range(1, PLANE):
        to = (p + k) % PLANE
        send(b.act.at[pl.ds(2 * to, 2)], b.fgu.at[p], b.rF.at[p], dev(r, to))
    b.fgu[p] = b.act[pl.ds(2 * p, 2)]
    for k in range(planes - 1):
        chain_step(attn_part, b.aR3, b.rA3, k)
    b.fwd[...] = b.WD[r].astype(F32)
    chain_end(b.fwd, b.zD, b.rW)
    b.fa[...] = b.aR2[0, r].astype(F32)
    chain_end(b.fa, b.aR3, b.rA3)
    for k in range(1, PLANE):
        origin = (p + PLANE - k) % PLANE
        arrived(b.fgu.at[origin], b.rF.at[origin])
    for where in range(CHIPS):
        first_copy(where, b.oP, b.oR1, b.osem, b.rO1).wait_send()
        first_copy(where, b.dP, b.dR1, b.dsem, b.rD1).wait_send()
    for k in range(1, CHIPS):
        second_copy(k, b.oP, b.oR2, b.osem2, b.rO2).wait_send()
        second_copy(k, b.dP, b.dR2, b.dsem2, b.rD2).wait_send()
    drain()


def run_layer(dm, operands):
    n, planes, rp, tok = dm.n, dm.planes, dm.rp, dm.tok
    vm = pltpu.VMEM
    sem = pltpu.SemaphoreType.DMA
    quads = planes * CHIPS
    pairs = dm.heads + dm.kv
    outs = {
        "out": jax.ShapeDtypeStruct((tok, dm.d), BF16),
        "gin": jax.ShapeDtypeStruct((tok, dm.d), BF16),
        "fa": jax.ShapeDtypeStruct((rp, dm.wide), F32),
        "fgu": jax.ShapeDtypeStruct((PLANE, 2, rp, dm.ffr), BF16),
        "fwd": jax.ShapeDtypeStruct((dm.rfp, dm.d), F32),
    }
    n_sends = 1 + (planes - 1) * 5 + 8 * PLANE + 8 * quads + 64
    scratch = {
        "W": vm((quads, 2, rp, dm.wide), BF16),
        "GU": vm((planes * dm.groups, dm.gs, 2 * dm.ffr), BF16),
        "WD": vm((planes, dm.rfp, dm.d), BF16),
        "nfA": vm((PLANE, tok, dm.d), BF16),
        "gA": vm((PLANE, tok, dm.d), BF16),
        "act": vm((PLANE * tok // rp, rp, dm.ffr), BF16),
        "BIG": vm((quads, 2, rp, 4 * dm.ffr), BF16),
        "oP": vm((CHIPS, 2, tok, dm.d), BF16),
        "dP": vm((CHIPS, 2, tok, dm.d), BF16),
        "oR1": vm((CHIPS, tok, dm.d), BF16),
        "dR1": vm((CHIPS, tok, dm.d), BF16),
        "oR2": vm((CHIPS - 1, tok, dm.d), BF16),
        "dR2": vm((CHIPS - 1, tok, dm.d), BF16),
        "zR": vm((planes + 1, dm.groups, dm.gs, 2 * dm.ffr), BF16),
        "zD": vm((planes + 1, dm.rfp, dm.d), BF16),
        "aR1": vm((quads, rp, dm.wide), BF16),
        "aR2": vm((CHIPS - 1, planes, rp, dm.wide), BF16),
        "aR3": vm((planes + 1, rp, dm.wide), BF16),
        "QS": vm((dm.micro, HEADS * dm.slots, LANES), BF16),
        "PF": vm((dm.micro, HEADS * dm.slots, dm.slots), F32),
        "hid": vm((tok, dm.d), F32),
        "dhid": vm((tok, dm.d), F32),
        "npad": vm((tok, dm.dp), BF16),
        "mpad": vm((tok, dm.dp), BF16),
        "spr": vm((dm.d, dm.dp), BF16),
        "kd": vm((KV_HEADS, tok, LANES), BF16),
        "vd": vm((KV_HEADS, tok, LANES), BF16),
        "FQ": vm((tok, pairs), F32),
        "tabs": vm((2, tok, LANES), F32),
        "vec": vm((8, dm.d), F32),
        "ssem": sem((n_sends,)),
        "csem": sem((4,)),
        "osem": sem((CHIPS,)),
        "dsem": sem((CHIPS,)),
        "osem2": sem((CHIPS - 1,)),
        "dsem2": sem((CHIPS - 1,)),
        "rA": sem((n,)),
        "rGU": sem((PLANE,)),
        "rGZ": sem((planes,)),
        "rG": sem((PLANE,)),
        "rWD": sem((planes,)),
        "rNF": sem((PLANE,)),
        "rO1": sem((CHIPS,)),
        "rD1": sem((CHIPS,)),
        "rO2": sem((CHIPS - 1,)),
        "rD2": sem((CHIPS - 1,)),
        "rZ": sem((planes + 1,)),
        "rF": sem((PLANE,)),
        "rW": sem((planes + 1,)),
        "rA1": sem((planes,)),
        "rA2": sem((CHIPS - 1, planes)),
        "rA3": sem((planes + 1,)),
    }
    return pl.pallas_call(
        functools.partial(layer_kernel, dm, (*operands, *outs, *scratch)),
        name="layer",
        out_shape=list(outs.values()),
        in_specs=[pl.BlockSpec(memory_space=pltpu.VMEM)] * len(operands),
        out_specs=[pl.BlockSpec(memory_space=pltpu.VMEM)] * len(outs),
        scratch_shapes=list(scratch.values()),
        compiler_params=pltpu.CompilerParams(
            collective_id=0, has_side_effects=True, vmem_limit_bytes=67043328
        ),
    )(*operands.values())


def per_device(n, *args):
    (
        tokens,
        positions,
        cotangent,
        norm_attn,
        w_query,
        b_query,
        w_key,
        b_key,
        w_value,
        b_value,
        w_out,
        norm_ffn,
        w_gate,
        w_up,
        w_down,
    ) = args
    micro, slots, d = tokens.shape
    dm = Dims(n, d, w_gate.shape[0] * n // d, slots, micro)
    rows, rp = dm.rows, dm.rp

    def lanes(vector):
        return jnp.pad(vector, (0, FIELD - vector.shape[0]))

    spare = jnp.concatenate([lanes(v) for v in (norm_attn, b_query, norm_ffn, b_value)])
    spare = jnp.pad(spare, (0, dm.wide - spare.shape[0]))
    pack = jnp.concatenate(
        [w.reshape(rows, -1) for w in (w_query, w_key, w_value, w_out)], axis=1
    )
    pack = jnp.concatenate([pack, spare[None]], axis=0)
    pack = jnp.pad(pack, ((0, rp - rows - 1), (0, 0)))

    def columns(weight):
        weight = weight.reshape(rows, dm.planes, PLANE, dm.rf)
        weight = jnp.pad(weight, ((0, rp - rows), (0, 0), (0, 0), (0, dm.rfp - dm.rf)))
        return weight.transpose(2, 0, 1, 3).reshape(PLANE, rp, dm.ffr)

    both = jnp.stack([columns(w_gate), columns(w_up)], axis=1)
    down = jnp.pad(w_down.reshape(dm.rf, d), ((0, dm.rfp - dm.rf), (0, 0)))
    half_dim = HEAD_DIM // 2
    freq = 1000000.0 ** (-(jnp.arange(half_dim).astype(F32) * 2.0 / HEAD_DIM))
    freq = jnp.tile(freq, LANES // half_dim)[None]
    operands = {
        "x": tokens.reshape(dm.tok, d),
        "g": cotangent.reshape(dm.tok, d),
        "posc": positions.reshape(dm.tok, 1),
        "posr": positions,
        "freq": freq,
        "bkey": b_key[None],
        "ap": pack,
        "gus": both,
        "wds": down,
    }
    out, gin, fa, fgu, fwd = run_layer(dm, operands)

    def field(i, size):
        return fa[rows, i * FIELD : i * FIELD + size]

    def flat(start, stop):
        return fa[:rows, start:stop].reshape(-1)

    def gate_part(i):
        part = fgu[:, i, :rows].astype(F32)
        part = part.reshape(PLANE, rows, dm.planes, dm.rfp)[..., : dm.rf]
        return part.transpose(1, 2, 0, 3).reshape(-1)

    h, kv = dm.heads, dm.kv
    return (
        out.reshape(micro, slots, d),
        gin.reshape(micro, slots, d),
        field(0, rows),
        flat(0, h),
        field(1, rows),
        flat(h, h + kv),
        fa[rows, LANES : LANES + kv],
        flat(h + kv, h + 2 * kv),
        field(3, dm.rv),
        flat(h + 2 * kv, dm.wide),
        field(2, rows),
        gate_part(0),
        gate_part(1),
        fwd[: dm.rf].reshape(-1),
    )


def solution(mesh):
    n = mesh.shape["dp"]
    split, row = P("dp"), P(None, "dp", None)
    in_specs = (row, P(None, "dp"), row, *[split] * 4, P(), *[split] * 7)
    out_specs = (row, row, *[split] * 4, P(), *[split] * 7)
    return jax.shard_map(
        functools.partial(per_device, n),
        mesh=mesh,
        in_specs=in_specs,
        out_specs=out_specs,
        check_vma=False,
    )
```

```python
import functools
import math

import jax
import jax.numpy as jnp
from jax import lax
from jax.experimental import pallas as pl
from jax.experimental.pallas import tpu as pltpu
from jax.sharding import PartitionSpec as P

HEADS = 14
KV_HEADS = 2
HEAD_DIM = 64
GROUP = HEADS // KV_HEADS
PLANE = 8
CHIPS = 4
LANES = 128
ROTARY_LOG = math.log(1000000.0)
FIELD = 32
MESH = pl.DeviceIdType.MESH
F32 = jnp.float32
BF16 = jnp.bfloat16


def up(value, step):
    return -(-value // step) * step


def mm(left, right, dims=((1,), (0,))):
    return lax.dot_general(left, right, (dims, ((), ())), preferred_element_type=F32)


def mm_nt(left, right):
    return mm(left, right, ((1,), (1,)))


def mm_tn(left, right):
    return mm(left, right, ((0,), (0,)))


def split_mm(left, right, nt=False):
    high = left.astype(BF16)
    low = (left - high.astype(F32)).astype(BF16)
    dot = mm_nt if nt else mm
    return dot(high, right) + dot(low, right)


def iota(shape, dim):
    return lax.broadcasted_iota(jnp.int32, shape, dim)


class Dims:
    def __init__(self, n, d, ff, slots, micro):
        self.n, self.d, self.ff = n, d, ff
        self.planes = n // PLANE
        self.rows = d // n
        self.rp = 8
        while self.rp < self.rows + 1:
            self.rp *= 2
        self.dp = n * self.rp
        self.rf = ff // n
        self.ffr = up(ff // PLANE, LANES)
        self.rfp = self.ffr // self.planes
        self.slots, self.micro = slots, micro
        self.tok = slots * micro
        self.heads = HEADS * HEAD_DIM
        self.kv = KV_HEADS * HEAD_DIM
        self.qkv = self.heads + 2 * self.kv
        self.wide = self.qkv + d
        self.rv = self.kv // n
        self.unit = PLANE * self.rows
        self.gs = 16 if self.unit % 16 == 0 else 8
        self.groups = self.unit // self.gs
        blocks = self.ffr // LANES
        wide = (blocks + 1) // 2 * LANES
        self.parts = ((0, wide), (wide, self.ffr - wide))


def spread_matrix(dm):
    shape = (dm.d, dm.dp)
    row, col = iota(shape, 0), iota(shape, 1)
    inner = col & (dm.rp - 1)
    hit = (row == (col // dm.rp) * dm.rows + inner) & (inner < dm.rows)
    return jnp.where(hit, 1.0, 0.0).astype(BF16)


def field_matrix(dm, offset):
    shape = (LANES, dm.dp)
    row, col = iota(shape, 0), iota(shape, 1)
    inner = col & (dm.rp - 1)
    return jnp.where((row == offset + inner) & (inner < dm.rows), 1.0, 0.0).astype(BF16)


def own_block(dm):
    shape = (dm.n, dm.dp)
    return iota(shape, 1) // dm.rp == iota(shape, 0)


def spare_rows(dm):
    shape = (dm.n, dm.dp)
    return jnp.where(iota(shape, 1) == iota(shape, 0) * dm.rp + dm.rows, 1.0, 0.0).astype(BF16)


def value_field(dm):
    shape = (LANES, LANES)
    return jnp.where(
        iota(shape, 0) == 3 * FIELD + (iota(shape, 1) & (dm.rv - 1)), 1.0, 0.0
    ).astype(BF16)


def value_block(dm):
    shape = (dm.n, LANES)
    return iota(shape, 1) // dm.rv == iota(shape, 0)


def half_turn(field):
    width = field.shape[-1]
    first = (iota(field.shape, 1) & (HEAD_DIM - 1)) < HEAD_DIM // 2
    ahead = pltpu.roll(field, width - HEAD_DIM // 2, 1)
    behind = pltpu.roll(field, HEAD_DIM // 2, 1)
    return first, ahead, behind


def twice(field):
    low = iota(field.shape, 1) < HEAD_DIM
    turned = pltpu.roll(field, HEAD_DIM, 1)
    return jnp.where(low, field, turned), jnp.where(low, turned, field)


class Refs:
    def __init__(self, names, refs):
        self.__dict__.update(zip(names, refs, strict=True))


def layer_kernel(dm, names, *refs):
    b = Refs(names, refs)
    n, planes, rp = dm.n, dm.planes, dm.rp
    me = lax.axis_index("dp")
    r, p = me // PLANE, me % PLANE
    q, c = p // 2, p % 2
    other = 1 - c
    partner = r * PLANE + q * 2 + other

    def dev(plane, place):
        return (plane * PLANE + place,)

    barrier = pltpu.get_barrier_semaphore()
    peers = [dev(r, (p + k) % PLANE) for k in range(1, PLANE)]
    peers += [dev((r + k) % planes, p) for k in range(1, planes)]
    for peer in peers:
        pl.semaphore_signal(barrier, inc=1, device_id=peer, device_id_type=MESH)
    pl.semaphore_wait(barrier, len(peers))

    pending = []
    count = [0]

    def prepare(src, dst, arrive, to, cond=None, tag=None):
        copy = pltpu.make_async_remote_copy(
            src_ref=src,
            dst_ref=dst,
            send_sem=b.ssem.at[count[0]],
            recv_sem=arrive,
            device_id=to,
            device_id_type=MESH,
        )
        count[0] += 1
        pending.append((copy, cond, tag))
        return copy

    def send(src, dst, arrive, to, cond=None, tag=None):
        copy = prepare(src, dst, arrive, to, cond, tag)
        if cond is None:
            copy.start()
        else:
            pl.when(cond)(copy.start)

    def drain(tag=None):
        now = [item for item in pending if tag in (None, item[2])]
        for copy, cond, _ in now:
            if cond is None:
                copy.wait_send()
            else:
                pl.when(cond)(copy.wait_send)
        pending[:] = [item for item in pending if tag not in (None, item[2])]

    upper = r // max(planes // 2, 1)
    mirror = r + upper * (planes - 1 - 2 * r)

    def origin_of(k):
        spot = k - (mirror + planes - k) // planes
        return spot + upper * (planes - 1 - 2 * spot)

    def relay_own(src, dst, arrive, tag=None):
        send(src, dst, arrive, dev(r + 1, p), r + 1 < planes, tag)
        send(src, dst, arrive, dev(r - 1, p), r >= 1, tag)

    def onward(part, sems, k, tag=None):
        origin = origin_of(k)
        to = r - 1 + 2 * ((r - origin - 1 + planes) // planes)
        cond = (to >= 0) & (to < planes)
        piece, arrive = part(origin), sems.at[origin]
        return piece, arrive, cond, prepare(piece, piece, arrive, dev(to, p), cond, tag)

    def pass_on(piece, arrive, cond, copy):
        @pl.when(cond)
        def _():
            arrived(piece, arrive)
            copy.start()

    def settle(piece, arrive, cond, copy):
        pl.when(jnp.logical_not(cond))(lambda: arrived(piece, arrive))

    def arrived(dst, arrive):
        pltpu.make_async_remote_copy(
            src_ref=dst,
            dst_ref=dst,
            send_sem=b.ssem.at[0],
            recv_sem=arrive,
            device_id=(partner,),
            device_id_type=MESH,
        ).wait_recv()

    def block(ref, index):
        return ref.at[index // 2, index % 2]

    def plane_rows(ref, plane):
        return ref.at[pl.ds(plane * dm.groups, dm.groups)]

    keep = [
        pltpu.make_async_copy(b.ap, block(b.W, me), b.csem.at[0]),
        pltpu.make_async_copy(b.gus.at[p], b.fgu.at[p], b.csem.at[1]),
        pltpu.make_async_copy(b.g, b.gA.at[p], b.csem.at[2]),
        pltpu.make_async_copy(b.wds, b.WD.at[r], b.csem.at[3]),
    ]
    for copy in keep:
        copy.start()

    relay_own(b.ap, block(b.W, me), b.rA.at[me])

    across, along = q + 1 - 2 * (q % 2), (q + 2) % CHIPS
    near = across * other + along * c
    next_to = along * other + across * c
    spots = (near, next_to, CHIPS - 1 - q)

    def fan(index, src):
        for where in (next_to, near):
            send(src, block(b.W, index), b.rA.at[index], dev(r, where * 2 + c))

    def spread_out(src, ref, arrive):
        for where in (next_to, near):
            send(src, ref.at[p], arrive.at[p], dev(r, where * 2 + c))
        send(src, ref.at[p], arrive.at[p], (partner,))

    def take_in(ref, arrive):
        for i, where in enumerate(spots):
            place = where * 2 + c
            arrived(ref.at[place], arrive.at[place])
            if i == 0:
                send(ref.at[place], ref.at[place], arrive.at[place], dev(r, next_to * 2 + c))
            send(ref.at[place], ref.at[place], arrive.at[place], (partner,))

    fan(me, b.ap)
    send(b.ap, block(b.W, me), b.rA.at[me], (partner,))
    for k in range(1, PLANE):
        send(b.gus.at[(p + k) % PLANE], b.fgu.at[p], b.rGU.at[p], dev(r, (p + k) % PLANE))
    relay_own(b.wds, b.WD.at[r], b.rWD.at[r])

    tok = dm.tok
    xf = b.x[...].astype(F32)
    scale1 = lax.rsqrt(jnp.mean(xf * xf, axis=-1, keepdims=True) + 1e-06)
    diagonal = iota((dm.slots, dm.slots), 0) == iota((dm.slots, dm.slots), 1)
    posc = [
        jnp.sum(jnp.where(diagonal, b.posr[m : m + 1].astype(F32), 0.0), axis=1, keepdims=True)
        for m in range(dm.micro)
    ]
    power = (iota((1, LANES), 1) & (HEAD_DIM // 2 - 1)).astype(F32) * (-2.0 / HEAD_DIM * ROTARY_LOG)
    angle = jnp.concatenate(posc, axis=0) * jnp.exp(power)
    b.tabs[0] = jnp.cos(angle)
    b.tabs[1] = jnp.sin(angle)
    b.spr[...] = spread_matrix(dm)

    for k in range(1, planes):
        origin = origin_of(k)
        index = origin * PLANE + p
        arrived(block(b.W, index), b.rA.at[index])
        to = r - 1 + 2 * ((r - origin - 1 + planes) // planes)
        send(block(b.W, index), block(b.W, index), b.rA.at[index], dev(to, p), (to >= 0) & (to < planes))
        fan(index, block(b.W, index))
        send(block(b.W, index), block(b.W, index), b.rA.at[index], (partner,))
    for k in range(1, PLANE):
        origin = (p + PLANE - k) % PLANE
        arrived(b.fgu.at[origin], b.rGU.at[origin])
    keep[1].wait()
    GU = [ref.reshape(dm.d, ref.shape[-1]) for ref in (b.GU0, b.GU1)]
    my_rows = pl.ds(pl.multiple_of(r * dm.unit, dm.gs), dm.unit)
    squeeze = b.spr[: dm.unit, : PLANE * rp]
    for h, (start, width) in enumerate(dm.parts):
        for i in range(2):
            piece = b.fgu[:, i, :, start : start + width].reshape(PLANE * rp, width)
            GU[h][my_rows, i * width : (i + 1) * width] = mm(squeeze, piece).astype(BF16)

    def gate_part(h):
        ref = (b.GU0, b.GU1)[h]
        return lambda plane: plane_rows(ref, plane)

    def down_part(plane):
        return b.WD.at[plane]

    relay_own(gate_part(0)(r), gate_part(0)(r), b.rGZ0.at[r], "gate0")
    steps = range(1, planes)
    down_on = [onward(down_part, b.rWD, k, "down") for k in steps]
    gate_on = [[onward(gate_part(h), sems, k, f"gate{h}") for k in steps] for h, sems in ((0, b.rGZ0), (1, b.rGZ1))]
    pass_on(*down_on[0])
    origins = [r, *(origin_of(k) for k in steps)]
    for i, where in enumerate(spots):
        for origin in origins:
            index = origin * PLANE + where * 2 + c
            arrived(block(b.W, index), b.rA.at[index])
            if i == 0:
                send(block(b.W, index), block(b.W, index), b.rA.at[index], dev(r, next_to * 2 + c))
            send(block(b.W, index), block(b.W, index), b.rA.at[index], (partner,))
    spread_out(b.g, b.gA, b.rG)
    for item in down_on[1:]:
        pass_on(*item)

    keep[0].wait()
    for k in range(CHIPS):
        for shift in range(planes):
            index = ((r + planes - shift) % planes) * PLANE + ((q + CHIPS - k) % CHIPS) * 2 + other
            arrived(block(b.W, index), b.rA.at[index])

    W = b.W.reshape(dm.dp, dm.wide)
    small = mm(spare_rows(dm), W[:, :LANES]).astype(BF16)
    mine = own_block(dm)
    rows8 = iota((8, dm.dp), 0)
    padded = jnp.zeros((8, dm.dp), F32)
    for i in range(3):
        piece = mm(small, field_matrix(dm, i * FIELD))
        piece = jnp.sum(jnp.where(mine, piece, 0.0), axis=0, keepdims=True)
        padded = jnp.where(rows8 == i, piece, padded)
    b.vec[...] = mm_nt(padded.astype(BF16), b.spr[...])
    gain1, bias_q, gain2 = b.vec[0:1], b.vec[1:2], b.vec[2:3]
    bias_v = jnp.sum(
        jnp.where(value_block(dm), mm(small, value_field(dm)), 0.0), axis=0, keepdims=True
    )
    bias_k = b.bkey[...].astype(F32)

    normed = (xf * scale1 * gain1).astype(BF16)
    b.npad[...] = mm(normed, b.spr[...]).astype(BF16)
    lin = mm(b.npad[...], W[:, : dm.qkv])
    turn_in = jnp.concatenate([lin[:, : dm.heads] + bias_q, lin[:, dm.heads : dm.heads + dm.kv] + bias_k], axis=1)
    reps = (dm.heads + dm.kv) // LANES
    cosine = jnp.concatenate([b.tabs[0]] * reps, axis=1)
    sine = jnp.concatenate([b.tabs[1]] * reps, axis=1)
    first, ahead, behind = half_turn(turn_in)
    turned = turn_in * cosine + jnp.where(first, -ahead, behind) * sine
    values = lin[:, dm.heads + dm.kv :] + bias_v
    for i, piece in enumerate(twice(turned[:, dm.heads :])):
        b.kd[i] = piece.astype(BF16)
    for i, piece in enumerate(twice(values)):
        b.vd[i] = piece.astype(BF16)
    low = iota((dm.slots, LANES), 1) < HEAD_DIM

    def stack_heads(field, store):
        for h in range(HEADS):
            part = field[:, LANES * (h // 2) : LANES * (h // 2) + LANES]
            part = jnp.where(low if h % 2 == 0 else ~low, part, 0.0)
            store(h)[...] = part.astype(BF16)

    span = GROUP * dm.slots
    mix = b.oP.at[0, 0]
    BIG = b.BIG.reshape(dm.dp, 4 * dm.ffr)
    dms = [BIG.at[:span, dm.wide + kv * LANES : dm.wide + (kv + 1) * LANES] for kv in range(KV_HEADS)]

    def head_rows(h):
        return dms[h // GROUP].at[(h % GROUP) * dm.slots : (h % GROUP + 1) * dm.slots]

    for m in range(dm.micro):
        here = slice(m * dm.slots, (m + 1) * dm.slots)
        stack_heads(turned[here, : dm.heads], lambda h: b.QS.at[m, h * dm.slots : (h + 1) * dm.slots])
        grid = (dm.slots, dm.slots)
        start_row = iota((dm.slots, 1), 0).astype(F32) - posc[m]
        start_col = (iota((1, dm.slots), 1) - b.posr[m : m + 1]).astype(F32)
        allowed = (start_row == start_col) & (iota(grid, 1) <= iota(grid, 0))
        for kv in range(KV_HEADS):
            rows = slice(kv * span, (kv + 1) * span)
            score = mm_nt(b.QS[m, rows], b.kd[kv, here]) * 0.125
            score = jnp.where(allowed[None], score.reshape(GROUP, *grid), -1e30)
            top = jnp.max(score, axis=-1, keepdims=True)
            expo = jnp.exp(score - top)
            prob = expo / jnp.sum(expo, axis=-1, keepdims=True)
            prob = prob.reshape(span, dm.slots)
            b.PF[m, rows] = prob
            dms[kv][...] = mm(prob.astype(BF16), b.vd[kv, here]).astype(BF16)
        for t in range(HEADS // 2):
            even, odd = head_rows(2 * t)[...], head_rows(2 * t + 1)[...]
            mix[here, t * LANES : (t + 1) * LANES] = jnp.where(low, even, odd)
    b.mpad[...] = mm(mix[...], b.spr[...]).astype(BF16)
    hidden = xf + mm(b.mpad[...], W[:, dm.qkv :])
    b.hid[...] = hidden
    scale2 = lax.rsqrt(jnp.mean(hidden * hidden, axis=-1, keepdims=True) + 1e-06)
    nf = (hidden * scale2 * gain2).astype(BF16)
    b.nfA[p] = nf

    spread_out(b.nfA.at[p], b.nfA, b.rNF)
    pass_on(*gate_on[0][0])
    relay_own(gate_part(1)(r), gate_part(1)(r), b.rGZ1.at[r], "gate1")
    take_in(b.gA, b.rG)
    for item in gate_on[0][1:]:
        pass_on(*item)
    take_in(b.nfA, b.rNF)
    for item in (*down_on, *gate_on[0]):
        settle(*item)
    pass_on(*gate_on[1][0])
    keep[2].wait()
    keep[3].wait()
    for k in range(CHIPS):
        place = ((q + CHIPS - k) % CHIPS) * 2 + other
        arrived(b.gA.at[place], b.rG.at[place])
        arrived(b.nfA.at[place], b.rNF.at[place])

    ACT = b.act.reshape(PLANE * tok, dm.ffr)
    WD = b.WD.reshape(dm.ffr, dm.d)
    half = PLANE // 2

    base = (0, 4 * dm.parts[0][1])

    def feed(h, place_q, place_c):
        place = place_q * 2 + place_c
        start, width = dm.parts[h]
        nf_t, g_t = b.nfA[place], b.gA[place]
        down = WD[start : start + width]
        pre = mm(nf_t, GU[h][...])
        gate, upper = pre[:, :width], pre[:, width:]
        sigma = jax.nn.sigmoid(gate)
        silu = gate * sigma
        act = (silu * upper).astype(BF16)
        ACT[pl.ds(pl.multiple_of(place * tok, tok), tok), start : start + width] = act
        d_act = mm_nt(g_t, down)
        d_gate = (d_act * upper * (sigma + silu * (1.0 - sigma))).astype(BF16)
        d_up = (d_act * silu).astype(BF16)
        d_both = jnp.concatenate([d_gate, d_up], axis=1)
        rows = pl.ds(pl.multiple_of((place % half) * tok, tok), tok)
        cols = pl.ds(pl.multiple_of(base[h] + (place // half) * 2 * width, LANES), 2 * width)
        BIG[rows, cols] = d_both
        for ref, value in ((b.oP, mm(act, down)), (b.dP, mm_nt(d_both, GU[h][...]))):
            if h:
                value = value + ref[place_q, place_c].astype(F32)
            ref[place_q, place_c] = value.astype(BF16)

    def first_copy(where, part, landing, sems, arrive):
        return pltpu.make_async_remote_copy(
            src_ref=part.at[where, other],
            dst_ref=landing.at[where],
            send_sem=sems.at[where],
            recv_sem=arrive.at[where],
            device_id=(partner,),
            device_id_type=MESH,
        )

    def second_copy(k, part, landing, sems, arrive):
        where = (q + k) % CHIPS
        return pltpu.make_async_remote_copy(
            src_ref=part.at[where, c],
            dst_ref=landing.at[k - 1],
            send_sem=sems.at[k - 1],
            recv_sem=arrive.at[k - 1],
            device_id=dev(r, where * 2 + c),
            device_id_type=MESH,
        )

    def hop(part, landing, arrive, to, cond):
        ahead = (to - r - 1 + planes) // planes
        beyond = r - to - 1 + 2 * planes * ahead
        last = 1 - (beyond + 4 * planes - 1) // (4 * planes)
        slot = to + (planes - to) * last
        send(part(to), landing.at[slot], arrive.at[slot], dev(r - 1 + 2 * ahead, p), cond)

    def behind_of(to):
        ahead = (to - r - 1 + planes) // planes
        follows = r + 1 - 2 * ahead
        return (follows >= 0) & (follows < planes)

    far = [origin_of(planes - k) for k in range(1, planes)]

    def chain_start(part, landing, arrive):
        for to in far:
            hop(part, landing, arrive, to, jnp.logical_not(behind_of(to)))

    def chain_step(part, landing, arrive, k):
        to = far[k]
        has = behind_of(to)

        @pl.when(has)
        def _():
            arrived(landing.at[to], arrive.at[to])
            mine = part(to)
            mine[...] = (mine[...].astype(F32) + landing[to].astype(F32)).astype(BF16)

        hop(part, landing, arrive, to, has)

    def chain_end(total, landing, arrive):
        for slot, cond in ((r, r >= 1), (planes, r + 1 < planes)):

            @pl.when(cond)
            def _():
                arrived(landing.at[slot], arrive.at[slot])
                total[...] = (total[...].astype(F32) + landing[slot].astype(F32)).astype(total.dtype)

    nf_all = b.nfA.reshape(PLANE * tok, dm.d)
    g_all = b.gA.reshape(PLANE * tok, dm.d)
    wide_rows = half * tok
    chunk = 2 * LANES

    def gate_grad(h):
        width = dm.parts[h][1]

        def some(start, count):
            cols = pl.ds(start, count)
            total = mm_tn(nf_all[:wide_rows, cols], BIG[:, base[h] : base[h] + 2 * width])
            total = total + mm_tn(nf_all[wide_rows:, cols], BIG[:, base[h] + 2 * width : base[h] + 4 * width])
            GU[h][cols, :] = total.astype(BF16)

        @pl.loop(0, dm.d // chunk)
        def _(i):
            some(pl.multiple_of(i * chunk, chunk), chunk)

        if dm.d % chunk:
            some(dm.d - dm.d % chunk, dm.d % chunk)

    @pl.loop(0, PLANE)
    def _(turn):
        feed(0, turn // 2, turn % 2)

        @pl.when(turn == half - 1)
        def _():
            for item in gate_on[1][1:]:
                pass_on(*item)

    drain("gate0")
    gate_grad(0)
    chain_start(gate_part(0), b.zR0, b.rZ0)
    for item in gate_on[1]:
        settle(*item)

    def join(where):
        for part, one, arrive in ((b.dP, b.dR1, b.rD1), (b.oP, b.oR1, b.rO1)):
            arrived(one.at[where], arrive.at[where])
            part[where, c] = (part[where, c].astype(F32) + one[where].astype(F32)).astype(BF16)

    @pl.loop(0, CHIPS)
    def _(step):
        where = (q + 1 + step) % CHIPS

        @pl.loop(0, 2)
        def _(turn):
            feed(1, where, (other + turn) % 2)

            @pl.when(turn == 0)
            def _():
                first_copy(where, b.dP, b.dR1, b.dsem, b.rD1).start()
                first_copy(where, b.oP, b.oR1, b.osem, b.rO1).start()

        @pl.when(step > 0)
        def _():
            join((q + step) % CHIPS)
            second_copy(step, b.dP, b.dR2, b.dsem2, b.rD2).start()

    for k in range(1, CHIPS):
        second_copy(k, b.oP, b.oR2, b.osem2, b.rO2).start()
    join(q)

    def attn_part(plane):
        return b.aR2.at[0, plane]

    drain("down")
    WD[...] = mm_tn(ACT[...], g_all[...]).astype(BF16)
    chain_start(down_part, b.zD, b.rW)
    drain("gate1")
    gate_grad(1)
    chain_start(gate_part(1), b.zR1, b.rZ1)
    chain_step(gate_part(0), b.zR0, b.rZ0, 0)
    d_nf = b.dP[q, c].astype(F32)
    for k in range(1, CHIPS):
        arrived(b.dR2.at[k - 1], b.rD2.at[k - 1])
        d_nf = d_nf + b.dR2[k - 1].astype(F32)
    hidden = b.hid[...]
    scale2 = lax.rsqrt(jnp.mean(hidden * hidden, axis=-1, keepdims=True) + 1e-06)

    def norm_back(grad, field, scale, gain):
        weighted = grad * gain
        d_gain = jnp.sum(grad * field * scale, axis=0, keepdims=True)
        d_field = weighted * scale - field * (scale * scale * scale) * jnp.mean(
            weighted * field, axis=-1, keepdims=True
        )
        return d_gain, d_field

    d_gain2, d_part = norm_back(d_nf, hidden, scale2, b.vec[2:3])
    d_hidden = b.g[...].astype(F32) + d_part
    b.dhid[...] = d_hidden
    d_attn = d_hidden.astype(BF16)
    BIG[:, dm.qkv : dm.wide] = mm_tn(b.mpad[...], d_attn).astype(BF16)
    d_mixed = mm_nt(d_attn, W[:, dm.qkv :]).astype(BF16)
    d_mixed = mm_nt(d_mixed, b.spr[...])
    d_values = []
    for m in range(dm.micro):
        here = slice(m * dm.slots, (m + 1) * dm.slots)
        stack_heads(d_mixed[here], head_rows)
        d_v, d_k = [], []
        for kv in range(KV_HEADS):
            rows = slice(kv * span, (kv + 1) * span)
            d_mix, prob, qs = dms[kv][...], b.PF[m, rows], b.QS[m, rows]
            d_v.append(mm_tn(prob.astype(BF16), d_mix))
            d_prob = mm_nt(d_mix, b.vd[kv, here])
            delta = jnp.sum(d_prob * prob, axis=-1, keepdims=True)
            d_score = (prob * (d_prob - delta)).astype(BF16)
            d_k.append(0.125 * mm_tn(d_score, qs))
            b.PF[m, rows] = 0.125 * mm(d_score, b.kd[kv, here])
        for t in range(HEADS // 2):
            even = b.PF[m, 2 * t * dm.slots : (2 * t + 1) * dm.slots]
            odd = b.PF[m, (2 * t + 1) * dm.slots : (2 * t + 2) * dm.slots]
            b.FQ[here, t * LANES : (t + 1) * LANES] = jnp.where(low, even, odd)

        def joined(pair):
            zero, one = (piece + pltpu.roll(piece, HEAD_DIM, 1) for piece in pair)
            return jnp.where(low, zero, one)

        b.FQ[here, dm.heads : dm.heads + dm.kv] = joined(d_k)
        d_values.append(joined(d_v))
    d_turned = b.FQ[...]
    cosine = jnp.concatenate([b.tabs[0]] * reps, axis=1)
    sine = jnp.concatenate([b.tabs[1]] * reps, axis=1)
    first, ahead, behind = half_turn(d_turned * sine)
    d_lin = (d_turned * cosine + jnp.where(first, ahead, -behind)).astype(BF16)
    d_lin = jnp.concatenate([d_lin, jnp.concatenate(d_values, axis=0).astype(BF16)], axis=1)
    BIG[:, : dm.qkv] = mm_tn(b.npad[...], d_lin).astype(BF16)
    d_bias = jnp.sum(d_lin.astype(F32), axis=0, keepdims=True)
    d_normed = split_mm(mm_nt(d_lin, W[:, : dm.qkv]), b.spr[...], nt=True)
    xf = b.x[...].astype(F32)
    scale1 = lax.rsqrt(jnp.mean(xf * xf, axis=-1, keepdims=True) + 1e-06)
    d_gain1, d_part = norm_back(d_normed, xf, scale1, b.vec[0:1])
    b.gin[...] = (b.dhid[...] + d_part).astype(BF16)

    rows8 = iota((8, dm.d), 0)
    packed = jnp.zeros((8, dm.d), F32)
    for i, piece in enumerate((d_gain1, d_bias[:, : dm.heads], d_gain2)):
        packed = jnp.where(rows8 == i, piece, packed)
    packed = split_mm(packed, b.spr[...])
    mine = own_block(dm)
    spare = jnp.zeros((n, LANES), F32)
    for i in range(3):
        piece = jnp.where(mine, packed[i : i + 1], 0.0).astype(BF16)
        spare = spare + mm_nt(piece, field_matrix(dm, i * FIELD))
    piece = jnp.where(value_block(dm), d_bias[:, dm.heads + dm.kv :], 0.0).astype(BF16)
    spare = spare + mm_nt(piece, value_field(dm))
    key_bias = jnp.broadcast_to(d_bias[:, dm.heads : dm.heads + dm.kv], (n, LANES))
    spare = jnp.concatenate([spare, key_bias], axis=1).astype(BF16)
    BIG[:, : 2 * LANES] = (
        BIG[:, : 2 * LANES].astype(F32) + mm_tn(spare_rows(dm), spare)
    ).astype(BF16)

    cols = pl.ds(0, dm.wide)

    def quad(plane):
        return pl.ds(plane * CHIPS, CHIPS)

    for to in (*far, r):
        send(b.BIG.at[quad(to), other, :, cols], b.aR1.at[quad(to)], b.rA1.at[to], (partner,))
    for to in (*far, r):
        arrived(b.aR1.at[quad(to)], b.rA1.at[to])
        mine_now = b.BIG[quad(to), c, :, cols].astype(F32) + b.aR1[quad(to)].astype(F32)
        b.aR1[quad(to)] = mine_now.astype(BF16)
        for j in range(1, CHIPS):
            where = (q + j) % CHIPS
            send(
                b.aR1.at[to * CHIPS + where],
                b.aR2.at[j - 1, to],
                b.rA2.at[j - 1, to],
                dev(r, where * 2 + c),
            )
    total = b.hid[...] + b.oP[q, c].astype(F32)
    for k in range(1, CHIPS):
        arrived(b.oR2.at[k - 1], b.rO2.at[k - 1])
        total = total + b.oR2[k - 1].astype(F32)
    b.out[...] = total.astype(BF16)
    for k in range(1, planes - 1):
        chain_step(gate_part(0), b.zR0, b.rZ0, k)
    for k in range(planes - 1):
        chain_step(down_part, b.zD, b.rW, k)
    for k in range(planes - 2):
        chain_step(gate_part(1), b.zR1, b.rZ1, k)
    for to in (*far, r):
        total = b.aR1[to * CHIPS + q].astype(F32)
        for j in range(1, CHIPS):
            arrived(b.aR2.at[j - 1, to], b.rA2.at[j - 1, to])
            total = total + b.aR2[j - 1, to].astype(F32)
        b.aR2[0, to] = total.astype(BF16)
    chain_start(attn_part, b.aR3, b.rA3)
    squeeze = b.spr[: dm.unit, : PLANE * rp]

    def home(h, landing, arrive, final):
        start, width = dm.parts[h]
        cols = pl.ds(start, width)
        chain_end(gate_part(h)(r), landing, arrive)
        for i in range(2):
            piece = mm_tn(squeeze, GU[h][my_rows, i * width : (i + 1) * width]).astype(BF16)
            piece = piece.reshape(PLANE, rp, width)
            for place in range(PLANE):
                b.act[2 * place + i, :, cols] = piece[place]
        for k in range(1, PLANE):
            to = (p + k) % PLANE
            send(b.act.at[pl.ds(2 * to, 2), :, cols], b.fgu.at[p, :, :, cols], final.at[p], dev(r, to))
        b.fgu[p, :, :, cols] = b.act[pl.ds(2 * p, 2), :, cols]

    home(0, b.zR0, b.rZ0, b.rF0)
    chain_step(gate_part(1), b.zR1, b.rZ1, planes - 2)
    home(1, b.zR1, b.rZ1, b.rF1)
    for k in range(planes - 1):
        chain_step(attn_part, b.aR3, b.rA3, k)
    b.fwd[...] = b.WD[r].astype(F32)
    chain_end(b.fwd, b.zD, b.rW)
    b.fa[...] = b.aR2[0, r].astype(F32)
    chain_end(b.fa, b.aR3, b.rA3)
    for k in range(1, PLANE):
        origin = (p + PLANE - k) % PLANE
        for (start, width), final in zip(dm.parts, (b.rF0, b.rF1)):
            arrived(b.fgu.at[origin, :, :, pl.ds(start, width)], final.at[origin])
    for where in range(CHIPS):
        first_copy(where, b.oP, b.oR1, b.osem, b.rO1).wait_send()
        first_copy(where, b.dP, b.dR1, b.dsem, b.rD1).wait_send()
    for k in range(1, CHIPS):
        second_copy(k, b.oP, b.oR2, b.osem2, b.rO2).wait_send()
        second_copy(k, b.dP, b.dR2, b.dsem2, b.rD2).wait_send()
    drain()


def run_layer(dm, operands):
    n, planes, rp, tok = dm.n, dm.planes, dm.rp, dm.tok
    vm = pltpu.VMEM
    sem = pltpu.SemaphoreType.DMA
    quads = planes * CHIPS
    pairs = dm.heads + dm.kv
    outs = {
        "out": jax.ShapeDtypeStruct((tok, dm.d), BF16),
        "gin": jax.ShapeDtypeStruct((tok, dm.d), BF16),
        "fa": jax.ShapeDtypeStruct((rp, dm.wide), F32),
        "fgu": jax.ShapeDtypeStruct((PLANE, 2, rp, dm.ffr), BF16),
        "fwd": jax.ShapeDtypeStruct((dm.rfp, dm.d), F32),
    }
    n_sends = 1 + (planes - 1) * 16 + 16 * PLANE + 8 * quads + 64
    scratch = {
        "W": vm((quads, 2, rp, dm.wide), BF16),
        "GU0": vm((planes * dm.groups, dm.gs, 2 * dm.parts[0][1]), BF16),
        "GU1": vm((planes * dm.groups, dm.gs, 2 * dm.parts[1][1]), BF16),
        "WD": vm((planes, dm.rfp, dm.d), BF16),
        "nfA": vm((PLANE, tok, dm.d), BF16),
        "gA": vm((PLANE, tok, dm.d), BF16),
        "act": vm((PLANE * tok // rp, rp, dm.ffr), BF16),
        "BIG": vm((quads, 2, rp, 4 * dm.ffr), BF16),
        "oP": vm((CHIPS, 2, tok, dm.d), BF16),
        "dP": vm((CHIPS, 2, tok, dm.d), BF16),
        "oR1": vm((CHIPS, tok, dm.d), BF16),
        "dR1": vm((CHIPS, tok, dm.d), BF16),
        "oR2": vm((CHIPS - 1, tok, dm.d), BF16),
        "dR2": vm((CHIPS - 1, tok, dm.d), BF16),
        "zR0": vm((planes + 1, dm.groups, dm.gs, 2 * dm.parts[0][1]), BF16),
        "zR1": vm((planes + 1, dm.groups, dm.gs, 2 * dm.parts[1][1]), BF16),
        "zD": vm((planes + 1, dm.rfp, dm.d), BF16),
        "aR1": vm((quads, rp, dm.wide), BF16),
        "aR2": vm((CHIPS - 1, planes, rp, dm.wide), BF16),
        "aR3": vm((planes + 1, rp, dm.wide), BF16),
        "QS": vm((dm.micro, HEADS * dm.slots, LANES), BF16),
        "PF": vm((dm.micro, HEADS * dm.slots, dm.slots), F32),
        "hid": vm((tok, dm.d), F32),
        "dhid": vm((tok, dm.d), F32),
        "npad": vm((tok, dm.dp), BF16),
        "mpad": vm((tok, dm.dp), BF16),
        "spr": vm((dm.d, dm.dp), BF16),
        "kd": vm((KV_HEADS, tok, LANES), BF16),
        "vd": vm((KV_HEADS, tok, LANES), BF16),
        "FQ": vm((tok, pairs), F32),
        "tabs": vm((2, tok, LANES), F32),
        "vec": vm((8, dm.d), F32),
        "ssem": sem((n_sends,)),
        "csem": sem((4,)),
        "osem": sem((CHIPS,)),
        "dsem": sem((CHIPS,)),
        "osem2": sem((CHIPS - 1,)),
        "dsem2": sem((CHIPS - 1,)),
        "rA": sem((n,)),
        "rGU": sem((PLANE,)),
        "rGZ0": sem((planes,)),
        "rGZ1": sem((planes,)),
        "rG": sem((PLANE,)),
        "rWD": sem((planes,)),
        "rNF": sem((PLANE,)),
        "rO1": sem((CHIPS,)),
        "rD1": sem((CHIPS,)),
        "rO2": sem((CHIPS - 1,)),
        "rD2": sem((CHIPS - 1,)),
        "rZ0": sem((planes + 1,)),
        "rZ1": sem((planes + 1,)),
        "rF0": sem((PLANE,)),
        "rF1": sem((PLANE,)),
        "rW": sem((planes + 1,)),
        "rA1": sem((planes,)),
        "rA2": sem((CHIPS - 1, planes)),
        "rA3": sem((planes + 1,)),
    }
    return pl.pallas_call(
        functools.partial(layer_kernel, dm, (*operands, *outs, *scratch)),
        name="layer",
        out_shape=list(outs.values()),
        in_specs=[pl.BlockSpec(memory_space=pltpu.VMEM)] * len(operands),
        out_specs=[pl.BlockSpec(memory_space=pltpu.VMEM)] * len(outs),
        scratch_shapes=list(scratch.values()),
        compiler_params=pltpu.CompilerParams(
            collective_id=0, has_side_effects=True, vmem_limit_bytes=67043328
        ),
    )(*operands.values())


def per_device(n, *args):
    (
        tokens,
        positions,
        cotangent,
        norm_attn,
        w_query,
        b_query,
        w_key,
        b_key,
        w_value,
        b_value,
        w_out,
        norm_ffn,
        w_gate,
        w_up,
        w_down,
    ) = args
    micro, slots, d = tokens.shape
    dm = Dims(n, d, w_gate.shape[0] * n // d, slots, micro)
    rows, rp = dm.rows, dm.rp

    def lanes(vector):
        return jnp.pad(vector, (0, FIELD - vector.shape[0]))

    spare = jnp.concatenate([lanes(v) for v in (norm_attn, b_query, norm_ffn, b_value)])
    spare = jnp.pad(spare, (0, dm.wide - spare.shape[0]))
    pack = jnp.concatenate(
        [w.reshape(rows, -1) for w in (w_query, w_key, w_value, w_out)], axis=1
    )
    pack = jnp.concatenate([pack, spare[None]], axis=0)
    pack = jnp.pad(pack, ((0, rp - rows - 1), (0, 0)))

    def columns(weight):
        weight = weight.reshape(rows, dm.planes, PLANE, dm.rf)
        weight = jnp.pad(weight, ((0, rp - rows), (0, 0), (0, 0), (0, dm.rfp - dm.rf)))
        return weight.transpose(2, 0, 1, 3).reshape(PLANE, rp, dm.ffr)

    both = jnp.stack([columns(w_gate), columns(w_up)], axis=1)
    down = jnp.pad(w_down.reshape(dm.rf, d), ((0, dm.rfp - dm.rf), (0, 0)))
    operands = {
        "x": tokens.reshape(dm.tok, d),
        "g": cotangent.reshape(dm.tok, d),
        "posr": positions,
        "bkey": b_key[None],
        "ap": pack,
        "gus": both,
        "wds": down,
    }
    out, gin, fa, fgu, fwd = run_layer(dm, operands)

    def field(i, size):
        return fa[rows, i * FIELD : i * FIELD + size]

    def flat(start, stop):
        return fa[:rows, start:stop].reshape(-1)

    def gate_part(i):
        part = fgu[:, i, :rows].astype(F32)
        part = part.reshape(PLANE, rows, dm.planes, dm.rfp)[..., : dm.rf]
        return part.transpose(1, 2, 0, 3).reshape(-1)

    h, kv = dm.heads, dm.kv
    return (
        out.reshape(micro, slots, d),
        gin.reshape(micro, slots, d),
        field(0, rows),
        flat(0, h),
        field(1, rows),
        flat(h, h + kv),
        fa[rows, LANES : LANES + kv],
        flat(h + kv, h + 2 * kv),
        field(3, dm.rv),
        flat(h + 2 * kv, dm.wide),
        field(2, rows),
        gate_part(0),
        gate_part(1),
        fwd[: dm.rf].reshape(-1),
    )


def solution(mesh):
    n = mesh.shape["dp"]
    split, row = P("dp"), P(None, "dp", None)
    in_specs = (row, P(None, "dp"), row, *[split] * 4, P(), *[split] * 7)
    out_specs = (row, row, *[split] * 4, P(), *[split] * 7)
    return jax.shard_map(
        functools.partial(per_device, n),
        mesh=mesh,
        in_specs=in_specs,
        out_specs=out_specs,
        check_vma=False,
    )
```

```python
import functools
import math

import jax
import jax.numpy as jnp
from jax import lax
from jax.experimental import pallas as pl
from jax.experimental.pallas import tpu as pltpu
from jax.sharding import PartitionSpec as P

HEADS = 14
KV_HEADS = 2
HEAD_DIM = 64
GROUP = HEADS // KV_HEADS
PLANE = 8
CHIPS = 4
LANES = 128
ROTARY_LOG = math.log(1000000.0)
FIELD = 32
MESH = pl.DeviceIdType.MESH
F32 = jnp.float32
BF16 = jnp.bfloat16


def up(value, step):
    return -(-value // step) * step


def mm(left, right, dims=((1,), (0,))):
    return lax.dot_general(left, right, (dims, ((), ())), preferred_element_type=F32)


def mm_nt(left, right):
    return mm(left, right, ((1,), (1,)))


def mm_tn(left, right):
    return mm(left, right, ((0,), (0,)))


def split_mm(left, right, nt=False):
    high = left.astype(BF16)
    low = (left - high.astype(F32)).astype(BF16)
    dot = mm_nt if nt else mm
    return dot(high, right) + dot(low, right)


def iota(shape, dim):
    return lax.broadcasted_iota(jnp.int32, shape, dim)


class Dims:
    def __init__(self, n, d, ff, slots, micro):
        self.n, self.d, self.ff = n, d, ff
        self.planes = n // PLANE
        self.rows = d // n
        self.rp = 8
        while self.rp < self.rows + 1:
            self.rp *= 2
        self.dp = n * self.rp
        self.rf = ff // n
        self.ffr = up(ff // PLANE, LANES)
        self.rfp = self.ffr // self.planes
        self.slots, self.micro = slots, micro
        self.tok = slots * micro
        self.heads = HEADS * HEAD_DIM
        self.kv = KV_HEADS * HEAD_DIM
        self.qkv = self.heads + 2 * self.kv
        self.wide = self.qkv + d
        self.rv = self.kv // n
        self.unit = PLANE * self.rows
        self.gs = 16 if self.unit % 16 == 0 else 8
        self.groups = self.unit // self.gs
        blocks = self.ffr // LANES
        wide = (blocks + 1) // 2 * LANES
        self.parts = ((0, wide), (wide, self.ffr - wide))


def spread_matrix(dm):
    shape = (dm.d, dm.dp)
    row, col = iota(shape, 0), iota(shape, 1)
    inner = col & (dm.rp - 1)
    hit = (row == (col // dm.rp) * dm.rows + inner) & (inner < dm.rows)
    return jnp.where(hit, 1.0, 0.0).astype(BF16)


def field_matrix(dm, offset):
    shape = (LANES, dm.dp)
    row, col = iota(shape, 0), iota(shape, 1)
    inner = col & (dm.rp - 1)
    return jnp.where((row == offset + inner) & (inner < dm.rows), 1.0, 0.0).astype(BF16)


def own_block(dm):
    shape = (dm.n, dm.dp)
    return iota(shape, 1) // dm.rp == iota(shape, 0)


def spare_rows(dm):
    shape = (dm.n, dm.dp)
    return jnp.where(iota(shape, 1) == iota(shape, 0) * dm.rp + dm.rows, 1.0, 0.0).astype(BF16)


def value_field(dm):
    shape = (LANES, LANES)
    return jnp.where(
        iota(shape, 0) == 3 * FIELD + (iota(shape, 1) & (dm.rv - 1)), 1.0, 0.0
    ).astype(BF16)


def value_block(dm):
    shape = (dm.n, LANES)
    return iota(shape, 1) // dm.rv == iota(shape, 0)


def half_turn(field):
    width = field.shape[-1]
    first = (iota(field.shape, 1) & (HEAD_DIM - 1)) < HEAD_DIM // 2
    ahead = pltpu.roll(field, width - HEAD_DIM // 2, 1)
    behind = pltpu.roll(field, HEAD_DIM // 2, 1)
    return first, ahead, behind


def twice(field):
    low = iota(field.shape, 1) < HEAD_DIM
    turned = pltpu.roll(field, HEAD_DIM, 1)
    return jnp.where(low, field, turned), jnp.where(low, turned, field)


class Refs:
    def __init__(self, names, refs):
        self.__dict__.update(zip(names, refs, strict=True))


def layer_kernel(dm, names, *refs):
    b = Refs(names, refs)
    n, planes, rp = dm.n, dm.planes, dm.rp
    me = lax.axis_index("dp")
    r, p = me // PLANE, me % PLANE
    q, c = p // 2, p % 2
    other = 1 - c
    partner = r * PLANE + q * 2 + other

    def dev(plane, place):
        return (plane * PLANE + place,)

    barrier = pltpu.get_barrier_semaphore()
    peers = [dev(r, (p + k) % PLANE) for k in range(1, PLANE)]
    peers += [dev((r + k) % planes, p) for k in range(1, planes)]
    for peer in peers:
        pl.semaphore_signal(barrier, inc=1, device_id=peer, device_id_type=MESH)
    pl.semaphore_wait(barrier, len(peers))

    pending = []
    count = [0]

    def prepare(src, dst, arrive, to, cond=None, tag=None):
        copy = pltpu.make_async_remote_copy(
            src_ref=src,
            dst_ref=dst,
            send_sem=b.ssem.at[count[0]],
            recv_sem=arrive,
            device_id=to,
            device_id_type=MESH,
        )
        count[0] += 1
        pending.append((copy, cond, tag))
        return copy

    def send(src, dst, arrive, to, cond=None, tag=None):
        copy = prepare(src, dst, arrive, to, cond, tag)
        if cond is None:
            copy.start()
        else:
            pl.when(cond)(copy.start)

    def drain(tag=None):
        now = [item for item in pending if tag in (None, item[2])]
        for copy, cond, _ in now:
            if cond is None:
                copy.wait_send()
            else:
                pl.when(cond)(copy.wait_send)
        pending[:] = [item for item in pending if tag not in (None, item[2])]

    upper = r // max(planes // 2, 1)
    mirror = r + upper * (planes - 1 - 2 * r)

    def origin_of(k):
        spot = k - (mirror + planes - k) // planes
        return spot + upper * (planes - 1 - 2 * spot)

    def relay_own(src, dst, arrive, tag=None):
        send(src, dst, arrive, dev(r + 1, p), r + 1 < planes, tag)
        send(src, dst, arrive, dev(r - 1, p), r >= 1, tag)

    def onward(part, sems, k, tag=None):
        origin = origin_of(k)
        to = r - 1 + 2 * ((r - origin - 1 + planes) // planes)
        cond = (to >= 0) & (to < planes)
        piece, arrive = part(origin), sems.at[origin]
        return piece, arrive, cond, prepare(piece, piece, arrive, dev(to, p), cond, tag)

    def pass_on(piece, arrive, cond, copy):
        @pl.when(cond)
        def _():
            arrived(piece, arrive)
            copy.start()

    def settle(piece, arrive, cond, copy):
        pl.when(jnp.logical_not(cond))(lambda: arrived(piece, arrive))

    def arrived(dst, arrive):
        pltpu.make_async_remote_copy(
            src_ref=dst,
            dst_ref=dst,
            send_sem=b.ssem.at[0],
            recv_sem=arrive,
            device_id=(partner,),
            device_id_type=MESH,
        ).wait_recv()

    def block(ref, index):
        return ref.at[index // 2, index % 2]

    def plane_rows(ref, plane):
        return ref.at[pl.ds(plane * dm.groups, dm.groups)]

    keep = [
        pltpu.make_async_copy(b.ap, block(b.W, me), b.csem.at[0]),
        pltpu.make_async_copy(b.gus.at[p], b.fgu.at[p], b.csem.at[1]),
        pltpu.make_async_copy(b.g, b.gA.at[p], b.csem.at[2]),
        pltpu.make_async_copy(b.wds, b.WD.at[r], b.csem.at[3]),
    ]
    for copy in keep:
        copy.start()

    relay_own(b.ap, block(b.W, me), b.rA.at[me])

    across, along = q + 1 - 2 * (q % 2), (q + 2) % CHIPS
    near = across * other + along * c
    next_to = along * other + across * c
    spots = (near, next_to, CHIPS - 1 - q)

    def fan(index, src):
        for where in (next_to, near):
            send(src, block(b.W, index), b.rA.at[index], dev(r, where * 2 + c))

    def spread_out(src, ref, arrive):
        for where in (next_to, near):
            send(src, ref.at[p], arrive.at[p], dev(r, where * 2 + c))
        send(src, ref.at[p], arrive.at[p], (partner,))

    def take_in(ref, arrive):
        for i, where in enumerate(spots):
            place = where * 2 + c
            arrived(ref.at[place], arrive.at[place])
            if i == 0:
                send(ref.at[place], ref.at[place], arrive.at[place], dev(r, next_to * 2 + c))
            send(ref.at[place], ref.at[place], arrive.at[place], (partner,))

    fan(me, b.ap)
    send(b.ap, block(b.W, me), b.rA.at[me], (partner,))
    for k in range(1, PLANE):
        send(b.gus.at[(p + k) % PLANE], b.fgu.at[p], b.rGU.at[p], dev(r, (p + k) % PLANE))
    relay_own(b.wds, b.WD.at[r], b.rWD.at[r])

    tok = dm.tok
    xf = b.x[...].astype(F32)
    scale1 = lax.rsqrt(jnp.mean(xf * xf, axis=-1, keepdims=True) + 1e-06)
    diagonal = iota((dm.slots, dm.slots), 0) == iota((dm.slots, dm.slots), 1)
    posc = [
        jnp.sum(jnp.where(diagonal, b.posr[m : m + 1].astype(F32), 0.0), axis=1, keepdims=True)
        for m in range(dm.micro)
    ]
    power = (iota((1, LANES), 1) & (HEAD_DIM // 2 - 1)).astype(F32) * (-2.0 / HEAD_DIM * ROTARY_LOG)
    angle = jnp.concatenate(posc, axis=0) * jnp.exp(power)
    b.tabs[0] = jnp.cos(angle)
    b.tabs[1] = jnp.sin(angle)
    b.spr[...] = spread_matrix(dm)

    for k in range(1, planes):
        origin = origin_of(k)
        index = origin * PLANE + p
        arrived(block(b.W, index), b.rA.at[index])
        to = r - 1 + 2 * ((r - origin - 1 + planes) // planes)
        send(block(b.W, index), block(b.W, index), b.rA.at[index], dev(to, p), (to >= 0) & (to < planes))
        fan(index, block(b.W, index))
        send(block(b.W, index), block(b.W, index), b.rA.at[index], (partner,))
    for k in range(1, PLANE):
        origin = (p + PLANE - k) % PLANE
        arrived(b.fgu.at[origin], b.rGU.at[origin])
    keep[1].wait()
    GU = [ref.reshape(dm.d, ref.shape[-1]) for ref in (b.GU0, b.GU1)]
    my_rows = pl.ds(pl.multiple_of(r * dm.unit, dm.gs), dm.unit)
    squeeze = b.spr[: dm.unit, : PLANE * rp]
    for h, (start, width) in enumerate(dm.parts):
        for i in range(2):
            piece = b.fgu[:, i, :, start : start + width].reshape(PLANE * rp, width)
            GU[h][my_rows, i * width : (i + 1) * width] = mm(squeeze, piece).astype(BF16)

    def gate_part(h):
        ref = (b.GU0, b.GU1)[h]
        return lambda plane: plane_rows(ref, plane)

    def down_part(plane):
        return b.WD.at[plane]

    relay_own(gate_part(0)(r), gate_part(0)(r), b.rGZ0.at[r], "gate0")
    steps = range(1, planes)
    down_on = [onward(down_part, b.rWD, k, "down") for k in steps]
    gate_on = [[onward(gate_part(h), sems, k, f"gate{h}") for k in steps] for h, sems in ((0, b.rGZ0), (1, b.rGZ1))]
    pass_on(*down_on[0])
    origins = [r, *(origin_of(k) for k in steps)]
    for i, where in enumerate(spots):
        for origin in origins:
            index = origin * PLANE + where * 2 + c
            arrived(block(b.W, index), b.rA.at[index])
            if i == 0:
                send(block(b.W, index), block(b.W, index), b.rA.at[index], dev(r, next_to * 2 + c))
            send(block(b.W, index), block(b.W, index), b.rA.at[index], (partner,))
    spread_out(b.g, b.gA, b.rG)
    for item in down_on[1:]:
        pass_on(*item)

    keep[0].wait()
    for k in range(CHIPS):
        for shift in range(planes):
            index = ((r + planes - shift) % planes) * PLANE + ((q + CHIPS - k) % CHIPS) * 2 + other
            arrived(block(b.W, index), b.rA.at[index])

    W = b.W.reshape(dm.dp, dm.wide)
    small = mm(spare_rows(dm), W[:, :LANES]).astype(BF16)
    mine = own_block(dm)
    rows8 = iota((8, dm.dp), 0)
    padded = jnp.zeros((8, dm.dp), F32)
    for i in range(3):
        piece = mm(small, field_matrix(dm, i * FIELD))
        piece = jnp.sum(jnp.where(mine, piece, 0.0), axis=0, keepdims=True)
        padded = jnp.where(rows8 == i, piece, padded)
    b.vec[...] = mm_nt(padded.astype(BF16), b.spr[...])
    gain1, bias_q, gain2 = b.vec[0:1], b.vec[1:2], b.vec[2:3]
    bias_v = jnp.sum(
        jnp.where(value_block(dm), mm(small, value_field(dm)), 0.0), axis=0, keepdims=True
    )
    bias_k = b.bkey[...].astype(F32)

    normed = (xf * scale1 * gain1).astype(BF16)
    b.npad[...] = mm(normed, b.spr[...]).astype(BF16)
    lin = mm(b.npad[...], W[:, : dm.qkv])
    turn_in = jnp.concatenate([lin[:, : dm.heads] + bias_q, lin[:, dm.heads : dm.heads + dm.kv] + bias_k], axis=1)
    reps = (dm.heads + dm.kv) // LANES
    cosine = jnp.concatenate([b.tabs[0]] * reps, axis=1)
    sine = jnp.concatenate([b.tabs[1]] * reps, axis=1)
    first, ahead, behind = half_turn(turn_in)
    turned = turn_in * cosine + jnp.where(first, -ahead, behind) * sine
    values = lin[:, dm.heads + dm.kv :] + bias_v
    for i, piece in enumerate(twice(turned[:, dm.heads :])):
        b.kd[i] = piece.astype(BF16)
    for i, piece in enumerate(twice(values)):
        b.vd[i] = piece.astype(BF16)
    low = iota((dm.slots, LANES), 1) < HEAD_DIM

    def stack_heads(field, store):
        for h in range(HEADS):
            part = field[:, LANES * (h // 2) : LANES * (h // 2) + LANES]
            part = jnp.where(low if h % 2 == 0 else ~low, part, 0.0)
            store(h)[...] = part.astype(BF16)

    span = GROUP * dm.slots
    mix = b.oP.at[0, 0]
    BIG = b.BIG.reshape(dm.dp, 4 * dm.ffr)
    dms = [BIG.at[:span, dm.wide + kv * LANES : dm.wide + (kv + 1) * LANES] for kv in range(KV_HEADS)]

    def head_rows(h):
        return dms[h // GROUP].at[(h % GROUP) * dm.slots : (h % GROUP + 1) * dm.slots]

    for m in range(dm.micro):
        here = slice(m * dm.slots, (m + 1) * dm.slots)
        stack_heads(turned[here, : dm.heads], lambda h: b.QS.at[m, h * dm.slots : (h + 1) * dm.slots])
        grid = (dm.slots, dm.slots)
        start_row = iota((dm.slots, 1), 0).astype(F32) - posc[m]
        start_col = (iota((1, dm.slots), 1) - b.posr[m : m + 1]).astype(F32)
        allowed = (start_row == start_col) & (iota(grid, 1) <= iota(grid, 0))
        for kv in range(KV_HEADS):
            rows = slice(kv * span, (kv + 1) * span)
            score = mm_nt(b.QS[m, rows], b.kd[kv, here]) * 0.125
            score = jnp.where(allowed[None], score.reshape(GROUP, *grid), -1e30)
            top = jnp.max(score, axis=-1, keepdims=True)
            expo = jnp.exp(score - top)
            prob = expo / jnp.sum(expo, axis=-1, keepdims=True)
            prob = prob.reshape(span, dm.slots)
            b.PF[m, rows] = prob
            dms[kv][...] = mm(prob.astype(BF16), b.vd[kv, here]).astype(BF16)
        for t in range(HEADS // 2):
            even, odd = head_rows(2 * t)[...], head_rows(2 * t + 1)[...]
            mix[here, t * LANES : (t + 1) * LANES] = jnp.where(low, even, odd)
    b.mpad[...] = mm(mix[...], b.spr[...]).astype(BF16)
    hidden = xf + mm(b.mpad[...], W[:, dm.qkv :])
    b.hid[...] = hidden
    scale2 = lax.rsqrt(jnp.mean(hidden * hidden, axis=-1, keepdims=True) + 1e-06)
    nf = (hidden * scale2 * gain2).astype(BF16)
    b.nfA[p] = nf

    spread_out(b.nfA.at[p], b.nfA, b.rNF)
    pass_on(*gate_on[0][0])
    relay_own(gate_part(1)(r), gate_part(1)(r), b.rGZ1.at[r], "gate1")
    take_in(b.gA, b.rG)
    for item in gate_on[0][1:]:
        pass_on(*item)
    take_in(b.nfA, b.rNF)
    for item in (*down_on, *gate_on[0]):
        settle(*item)
    pass_on(*gate_on[1][0])
    keep[2].wait()
    keep[3].wait()
    for k in range(CHIPS):
        place = ((q + CHIPS - k) % CHIPS) * 2 + other
        arrived(b.gA.at[place], b.rG.at[place])
        arrived(b.nfA.at[place], b.rNF.at[place])

    ACT = b.act.reshape(PLANE * tok, dm.ffr)
    WD = b.WD.reshape(dm.ffr, dm.d)
    half = PLANE // 2

    base = (0, 4 * dm.parts[0][1])

    def feed(h, place_q, place_c):
        place = place_q * 2 + place_c
        start, width = dm.parts[h]
        nf_t, g_t = b.nfA[place], b.gA[place]
        down = WD[start : start + width]
        pre = mm(nf_t, GU[h][...])
        gate, upper = pre[:, :width], pre[:, width:]
        sigma = jax.nn.sigmoid(gate)
        silu = gate * sigma
        act = (silu * upper).astype(BF16)
        ACT[pl.ds(pl.multiple_of(place * tok, tok), tok), start : start + width] = act
        d_act = mm_nt(g_t, down)
        d_gate = (d_act * upper * (sigma + silu * (1.0 - sigma))).astype(BF16)
        d_up = (d_act * silu).astype(BF16)
        d_both = jnp.concatenate([d_gate, d_up], axis=1)
        rows = pl.ds(pl.multiple_of((place % half) * tok, tok), tok)
        cols = pl.ds(pl.multiple_of(base[h] + (place // half) * 2 * width, LANES), 2 * width)
        BIG[rows, cols] = d_both
        for ref, value in ((b.oP, mm(act, down)), (b.dP, mm_nt(d_both, GU[h][...]))):
            if h:
                value = value + ref[place_q, place_c].astype(F32)
            ref[place_q, place_c] = value.astype(BF16)

    def first_copy(where, part, landing, sems, arrive):
        return pltpu.make_async_remote_copy(
            src_ref=part.at[where, other],
            dst_ref=landing.at[where],
            send_sem=sems.at[where],
            recv_sem=arrive.at[where],
            device_id=(partner,),
            device_id_type=MESH,
        )

    diag = CHIPS - 1 - q
    routes = ((diag, near), (near, near), (next_to, next_to))

    def second_copy(slot, part, landing, sems, arrive):
        source, to = routes[slot]
        return pltpu.make_async_remote_copy(
            src_ref=part.at[source, c],
            dst_ref=landing.at[slot],
            send_sem=sems.at[slot],
            recv_sem=arrive.at[slot],
            device_id=dev(r, to * 2 + c),
            device_id_type=MESH,
        )

    def add_on(part, landing, sems, arrive):
        arrived(landing.at[0], arrive.at[0])
        part[next_to, c] = (part[next_to, c].astype(F32) + landing[0].astype(F32)).astype(BF16)
        second_copy(2, part, landing, sems, arrive).start()

    d_route = (b.dP, b.dR2, b.dsem2, b.rD2)
    o_route = (b.oP, b.oR2, b.osem2, b.rO2)

    def hop(part, landing, arrive, to, cond):
        ahead = (to - r - 1 + planes) // planes
        beyond = r - to - 1 + 2 * planes * ahead
        last = 1 - (beyond + 4 * planes - 1) // (4 * planes)
        slot = to + (planes - to) * last
        send(part(to), landing.at[slot], arrive.at[slot], dev(r - 1 + 2 * ahead, p), cond)

    def behind_of(to):
        ahead = (to - r - 1 + planes) // planes
        follows = r + 1 - 2 * ahead
        return (follows >= 0) & (follows < planes)

    far = [origin_of(planes - k) for k in range(1, planes)]

    def chain_start(part, landing, arrive):
        for to in far:
            hop(part, landing, arrive, to, jnp.logical_not(behind_of(to)))

    def chain_step(part, landing, arrive, k):
        to = far[k]
        has = behind_of(to)

        @pl.when(has)
        def _():
            arrived(landing.at[to], arrive.at[to])
            mine = part(to)
            mine[...] = (mine[...].astype(F32) + landing[to].astype(F32)).astype(BF16)

        hop(part, landing, arrive, to, has)

    def chain_end(total, landing, arrive):
        for slot, cond in ((r, r >= 1), (planes, r + 1 < planes)):

            @pl.when(cond)
            def _():
                arrived(landing.at[slot], arrive.at[slot])
                total[...] = (total[...].astype(F32) + landing[slot].astype(F32)).astype(total.dtype)

    nf_all = b.nfA.reshape(PLANE * tok, dm.d)
    g_all = b.gA.reshape(PLANE * tok, dm.d)
    wide_rows = half * tok
    chunk = 2 * LANES

    def gate_grad(h):
        width = dm.parts[h][1]

        def some(start, count):
            cols = pl.ds(start, count)
            total = mm_tn(nf_all[:wide_rows, cols], BIG[:, base[h] : base[h] + 2 * width])
            total = total + mm_tn(nf_all[wide_rows:, cols], BIG[:, base[h] + 2 * width : base[h] + 4 * width])
            GU[h][cols, :] = total.astype(BF16)

        @pl.loop(0, dm.d // chunk)
        def _(i):
            some(pl.multiple_of(i * chunk, chunk), chunk)

        if dm.d % chunk:
            some(dm.d - dm.d % chunk, dm.d % chunk)

    @pl.loop(0, PLANE)
    def _(turn):
        feed(0, turn // 2, turn % 2)

        @pl.when(turn == half - 1)
        def _():
            for item in gate_on[1][1:]:
                pass_on(*item)

    drain("gate0")
    gate_grad(0)
    chain_start(gate_part(0), b.zR0, b.rZ0)
    for item in gate_on[1]:
        settle(*item)

    def join(where):
        for part, one, arrive in ((b.dP, b.dR1, b.rD1), (b.oP, b.oR1, b.rO1)):
            arrived(one.at[where], arrive.at[where])
            part[where, c] = (part[where, c].astype(F32) + one[where].astype(F32)).astype(BF16)

    @pl.loop(0, CHIPS)
    def _(step):
        one, two = (CHIPS - 1 - step) % 2, (CHIPS - 1 - step) // 2
        over_x, over_y = one * other + two * c, two * other + one * c
        where = 2 * ((q // 2 + over_y) % 2) + (q % 2 + over_x) % 2

        @pl.loop(0, 2)
        def _(turn):
            feed(1, where, (other + turn) % 2)

            @pl.when(turn == 0)
            def _():
                first_copy(where, b.dP, b.dR1, b.dsem, b.rD1).start()
                first_copy(where, b.oP, b.oR1, b.osem, b.rO1).start()

        for at, source in ((1, diag), (2, near)):

            @pl.when(step == at)
            def _():
                join(source)
                second_copy(at - 1, *d_route).start()

    join(next_to)
    add_on(*d_route)
    for slot in range(2):
        second_copy(slot, *o_route).start()
    join(q)

    def attn_part(plane):
        return b.aR2.at[0, plane]

    drain("down")
    WD[...] = mm_tn(ACT[...], g_all[...]).astype(BF16)
    chain_start(down_part, b.zD, b.rW)
    drain("gate1")
    gate_grad(1)
    chain_start(gate_part(1), b.zR1, b.rZ1)
    chain_step(gate_part(0), b.zR0, b.rZ0, 0)
    add_on(*o_route)
    d_nf = b.dP[q, c].astype(F32)
    for slot in (1, 2):
        arrived(b.dR2.at[slot], b.rD2.at[slot])
        d_nf = d_nf + b.dR2[slot].astype(F32)
    hidden = b.hid[...]
    scale2 = lax.rsqrt(jnp.mean(hidden * hidden, axis=-1, keepdims=True) + 1e-06)

    def norm_back(grad, field, scale, gain):
        weighted = grad * gain
        d_gain = jnp.sum(grad * field * scale, axis=0, keepdims=True)
        d_field = weighted * scale - field * (scale * scale * scale) * jnp.mean(
            weighted * field, axis=-1, keepdims=True
        )
        return d_gain, d_field

    d_gain2, d_part = norm_back(d_nf, hidden, scale2, b.vec[2:3])
    d_hidden = b.g[...].astype(F32) + d_part
    b.dhid[...] = d_hidden
    d_attn = d_hidden.astype(BF16)
    BIG[:, dm.qkv : dm.wide] = mm_tn(b.mpad[...], d_attn).astype(BF16)
    d_mixed = mm_nt(d_attn, W[:, dm.qkv :]).astype(BF16)
    d_mixed = mm_nt(d_mixed, b.spr[...])
    d_values = []
    for m in range(dm.micro):
        here = slice(m * dm.slots, (m + 1) * dm.slots)
        stack_heads(d_mixed[here], head_rows)
        d_v, d_k = [], []
        for kv in range(KV_HEADS):
            rows = slice(kv * span, (kv + 1) * span)
            d_mix, prob, qs = dms[kv][...], b.PF[m, rows], b.QS[m, rows]
            d_v.append(mm_tn(prob.astype(BF16), d_mix))
            d_prob = mm_nt(d_mix, b.vd[kv, here])
            delta = jnp.sum(d_prob * prob, axis=-1, keepdims=True)
            d_score = (prob * (d_prob - delta)).astype(BF16)
            d_k.append(0.125 * mm_tn(d_score, qs))
            b.PF[m, rows] = 0.125 * mm(d_score, b.kd[kv, here])
        for t in range(HEADS // 2):
            even = b.PF[m, 2 * t * dm.slots : (2 * t + 1) * dm.slots]
            odd = b.PF[m, (2 * t + 1) * dm.slots : (2 * t + 2) * dm.slots]
            b.FQ[here, t * LANES : (t + 1) * LANES] = jnp.where(low, even, odd)

        def joined(pair):
            zero, one = (piece + pltpu.roll(piece, HEAD_DIM, 1) for piece in pair)
            return jnp.where(low, zero, one)

        b.FQ[here, dm.heads : dm.heads + dm.kv] = joined(d_k)
        d_values.append(joined(d_v))
    d_turned = b.FQ[...]
    cosine = jnp.concatenate([b.tabs[0]] * reps, axis=1)
    sine = jnp.concatenate([b.tabs[1]] * reps, axis=1)
    first, ahead, behind = half_turn(d_turned * sine)
    d_lin = (d_turned * cosine + jnp.where(first, ahead, -behind)).astype(BF16)
    d_lin = jnp.concatenate([d_lin, jnp.concatenate(d_values, axis=0).astype(BF16)], axis=1)
    BIG[:, : dm.qkv] = mm_tn(b.npad[...], d_lin).astype(BF16)
    d_bias = jnp.sum(d_lin.astype(F32), axis=0, keepdims=True)
    d_normed = split_mm(mm_nt(d_lin, W[:, : dm.qkv]), b.spr[...], nt=True)
    xf = b.x[...].astype(F32)
    scale1 = lax.rsqrt(jnp.mean(xf * xf, axis=-1, keepdims=True) + 1e-06)
    d_gain1, d_part = norm_back(d_normed, xf, scale1, b.vec[0:1])
    b.gin[...] = (b.dhid[...] + d_part).astype(BF16)

    rows8 = iota((8, dm.d), 0)
    packed = jnp.zeros((8, dm.d), F32)
    for i, piece in enumerate((d_gain1, d_bias[:, : dm.heads], d_gain2)):
        packed = jnp.where(rows8 == i, piece, packed)
    packed = split_mm(packed, b.spr[...])
    mine = own_block(dm)
    spare = jnp.zeros((n, LANES), F32)
    for i in range(3):
        piece = jnp.where(mine, packed[i : i + 1], 0.0).astype(BF16)
        spare = spare + mm_nt(piece, field_matrix(dm, i * FIELD))
    piece = jnp.where(value_block(dm), d_bias[:, dm.heads + dm.kv :], 0.0).astype(BF16)
    spare = spare + mm_nt(piece, value_field(dm))
    key_bias = jnp.broadcast_to(d_bias[:, dm.heads : dm.heads + dm.kv], (n, LANES))
    spare = jnp.concatenate([spare, key_bias], axis=1).astype(BF16)
    BIG[:, : 2 * LANES] = (
        BIG[:, : 2 * LANES].astype(F32) + mm_tn(spare_rows(dm), spare)
    ).astype(BF16)

    cols = pl.ds(0, dm.wide)

    def quad(plane):
        return pl.ds(plane * CHIPS, CHIPS)

    for to in (*far, r):
        send(b.BIG.at[quad(to), other, :, cols], b.aR1.at[quad(to)], b.rA1.at[to], (partner,))
    for to in (*far, r):
        arrived(b.aR1.at[quad(to)], b.rA1.at[to])
        mine_now = b.BIG[quad(to), c, :, cols].astype(F32) + b.aR1[quad(to)].astype(F32)
        b.aR1[quad(to)] = mine_now.astype(BF16)
        for slot in range(2):
            source, place = routes[slot]
            send(b.aR1.at[to * CHIPS + source], b.aR2.at[slot, to], b.rA2.at[slot, to], dev(r, place * 2 + c))
    for k in range(1, planes - 1):
        chain_step(gate_part(0), b.zR0, b.rZ0, k)
    for to in (*far, r):
        arrived(b.aR2.at[0, to], b.rA2.at[0, to])
        piece = b.aR1.at[to * CHIPS + next_to]
        piece[...] = (piece[...].astype(F32) + b.aR2[0, to].astype(F32)).astype(BF16)
        send(piece, b.aR2.at[2, to], b.rA2.at[2, to], dev(r, next_to * 2 + c))
    total = b.hid[...] + b.oP[q, c].astype(F32)
    for slot in (1, 2):
        arrived(b.oR2.at[slot], b.rO2.at[slot])
        total = total + b.oR2[slot].astype(F32)
    b.out[...] = total.astype(BF16)
    for k in range(planes - 1):
        chain_step(down_part, b.zD, b.rW, k)
    for k in range(planes - 2):
        chain_step(gate_part(1), b.zR1, b.rZ1, k)
    for to in (*far, r):
        total = b.aR1[to * CHIPS + q].astype(F32)
        for slot in (1, 2):
            arrived(b.aR2.at[slot, to], b.rA2.at[slot, to])
            total = total + b.aR2[slot, to].astype(F32)
        b.aR2[0, to] = total.astype(BF16)
    chain_start(attn_part, b.aR3, b.rA3)
    squeeze = b.spr[: dm.unit, : PLANE * rp]

    def home(h, landing, arrive, final):
        start, width = dm.parts[h]
        cols = pl.ds(start, width)
        chain_end(gate_part(h)(r), landing, arrive)
        for i in range(2):
            piece = mm_tn(squeeze, GU[h][my_rows, i * width : (i + 1) * width]).astype(BF16)
            piece = piece.reshape(PLANE, rp, width)
            for place in range(PLANE):
                b.act[2 * place + i, :, cols] = piece[place]
        for k in range(1, PLANE):
            to = (p + k) % PLANE
            send(b.act.at[pl.ds(2 * to, 2), :, cols], b.fgu.at[p, :, :, cols], final.at[p], dev(r, to))
        b.fgu[p, :, :, cols] = b.act[pl.ds(2 * p, 2), :, cols]

    home(0, b.zR0, b.rZ0, b.rF0)
    chain_step(gate_part(1), b.zR1, b.rZ1, planes - 2)
    home(1, b.zR1, b.rZ1, b.rF1)
    for k in range(planes - 1):
        chain_step(attn_part, b.aR3, b.rA3, k)
    sums = b.hid.at[: dm.rfp]
    sums[...] = b.WD[r].astype(F32)
    chain_end(sums, b.zD, b.rW)

    def lay_flat(flat, field):
        blocks = field.shape[1] // LANES
        for j in range(blocks):
            flat[pl.ds(j, field.shape[0], stride=blocks), :] = field[:, j * LANES : (j + 1) * LANES]

    lay_flat(b.fd, sums[: dm.rf])
    b.fa[...] = b.aR2[0, r].astype(F32)
    chain_end(b.fa, b.aR3, b.rA3)
    own_rows = b.fa[: dm.rows]
    h, kv = dm.heads, dm.kv
    lay_flat(b.fq, own_rows[:, :h])
    b.fk[...] = own_rows[:, h : h + kv]
    b.fv[...] = own_rows[:, h + kv : h + 2 * kv]
    lay_flat(b.fo, own_rows[:, h + 2 * kv :])
    b.fs[...] = b.fa[dm.rows : dm.rows + 1, : 2 * LANES]
    for k in range(1, PLANE):
        origin = (p + PLANE - k) % PLANE
        for (start, width), final in zip(dm.parts, (b.rF0, b.rF1)):
            arrived(b.fgu.at[origin, :, :, pl.ds(start, width)], final.at[origin])
    for where in range(CHIPS):
        first_copy(where, b.oP, b.oR1, b.osem, b.rO1).wait_send()
        first_copy(where, b.dP, b.dR1, b.dsem, b.rD1).wait_send()
    for slot in range(CHIPS - 1):
        second_copy(slot, *o_route).wait_send()
        second_copy(slot, *d_route).wait_send()
    drain()


def run_layer(dm, operands):
    n, planes, rp, tok = dm.n, dm.planes, dm.rp, dm.tok
    vm = pltpu.VMEM
    sem = pltpu.SemaphoreType.DMA
    quads = planes * CHIPS
    pairs = dm.heads + dm.kv
    outs = {
        "out": jax.ShapeDtypeStruct((tok, dm.d), BF16),
        "gin": jax.ShapeDtypeStruct((tok, dm.d), BF16),
        "fq": jax.ShapeDtypeStruct((dm.rows * dm.heads // LANES, LANES), F32),
        "fk": jax.ShapeDtypeStruct((dm.rows, LANES), F32),
        "fv": jax.ShapeDtypeStruct((dm.rows, LANES), F32),
        "fo": jax.ShapeDtypeStruct((dm.rows * dm.d // LANES, LANES), F32),
        "fs": jax.ShapeDtypeStruct((1, 2 * LANES), F32),
        "fgu": jax.ShapeDtypeStruct((PLANE, 2, rp, dm.ffr), BF16),
        "fd": jax.ShapeDtypeStruct((dm.rf * dm.d // LANES, LANES), F32),
    }
    n_sends = 1 + (planes - 1) * 16 + 16 * PLANE + 8 * quads + 64
    scratch = {
        "W": vm((quads, 2, rp, dm.wide), BF16),
        "GU0": vm((planes * dm.groups, dm.gs, 2 * dm.parts[0][1]), BF16),
        "GU1": vm((planes * dm.groups, dm.gs, 2 * dm.parts[1][1]), BF16),
        "WD": vm((planes, dm.rfp, dm.d), BF16),
        "nfA": vm((PLANE, tok, dm.d), BF16),
        "gA": vm((PLANE, tok, dm.d), BF16),
        "act": vm((PLANE * tok // rp, rp, dm.ffr), BF16),
        "BIG": vm((quads, 2, rp, 4 * dm.ffr), BF16),
        "oP": vm((CHIPS, 2, tok, dm.d), BF16),
        "dP": vm((CHIPS, 2, tok, dm.d), BF16),
        "oR1": vm((CHIPS, tok, dm.d), BF16),
        "dR1": vm((CHIPS, tok, dm.d), BF16),
        "oR2": vm((CHIPS - 1, tok, dm.d), BF16),
        "dR2": vm((CHIPS - 1, tok, dm.d), BF16),
        "zR0": vm((planes + 1, dm.groups, dm.gs, 2 * dm.parts[0][1]), BF16),
        "zR1": vm((planes + 1, dm.groups, dm.gs, 2 * dm.parts[1][1]), BF16),
        "zD": vm((planes + 1, dm.rfp, dm.d), BF16),
        "aR1": vm((quads, rp, dm.wide), BF16),
        "aR2": vm((CHIPS - 1, planes, rp, dm.wide), BF16),
        "aR3": vm((planes + 1, rp, dm.wide), BF16),
        "QS": vm((dm.micro, HEADS * dm.slots, LANES), BF16),
        "PF": vm((dm.micro, HEADS * dm.slots, dm.slots), F32),
        "hid": vm((tok, dm.d), F32),
        "fa": vm((rp, dm.wide), F32),
        "dhid": vm((tok, dm.d), F32),
        "npad": vm((tok, dm.dp), BF16),
        "mpad": vm((tok, dm.dp), BF16),
        "spr": vm((dm.d, dm.dp), BF16),
        "kd": vm((KV_HEADS, tok, LANES), BF16),
        "vd": vm((KV_HEADS, tok, LANES), BF16),
        "FQ": vm((tok, pairs), F32),
        "tabs": vm((2, tok, LANES), F32),
        "vec": vm((8, dm.d), F32),
        "ssem": sem((n_sends,)),
        "csem": sem((4,)),
        "osem": sem((CHIPS,)),
        "dsem": sem((CHIPS,)),
        "osem2": sem((CHIPS - 1,)),
        "dsem2": sem((CHIPS - 1,)),
        "rA": sem((n,)),
        "rGU": sem((PLANE,)),
        "rGZ0": sem((planes,)),
        "rGZ1": sem((planes,)),
        "rG": sem((PLANE,)),
        "rWD": sem((planes,)),
        "rNF": sem((PLANE,)),
        "rO1": sem((CHIPS,)),
        "rD1": sem((CHIPS,)),
        "rO2": sem((CHIPS - 1,)),
        "rD2": sem((CHIPS - 1,)),
        "rZ0": sem((planes + 1,)),
        "rZ1": sem((planes + 1,)),
        "rF0": sem((PLANE,)),
        "rF1": sem((PLANE,)),
        "rW": sem((planes + 1,)),
        "rA1": sem((planes,)),
        "rA2": sem((CHIPS - 1, planes)),
        "rA3": sem((planes + 1,)),
    }
    return pl.pallas_call(
        functools.partial(layer_kernel, dm, (*operands, *outs, *scratch)),
        name="layer",
        out_shape=list(outs.values()),
        in_specs=[pl.BlockSpec(memory_space=pltpu.VMEM)] * len(operands),
        out_specs=[pl.BlockSpec(memory_space=pltpu.VMEM)] * len(outs),
        scratch_shapes=list(scratch.values()),
        compiler_params=pltpu.CompilerParams(
            collective_id=0, has_side_effects=True, vmem_limit_bytes=67043328
        ),
    )(*operands.values())


def per_device(n, *args):
    (
        tokens,
        positions,
        cotangent,
        norm_attn,
        w_query,
        b_query,
        w_key,
        b_key,
        w_value,
        b_value,
        w_out,
        norm_ffn,
        w_gate,
        w_up,
        w_down,
    ) = args
    micro, slots, d = tokens.shape
    dm = Dims(n, d, w_gate.shape[0] * n // d, slots, micro)
    rows, rp = dm.rows, dm.rp

    def lanes(vector):
        return jnp.pad(vector, (0, FIELD - vector.shape[0]))

    spare = jnp.concatenate([lanes(v) for v in (norm_attn, b_query, norm_ffn, b_value)])
    spare = jnp.pad(spare, (0, dm.wide - spare.shape[0]))
    pack = jnp.concatenate(
        [w.reshape(rows, -1) for w in (w_query, w_key, w_value, w_out)], axis=1
    )
    pack = jnp.concatenate([pack, spare[None]], axis=0)
    pack = jnp.pad(pack, ((0, rp - rows - 1), (0, 0)))

    def columns(weight):
        weight = weight.reshape(rows, dm.planes, PLANE, dm.rf)
        weight = jnp.pad(weight, ((0, rp - rows), (0, 0), (0, 0), (0, dm.rfp - dm.rf)))
        return weight.transpose(2, 0, 1, 3).reshape(PLANE, rp, dm.ffr)

    both = jnp.stack([columns(w_gate), columns(w_up)], axis=1)
    down = jnp.pad(w_down.reshape(dm.rf, d), ((0, dm.rfp - dm.rf), (0, 0)))
    operands = {
        "x": tokens.reshape(dm.tok, d),
        "g": cotangent.reshape(dm.tok, d),
        "posr": positions,
        "bkey": b_key[None],
        "ap": pack,
        "gus": both,
        "wds": down,
    }
    out, gin, fq, fk, fv, fo, fs, fgu, fd = run_layer(dm, operands)

    def field(i, size):
        return fs[0, i * FIELD : i * FIELD + size]

    def gate_part(i):
        part = fgu[:, i, :rows].astype(F32)
        part = part.reshape(PLANE, rows, dm.planes, dm.rfp)[..., : dm.rf]
        return part.transpose(1, 2, 0, 3).reshape(-1)

    return (
        out.reshape(micro, slots, d),
        gin.reshape(micro, slots, d),
        field(0, rows),
        fq.reshape(-1),
        field(1, rows),
        fk.reshape(-1),
        fs[0, LANES : LANES + dm.kv],
        fv.reshape(-1),
        field(3, dm.rv),
        fo.reshape(-1),
        field(2, rows),
        gate_part(0),
        gate_part(1),
        fd.reshape(-1),
    )


def solution(mesh):
    n = mesh.shape["dp"]
    split, row = P("dp"), P(None, "dp", None)
    in_specs = (row, P(None, "dp"), row, *[split] * 4, P(), *[split] * 7)
    out_specs = (row, row, *[split] * 4, P(), *[split] * 7)
    return jax.shard_map(
        functools.partial(per_device, n),
        mesh=mesh,
        in_specs=in_specs,
        out_specs=out_specs,
        check_vma=False,
    )
```

```python
import functools
import math

import jax
import jax.numpy as jnp
from jax import lax
from jax.experimental import pallas as pl
from jax.experimental.pallas import tpu as pltpu
from jax.sharding import PartitionSpec as P

HEADS = 14
KV_HEADS = 2
HEAD_DIM = 64
GROUP = HEADS // KV_HEADS
PLANE = 8
CHIPS = 4
LANES = 128
ROTARY_LOG = math.log(1000000.0)
FIELD = 32
MESH = pl.DeviceIdType.MESH
F32 = jnp.float32
BF16 = jnp.bfloat16


def up(value, step):
    return -(-value // step) * step


def mm(left, right, dims=((1,), (0,))):
    return lax.dot_general(left, right, (dims, ((), ())), preferred_element_type=F32)


def mm_nt(left, right):
    return mm(left, right, ((1,), (1,)))


def mm_tn(left, right):
    return mm(left, right, ((0,), (0,)))


def split_mm(left, right, nt=False):
    high = left.astype(BF16)
    low = (left - high.astype(F32)).astype(BF16)
    dot = mm_nt if nt else mm
    return dot(high, right) + dot(low, right)


def iota(shape, dim):
    return lax.broadcasted_iota(jnp.int32, shape, dim)


class Dims:
    def __init__(self, n, d, ff, slots, micro):
        self.n, self.d, self.ff = n, d, ff
        self.planes = n // PLANE
        self.rows = d // n
        self.rp = 8
        while self.rp < self.rows + 1:
            self.rp *= 2
        self.dp = n * self.rp
        self.rf = ff // n
        self.ffr = up(ff // PLANE, LANES)
        self.rfp = self.ffr // self.planes
        self.slots, self.micro = slots, micro
        self.tok = slots * micro
        self.heads = HEADS * HEAD_DIM
        self.kv = KV_HEADS * HEAD_DIM
        self.qkv = self.heads + 2 * self.kv
        self.wide = self.qkv + d
        self.rv = self.kv // n
        self.unit = PLANE * self.rows
        self.gs = 16 if self.unit % 16 == 0 else 8
        self.groups = self.unit // self.gs
        blocks = self.ffr // LANES
        first = blocks // 2 * LANES
        self.parts = ((0, first), (first, self.ffr - first))


def spread_matrix(dm):
    shape = (dm.d, dm.dp)
    row, col = iota(shape, 0), iota(shape, 1)
    inner = col & (dm.rp - 1)
    hit = (row == (col // dm.rp) * dm.rows + inner) & (inner < dm.rows)
    return jnp.where(hit, 1.0, 0.0).astype(BF16)


def field_matrix(dm, offset):
    shape = (LANES, dm.dp)
    row, col = iota(shape, 0), iota(shape, 1)
    inner = col & (dm.rp - 1)
    return jnp.where((row == offset + inner) & (inner < dm.rows), 1.0, 0.0).astype(BF16)


def own_block(dm):
    shape = (dm.n, dm.dp)
    return iota(shape, 1) // dm.rp == iota(shape, 0)


def spare_rows(dm):
    shape = (dm.n, dm.dp)
    return jnp.where(iota(shape, 1) == iota(shape, 0) * dm.rp + dm.rows, 1.0, 0.0).astype(BF16)


def value_field(dm):
    shape = (LANES, LANES)
    return jnp.where(
        iota(shape, 0) == 3 * FIELD + (iota(shape, 1) & (dm.rv - 1)), 1.0, 0.0
    ).astype(BF16)


def value_block(dm):
    shape = (dm.n, LANES)
    return iota(shape, 1) // dm.rv == iota(shape, 0)


def half_turn(field):
    width = field.shape[-1]
    first = (iota(field.shape, 1) & (HEAD_DIM - 1)) < HEAD_DIM // 2
    ahead = pltpu.roll(field, width - HEAD_DIM // 2, 1)
    behind = pltpu.roll(field, HEAD_DIM // 2, 1)
    return first, ahead, behind


def twice(field):
    low = iota(field.shape, 1) < HEAD_DIM
    turned = pltpu.roll(field, HEAD_DIM, 1)
    return jnp.where(low, field, turned), jnp.where(low, turned, field)


class Refs:
    def __init__(self, names, refs):
        self.__dict__.update(zip(names, refs, strict=True))


def layer_kernel(dm, names, *refs):
    b = Refs(names, refs)
    n, planes, rp = dm.n, dm.planes, dm.rp
    me = lax.axis_index("dp")
    r, p = me // PLANE, me % PLANE
    q, c = p // 2, p % 2
    other = 1 - c
    partner = r * PLANE + q * 2 + other

    def dev(plane, place):
        return (plane * PLANE + place,)

    barrier = pltpu.get_barrier_semaphore()
    peers = [dev(r, (p + k) % PLANE) for k in range(1, PLANE)]
    peers += [dev((r + k) % planes, p) for k in range(1, planes)]
    for peer in peers:
        pl.semaphore_signal(barrier, inc=1, device_id=peer, device_id_type=MESH)
    pl.semaphore_wait(barrier, len(peers))

    pending = []
    count = [0]

    def prepare(src, dst, arrive, to, cond=None, tag=None):
        copy = pltpu.make_async_remote_copy(
            src_ref=src,
            dst_ref=dst,
            send_sem=b.ssem.at[count[0]],
            recv_sem=arrive,
            device_id=to,
            device_id_type=MESH,
        )
        count[0] += 1
        pending.append((copy, cond, tag))
        return copy

    def send(src, dst, arrive, to, cond=None, tag=None):
        copy = prepare(src, dst, arrive, to, cond, tag)
        if cond is None:
            copy.start()
        else:
            pl.when(cond)(copy.start)

    def drain(tag=None):
        now = [item for item in pending if tag in (None, item[2])]
        for copy, cond, _ in now:
            if cond is None:
                copy.wait_send()
            else:
                pl.when(cond)(copy.wait_send)
        pending[:] = [item for item in pending if tag not in (None, item[2])]

    upper = r // max(planes // 2, 1)
    mirror = r + upper * (planes - 1 - 2 * r)

    def origin_of(k):
        spot = k - (mirror + planes - k) // planes
        return spot + upper * (planes - 1 - 2 * spot)

    def relay_own(src, dst, arrive, tag=None):
        send(src, dst, arrive, dev(r + 1, p), r + 1 < planes, tag)
        send(src, dst, arrive, dev(r - 1, p), r >= 1, tag)

    def onward(part, sems, k, tag=None):
        origin = origin_of(k)
        to = r - 1 + 2 * ((r - origin - 1 + planes) // planes)
        cond = (to >= 0) & (to < planes)
        piece, arrive = part(origin), sems.at[origin]
        return piece, arrive, cond, prepare(piece, piece, arrive, dev(to, p), cond, tag)

    def pass_on(piece, arrive, cond, copy):
        @pl.when(cond)
        def _():
            arrived(piece, arrive)
            copy.start()

    def settle(piece, arrive, cond, copy):
        pl.when(jnp.logical_not(cond))(lambda: arrived(piece, arrive))

    def arrived(dst, arrive):
        pltpu.make_async_remote_copy(
            src_ref=dst,
            dst_ref=dst,
            send_sem=b.ssem.at[0],
            recv_sem=arrive,
            device_id=(partner,),
            device_id_type=MESH,
        ).wait_recv()

    def block(ref, index):
        return ref.at[index // 2, index % 2]

    def plane_rows(ref, plane):
        return ref.at[pl.ds(plane * dm.groups, dm.groups)]

    keep = [
        pltpu.make_async_copy(b.ap, block(b.W, me), b.csem.at[0]),
        pltpu.make_async_copy(b.gus.at[p], b.fgu.at[p], b.csem.at[1]),
        pltpu.make_async_copy(b.g, b.gA.at[p], b.csem.at[2]),
        pltpu.make_async_copy(b.wds, b.WD.at[r], b.csem.at[3]),
    ]
    for copy in keep:
        copy.start()

    relay_own(b.ap, block(b.W, me), b.rA.at[me])

    across, along = q + 1 - 2 * (q % 2), (q + 2) % CHIPS
    near = across * other + along * c
    next_to = along * other + across * c
    spots = (near, next_to, CHIPS - 1 - q)

    def fan(index, src):
        for where in (next_to, near):
            send(src, block(b.W, index), b.rA.at[index], dev(r, where * 2 + c))

    def spread_out(src, ref, arrive):
        for where in (next_to, near):
            send(src, ref.at[p], arrive.at[p], dev(r, where * 2 + c))
        send(src, ref.at[p], arrive.at[p], (partner,))

    def hand_on(ref, arrive, where):
        place = where * 2 + c
        arrived(ref.at[place], arrive.at[place])
        if where is near:
            send(ref.at[place], ref.at[place], arrive.at[place], dev(r, next_to * 2 + c))
        send(ref.at[place], ref.at[place], arrive.at[place], (partner,))

    fan(me, b.ap)
    send(b.ap, block(b.W, me), b.rA.at[me], (partner,))
    for k in range(1, PLANE):
        send(b.gus.at[(p + k) % PLANE], b.fgu.at[p], b.rGU.at[p], dev(r, (p + k) % PLANE))
    relay_own(b.wds, b.WD.at[r], b.rWD.at[r])

    tok = dm.tok
    xf = b.x[...].astype(F32)
    scale1 = lax.rsqrt(jnp.mean(xf * xf, axis=-1, keepdims=True) + 1e-06)
    diagonal = iota((dm.slots, dm.slots), 0) == iota((dm.slots, dm.slots), 1)
    posc = [
        jnp.sum(jnp.where(diagonal, b.posr[m : m + 1].astype(F32), 0.0), axis=1, keepdims=True)
        for m in range(dm.micro)
    ]
    power = (iota((1, LANES), 1) & (HEAD_DIM // 2 - 1)).astype(F32) * (-2.0 / HEAD_DIM * ROTARY_LOG)
    angle = jnp.concatenate(posc, axis=0) * jnp.exp(power)
    b.tabs[0] = jnp.cos(angle)
    b.tabs[1] = jnp.sin(angle)
    b.spr[...] = spread_matrix(dm)

    for k in range(1, planes):
        origin = origin_of(k)
        index = origin * PLANE + p
        arrived(block(b.W, index), b.rA.at[index])
        to = r - 1 + 2 * ((r - origin - 1 + planes) // planes)
        send(block(b.W, index), block(b.W, index), b.rA.at[index], dev(to, p), (to >= 0) & (to < planes))
        fan(index, block(b.W, index))
        send(block(b.W, index), block(b.W, index), b.rA.at[index], (partner,))
    for k in range(1, PLANE):
        origin = (p + PLANE - k) % PLANE
        arrived(b.fgu.at[origin], b.rGU.at[origin])
    keep[1].wait()
    GU = [ref.reshape(dm.d, ref.shape[-1]) for ref in (b.GU0, b.GU1)]
    my_rows = pl.ds(pl.multiple_of(r * dm.unit, dm.gs), dm.unit)
    squeeze = b.spr[: dm.unit, : PLANE * rp]
    for h, (start, width) in enumerate(dm.parts):
        for i in range(2):
            piece = b.fgu[:, i, :, start : start + width].reshape(PLANE * rp, width)
            GU[h][my_rows, i * width : (i + 1) * width] = mm(squeeze, piece).astype(BF16)

    def gate_part(h):
        ref = (b.GU0, b.GU1)[h]
        return lambda plane: plane_rows(ref, plane)

    def down_part(plane):
        return b.WD.at[plane]

    relay_own(gate_part(0)(r), gate_part(0)(r), b.rGZ0.at[r], "gate0")
    steps = range(1, planes)
    down_on = [onward(down_part, b.rWD, k, "down") for k in steps]
    gate_on = [[onward(gate_part(h), sems, k, f"gate{h}") for k in steps] for h, sems in ((0, b.rGZ0), (1, b.rGZ1))]
    pass_on(*down_on[0])
    origins = [r, *(origin_of(k) for k in steps)]
    for i, where in enumerate(spots):
        for origin in origins:
            index = origin * PLANE + where * 2 + c
            arrived(block(b.W, index), b.rA.at[index])
            if i == 0:
                send(block(b.W, index), block(b.W, index), b.rA.at[index], dev(r, next_to * 2 + c))
            send(block(b.W, index), block(b.W, index), b.rA.at[index], (partner,))
    spread_out(b.g, b.gA, b.rG)
    for item in down_on[1:]:
        pass_on(*item)

    keep[0].wait()
    for k in range(CHIPS):
        for shift in range(planes):
            index = ((r + planes - shift) % planes) * PLANE + ((q + CHIPS - k) % CHIPS) * 2 + other
            arrived(block(b.W, index), b.rA.at[index])

    W = b.W.reshape(dm.dp, dm.wide)
    small = mm(spare_rows(dm), W[:, :LANES]).astype(BF16)
    mine = own_block(dm)
    rows8 = iota((8, dm.dp), 0)
    padded = jnp.zeros((8, dm.dp), F32)
    for i in range(3):
        piece = mm(small, field_matrix(dm, i * FIELD))
        piece = jnp.sum(jnp.where(mine, piece, 0.0), axis=0, keepdims=True)
        padded = jnp.where(rows8 == i, piece, padded)
    b.vec[...] = mm_nt(padded.astype(BF16), b.spr[...])
    gain1, bias_q, gain2 = b.vec[0:1], b.vec[1:2], b.vec[2:3]
    bias_v = jnp.sum(
        jnp.where(value_block(dm), mm(small, value_field(dm)), 0.0), axis=0, keepdims=True
    )
    bias_k = b.bkey[...].astype(F32)

    normed = (xf * scale1 * gain1).astype(BF16)
    b.npad[...] = mm(normed, b.spr[...]).astype(BF16)
    lin = mm(b.npad[...], W[:, : dm.qkv])
    turn_in = jnp.concatenate([lin[:, : dm.heads] + bias_q, lin[:, dm.heads : dm.heads + dm.kv] + bias_k], axis=1)
    reps = (dm.heads + dm.kv) // LANES
    cosine = jnp.concatenate([b.tabs[0]] * reps, axis=1)
    sine = jnp.concatenate([b.tabs[1]] * reps, axis=1)
    first, ahead, behind = half_turn(turn_in)
    turned = turn_in * cosine + jnp.where(first, -ahead, behind) * sine
    values = lin[:, dm.heads + dm.kv :] + bias_v
    for i, piece in enumerate(twice(turned[:, dm.heads :])):
        b.kd[i] = piece.astype(BF16)
    for i, piece in enumerate(twice(values)):
        b.vd[i] = piece.astype(BF16)
    low = iota((dm.slots, LANES), 1) < HEAD_DIM

    def stack_heads(field, store):
        for h in range(HEADS):
            part = field[:, LANES * (h // 2) : LANES * (h // 2) + LANES]
            part = jnp.where(low if h % 2 == 0 else ~low, part, 0.0)
            store(h)[...] = part.astype(BF16)

    span = GROUP * dm.slots
    mix = b.oP.at[0, 0]
    BIG = b.BIG.reshape(dm.dp, 4 * dm.ffr)
    dms = [BIG.at[:span, dm.wide + kv * LANES : dm.wide + (kv + 1) * LANES] for kv in range(KV_HEADS)]

    def head_rows(h):
        return dms[h // GROUP].at[(h % GROUP) * dm.slots : (h % GROUP + 1) * dm.slots]

    for m in range(dm.micro):
        here = slice(m * dm.slots, (m + 1) * dm.slots)
        stack_heads(turned[here, : dm.heads], lambda h: b.QS.at[m, h * dm.slots : (h + 1) * dm.slots])
        grid = (dm.slots, dm.slots)
        start_row = iota((dm.slots, 1), 0).astype(F32) - posc[m]
        start_col = (iota((1, dm.slots), 1) - b.posr[m : m + 1]).astype(F32)
        allowed = (start_row == start_col) & (iota(grid, 1) <= iota(grid, 0))
        for kv in range(KV_HEADS):
            rows = slice(kv * span, (kv + 1) * span)
            score = mm_nt(b.QS[m, rows], b.kd[kv, here]) * 0.125
            score = jnp.where(allowed[None], score.reshape(GROUP, *grid), -1e30)
            top = jnp.max(score, axis=-1, keepdims=True)
            expo = jnp.exp(score - top)
            prob = expo / jnp.sum(expo, axis=-1, keepdims=True)
            prob = prob.reshape(span, dm.slots)
            b.PF[m, rows] = prob
            dms[kv][...] = mm(prob.astype(BF16), b.vd[kv, here]).astype(BF16)
        for t in range(HEADS // 2):
            even, odd = head_rows(2 * t)[...], head_rows(2 * t + 1)[...]
            mix[here, t * LANES : (t + 1) * LANES] = jnp.where(low, even, odd)
    b.mpad[...] = mm(mix[...], b.spr[...]).astype(BF16)
    hidden = xf + mm(b.mpad[...], W[:, dm.qkv :])
    b.hid[...] = hidden
    scale2 = lax.rsqrt(jnp.mean(hidden * hidden, axis=-1, keepdims=True) + 1e-06)
    nf = (hidden * scale2 * gain2).astype(BF16)
    b.nfA[p] = nf

    spread_out(b.nfA.at[p], b.nfA, b.rNF)
    pass_on(*gate_on[0][0])
    hand_on(b.gA, b.rG, near)
    for item in gate_on[0][1:]:
        pass_on(*item)
    relay_own(gate_part(1)(r), gate_part(1)(r), b.rGZ1.at[r], "gate1")
    hand_on(b.nfA, b.rNF, near)
    for where in spots[1:]:
        hand_on(b.gA, b.rG, where)
    for where in spots[1:]:
        hand_on(b.nfA, b.rNF, where)
    for item in (*down_on, *gate_on[0]):
        settle(*item)
    pass_on(*gate_on[1][0])
    keep[2].wait()
    keep[3].wait()
    for k in range(CHIPS):
        place = ((q + CHIPS - k) % CHIPS) * 2 + other
        arrived(b.gA.at[place], b.rG.at[place])
        arrived(b.nfA.at[place], b.rNF.at[place])

    ACT = b.act.reshape(PLANE * tok, dm.ffr)
    WD = b.WD.reshape(dm.ffr, dm.d)
    half = PLANE // 2

    base = (0, 4 * dm.parts[0][1])

    def feed(h, place_q, place_c):
        place = place_q * 2 + place_c
        start, width = dm.parts[h]
        nf_t, g_t = b.nfA[place], b.gA[place]
        down = WD[start : start + width]
        pre = mm(nf_t, GU[h][...])
        gate, upper = pre[:, :width], pre[:, width:]
        sigma = jax.nn.sigmoid(gate)
        silu = gate * sigma
        act = (silu * upper).astype(BF16)
        ACT[pl.ds(pl.multiple_of(place * tok, tok), tok), start : start + width] = act
        d_act = mm_nt(g_t, down)
        d_gate = (d_act * upper * (sigma + silu * (1.0 - sigma))).astype(BF16)
        d_up = (d_act * silu).astype(BF16)
        d_both = jnp.concatenate([d_gate, d_up], axis=1)
        rows = pl.ds(pl.multiple_of((place % half) * tok, tok), tok)
        cols = pl.ds(pl.multiple_of(base[h] + (place // half) * 2 * width, LANES), 2 * width)
        BIG[rows, cols] = d_both
        for ref, value in ((b.oP, mm(act, down)), (b.dP, mm_nt(d_both, GU[h][...]))):
            if h:
                value = value + ref[place_q, place_c].astype(F32)
            ref[place_q, place_c] = value.astype(BF16)

    def first_copy(where, part, landing, sems, arrive):
        return pltpu.make_async_remote_copy(
            src_ref=part.at[where, other],
            dst_ref=landing.at[where],
            send_sem=sems.at[where],
            recv_sem=arrive.at[where],
            device_id=(partner,),
            device_id_type=MESH,
        )

    diag = CHIPS - 1 - q
    routes = ((diag, near), (near, near), (next_to, next_to))

    def second_copy(slot, part, landing, sems, arrive):
        source, to = routes[slot]
        return pltpu.make_async_remote_copy(
            src_ref=part.at[source, c],
            dst_ref=landing.at[slot],
            send_sem=sems.at[slot],
            recv_sem=arrive.at[slot],
            device_id=dev(r, to * 2 + c),
            device_id_type=MESH,
        )

    def add_on(part, landing, sems, arrive):
        arrived(landing.at[0], arrive.at[0])
        part[next_to, c] = (part[next_to, c].astype(F32) + landing[0].astype(F32)).astype(BF16)
        second_copy(2, part, landing, sems, arrive).start()

    d_route = (b.dP, b.dR2, b.dsem2, b.rD2)
    o_route = (b.oP, b.oR2, b.osem2, b.rO2)

    def hop(part, landing, arrive, to, cond):
        ahead = (to - r - 1 + planes) // planes
        beyond = r - to - 1 + 2 * planes * ahead
        last = 1 - (beyond + 4 * planes - 1) // (4 * planes)
        slot = to + (planes - to) * last
        send(part(to), landing.at[slot], arrive.at[slot], dev(r - 1 + 2 * ahead, p), cond)

    def behind_of(to):
        ahead = (to - r - 1 + planes) // planes
        follows = r + 1 - 2 * ahead
        return (follows >= 0) & (follows < planes)

    far = [origin_of(planes - k) for k in range(1, planes)]

    def chain_start(part, landing, arrive):
        for to in far:
            hop(part, landing, arrive, to, jnp.logical_not(behind_of(to)))

    def chain_step(part, landing, arrive, k):
        to = far[k]
        has = behind_of(to)

        @pl.when(has)
        def _():
            arrived(landing.at[to], arrive.at[to])
            mine = part(to)
            mine[...] = (mine[...].astype(F32) + landing[to].astype(F32)).astype(BF16)

        hop(part, landing, arrive, to, has)

    def chain_end(total, landing, arrive):
        for slot, cond in ((r, r >= 1), (planes, r + 1 < planes)):

            @pl.when(cond)
            def _():
                arrived(landing.at[slot], arrive.at[slot])
                total[...] = (total[...].astype(F32) + landing[slot].astype(F32)).astype(total.dtype)

    nf_all = b.nfA.reshape(PLANE * tok, dm.d)
    g_all = b.gA.reshape(PLANE * tok, dm.d)
    wide_rows = half * tok
    chunk = 2 * LANES

    def gate_grad(h):
        width = dm.parts[h][1]

        def some(start, count):
            cols = pl.ds(start, count)
            total = mm_tn(nf_all[:wide_rows, cols], BIG[:, base[h] : base[h] + 2 * width])
            total = total + mm_tn(nf_all[wide_rows:, cols], BIG[:, base[h] + 2 * width : base[h] + 4 * width])
            GU[h][cols, :] = total.astype(BF16)

        @pl.loop(0, dm.d // chunk)
        def _(i):
            some(pl.multiple_of(i * chunk, chunk), chunk)

        if dm.d % chunk:
            some(dm.d - dm.d % chunk, dm.d % chunk)

    @pl.loop(0, PLANE)
    def _(turn):
        feed(0, turn // 2, turn % 2)

        @pl.when(turn == half - 1)
        def _():
            for item in gate_on[1][1:]:
                pass_on(*item)

    drain("gate0")
    gate_grad(0)
    chain_start(gate_part(0), b.zR0, b.rZ0)
    for item in gate_on[1]:
        settle(*item)

    def join(where):
        for part, one, arrive in ((b.dP, b.dR1, b.rD1), (b.oP, b.oR1, b.rO1)):
            arrived(one.at[where], arrive.at[where])
            part[where, c] = (part[where, c].astype(F32) + one[where].astype(F32)).astype(BF16)

    @pl.loop(0, CHIPS)
    def _(step):
        one, two = (CHIPS - 1 - step) % 2, (CHIPS - 1 - step) // 2
        over_x, over_y = one * other + two * c, two * other + one * c
        where = 2 * ((q // 2 + over_y) % 2) + (q % 2 + over_x) % 2

        @pl.loop(0, 2)
        def _(turn):
            feed(1, where, (other + turn) % 2)

            @pl.when(turn == 0)
            def _():
                first_copy(where, b.dP, b.dR1, b.dsem, b.rD1).start()
                first_copy(where, b.oP, b.oR1, b.osem, b.rO1).start()

        for at, source in ((1, diag), (2, near)):

            @pl.when(step == at)
            def _():
                join(source)
                second_copy(at - 1, *d_route).start()

    join(next_to)
    add_on(*d_route)
    for slot in range(2):
        second_copy(slot, *o_route).start()
    join(q)

    def attn_part(plane):
        return b.aR2.at[0, plane]

    drain("down")
    WD[...] = mm_tn(ACT[...], g_all[...]).astype(BF16)
    chain_start(down_part, b.zD, b.rW)
    drain("gate1")
    gate_grad(1)
    chain_start(gate_part(1), b.zR1, b.rZ1)
    for k in range(planes - 1):
        chain_step(gate_part(0), b.zR0, b.rZ0, k)
    add_on(*o_route)
    d_nf = b.dP[q, c].astype(F32)
    for slot in (1, 2):
        arrived(b.dR2.at[slot], b.rD2.at[slot])
        d_nf = d_nf + b.dR2[slot].astype(F32)
    hidden = b.hid[...]
    scale2 = lax.rsqrt(jnp.mean(hidden * hidden, axis=-1, keepdims=True) + 1e-06)

    def norm_back(grad, field, scale, gain):
        weighted = grad * gain
        d_gain = jnp.sum(grad * field * scale, axis=0, keepdims=True)
        d_field = weighted * scale - field * (scale * scale * scale) * jnp.mean(
            weighted * field, axis=-1, keepdims=True
        )
        return d_gain, d_field

    d_gain2, d_part = norm_back(d_nf, hidden, scale2, b.vec[2:3])
    d_hidden = b.g[...].astype(F32) + d_part
    b.dhid[...] = d_hidden
    d_attn = d_hidden.astype(BF16)
    chain_step(down_part, b.zD, b.rW, 0)
    BIG[:, dm.qkv : dm.wide] = mm_tn(b.mpad[...], d_attn).astype(BF16)
    d_mixed = mm_nt(d_attn, W[:, dm.qkv :]).astype(BF16)
    d_mixed = mm_nt(d_mixed, b.spr[...])
    d_values = []
    for m in range(dm.micro):
        here = slice(m * dm.slots, (m + 1) * dm.slots)
        stack_heads(d_mixed[here], head_rows)
        d_v, d_k = [], []
        for kv in range(KV_HEADS):
            rows = slice(kv * span, (kv + 1) * span)
            d_mix, prob, qs = dms[kv][...], b.PF[m, rows], b.QS[m, rows]
            d_v.append(mm_tn(prob.astype(BF16), d_mix))
            d_prob = mm_nt(d_mix, b.vd[kv, here])
            delta = jnp.sum(d_prob * prob, axis=-1, keepdims=True)
            d_score = (prob * (d_prob - delta)).astype(BF16)
            d_k.append(0.125 * mm_tn(d_score, qs))
            b.PF[m, rows] = 0.125 * mm(d_score, b.kd[kv, here])
        for t in range(HEADS // 2):
            even = b.PF[m, 2 * t * dm.slots : (2 * t + 1) * dm.slots]
            odd = b.PF[m, (2 * t + 1) * dm.slots : (2 * t + 2) * dm.slots]
            b.FQ[here, t * LANES : (t + 1) * LANES] = jnp.where(low, even, odd)

        def joined(pair):
            zero, one = (piece + pltpu.roll(piece, HEAD_DIM, 1) for piece in pair)
            return jnp.where(low, zero, one)

        b.FQ[here, dm.heads : dm.heads + dm.kv] = joined(d_k)
        d_values.append(joined(d_v))
    d_turned = b.FQ[...]
    cosine = jnp.concatenate([b.tabs[0]] * reps, axis=1)
    sine = jnp.concatenate([b.tabs[1]] * reps, axis=1)
    first, ahead, behind = half_turn(d_turned * sine)
    d_lin = (d_turned * cosine + jnp.where(first, ahead, -behind)).astype(BF16)
    d_lin = jnp.concatenate([d_lin, jnp.concatenate(d_values, axis=0).astype(BF16)], axis=1)
    BIG[:, : dm.qkv] = mm_tn(b.npad[...], d_lin).astype(BF16)
    d_bias = jnp.sum(d_lin.astype(F32), axis=0, keepdims=True)
    d_normed = split_mm(mm_nt(d_lin, W[:, : dm.qkv]), b.spr[...], nt=True)
    xf = b.x[...].astype(F32)
    scale1 = lax.rsqrt(jnp.mean(xf * xf, axis=-1, keepdims=True) + 1e-06)
    d_gain1, d_part = norm_back(d_normed, xf, scale1, b.vec[0:1])
    b.gin[...] = (b.dhid[...] + d_part).astype(BF16)

    rows8 = iota((8, dm.d), 0)
    packed = jnp.zeros((8, dm.d), F32)
    for i, piece in enumerate((d_gain1, d_bias[:, : dm.heads], d_gain2)):
        packed = jnp.where(rows8 == i, piece, packed)
    packed = split_mm(packed, b.spr[...])
    mine = own_block(dm)
    spare = jnp.zeros((n, LANES), F32)
    for i in range(3):
        piece = jnp.where(mine, packed[i : i + 1], 0.0).astype(BF16)
        spare = spare + mm_nt(piece, field_matrix(dm, i * FIELD))
    piece = jnp.where(value_block(dm), d_bias[:, dm.heads + dm.kv :], 0.0).astype(BF16)
    spare = spare + mm_nt(piece, value_field(dm))
    key_bias = jnp.broadcast_to(d_bias[:, dm.heads : dm.heads + dm.kv], (n, LANES))
    spare = jnp.concatenate([spare, key_bias], axis=1).astype(BF16)
    BIG[:, : 2 * LANES] = (
        BIG[:, : 2 * LANES].astype(F32) + mm_tn(spare_rows(dm), spare)
    ).astype(BF16)

    cols = pl.ds(0, dm.wide)

    def quad(plane):
        return pl.ds(plane * CHIPS, CHIPS)

    for to in (*far, r):
        send(b.BIG.at[quad(to), other, :, cols], b.aR1.at[quad(to)], b.rA1.at[to], (partner,))
    for to in (*far, r):
        arrived(b.aR1.at[quad(to)], b.rA1.at[to])
        mine_now = b.BIG[quad(to), c, :, cols].astype(F32) + b.aR1[quad(to)].astype(F32)
        b.aR1[quad(to)] = mine_now.astype(BF16)
        send(b.aR1.at[to * CHIPS + diag], b.aR2.at[0, to], b.rA2.at[0, to], dev(r, near * 2 + c))
    for to in (*far, r):
        send(b.aR1.at[to * CHIPS + near], b.aR2.at[1, to], b.rA2.at[1, to], dev(r, near * 2 + c))
    for k in range(1, planes - 1):
        chain_step(down_part, b.zD, b.rW, k)
    chain_step(gate_part(1), b.zR1, b.rZ1, 0)
    for to in (*far, r):
        arrived(b.aR2.at[0, to], b.rA2.at[0, to])
        piece = b.aR1.at[to * CHIPS + next_to]
        piece[...] = (piece[...].astype(F32) + b.aR2[0, to].astype(F32)).astype(BF16)
        send(piece, b.aR2.at[2, to], b.rA2.at[2, to], dev(r, next_to * 2 + c))
    for k in range(1, planes - 2):
        chain_step(gate_part(1), b.zR1, b.rZ1, k)
    total = b.hid[...] + b.oP[q, c].astype(F32)
    for slot in (1, 2):
        arrived(b.oR2.at[slot], b.rO2.at[slot])
        total = total + b.oR2[slot].astype(F32)
    b.out[...] = total.astype(BF16)
    for to in (*far, r):
        total = b.aR1[to * CHIPS + q].astype(F32)
        for slot in (1, 2):
            arrived(b.aR2.at[slot, to], b.rA2.at[slot, to])
            total = total + b.aR2[slot, to].astype(F32)
        b.aR2[0, to] = total.astype(BF16)
    chain_start(attn_part, b.aR3, b.rA3)
    squeeze = b.spr[: dm.unit, : PLANE * rp]

    def home(h, landing, arrive, final):
        start, width = dm.parts[h]
        cols = pl.ds(start, width)
        chain_end(gate_part(h)(r), landing, arrive)
        for i in range(2):
            piece = mm_tn(squeeze, GU[h][my_rows, i * width : (i + 1) * width]).astype(BF16)
            piece = piece.reshape(PLANE, rp, width)
            for place in range(PLANE):
                b.act[2 * place + i, :, cols] = piece[place]
        for k in range(1, PLANE):
            to = (p + k) % PLANE
            send(b.act.at[pl.ds(2 * to, 2), :, cols], b.fgu.at[p, :, :, cols], final.at[p], dev(r, to))
        b.fgu[p, :, :, cols] = b.act[pl.ds(2 * p, 2), :, cols]

    home(0, b.zR0, b.rZ0, b.rF0)
    chain_step(gate_part(1), b.zR1, b.rZ1, planes - 2)
    home(1, b.zR1, b.rZ1, b.rF1)
    for k in range(planes - 1):
        chain_step(attn_part, b.aR3, b.rA3, k)
    sums = b.hid.at[: dm.rfp]
    sums[...] = b.WD[r].astype(F32)
    chain_end(sums, b.zD, b.rW)

    def lay_flat(flat, field):
        blocks = field.shape[1] // LANES
        for j in range(blocks):
            flat[pl.ds(j, field.shape[0], stride=blocks), :] = field[:, j * LANES : (j + 1) * LANES]

    lay_flat(b.fd, sums[: dm.rf])
    b.fa[...] = b.aR2[0, r].astype(F32)
    chain_end(b.fa, b.aR3, b.rA3)
    own_rows = b.fa[: dm.rows]
    h, kv = dm.heads, dm.kv
    lay_flat(b.fq, own_rows[:, :h])
    b.fk[...] = own_rows[:, h : h + kv]
    b.fv[...] = own_rows[:, h + kv : h + 2 * kv]
    lay_flat(b.fo, own_rows[:, h + 2 * kv :])
    b.fs[...] = b.fa[dm.rows : dm.rows + 1, : 2 * LANES]
    for k in range(1, PLANE):
        origin = (p + PLANE - k) % PLANE
        for (start, width), final in zip(dm.parts, (b.rF0, b.rF1)):
            arrived(b.fgu.at[origin, :, :, pl.ds(start, width)], final.at[origin])
    for where in range(CHIPS):
        first_copy(where, b.oP, b.oR1, b.osem, b.rO1).wait_send()
        first_copy(where, b.dP, b.dR1, b.dsem, b.rD1).wait_send()
    for slot in range(CHIPS - 1):
        second_copy(slot, *o_route).wait_send()
        second_copy(slot, *d_route).wait_send()
    drain()


def run_layer(dm, operands):
    n, planes, rp, tok = dm.n, dm.planes, dm.rp, dm.tok
    vm = pltpu.VMEM
    sem = pltpu.SemaphoreType.DMA
    quads = planes * CHIPS
    pairs = dm.heads + dm.kv
    outs = {
        "out": jax.ShapeDtypeStruct((tok, dm.d), BF16),
        "gin": jax.ShapeDtypeStruct((tok, dm.d), BF16),
        "fq": jax.ShapeDtypeStruct((dm.rows * dm.heads // LANES, LANES), F32),
        "fk": jax.ShapeDtypeStruct((dm.rows, LANES), F32),
        "fv": jax.ShapeDtypeStruct((dm.rows, LANES), F32),
        "fo": jax.ShapeDtypeStruct((dm.rows * dm.d // LANES, LANES), F32),
        "fs": jax.ShapeDtypeStruct((1, 2 * LANES), F32),
        "fgu": jax.ShapeDtypeStruct((PLANE, 2, rp, dm.ffr), BF16),
        "fd": jax.ShapeDtypeStruct((dm.rf * dm.d // LANES, LANES), F32),
    }
    n_sends = 1 + (planes - 1) * 16 + 16 * PLANE + 8 * quads + 64
    scratch = {
        "W": vm((quads, 2, rp, dm.wide), BF16),
        "GU0": vm((planes * dm.groups, dm.gs, 2 * dm.parts[0][1]), BF16),
        "GU1": vm((planes * dm.groups, dm.gs, 2 * dm.parts[1][1]), BF16),
        "WD": vm((planes, dm.rfp, dm.d), BF16),
        "nfA": vm((PLANE, tok, dm.d), BF16),
        "gA": vm((PLANE, tok, dm.d), BF16),
        "act": vm((PLANE * tok // rp, rp, dm.ffr), BF16),
        "BIG": vm((quads, 2, rp, 4 * dm.ffr), BF16),
        "oP": vm((CHIPS, 2, tok, dm.d), BF16),
        "dP": vm((CHIPS, 2, tok, dm.d), BF16),
        "oR1": vm((CHIPS, tok, dm.d), BF16),
        "dR1": vm((CHIPS, tok, dm.d), BF16),
        "oR2": vm((CHIPS - 1, tok, dm.d), BF16),
        "dR2": vm((CHIPS - 1, tok, dm.d), BF16),
        "zR0": vm((planes + 1, dm.groups, dm.gs, 2 * dm.parts[0][1]), BF16),
        "zR1": vm((planes + 1, dm.groups, dm.gs, 2 * dm.parts[1][1]), BF16),
        "zD": vm((planes + 1, dm.rfp, dm.d), BF16),
        "aR1": vm((quads, rp, dm.wide), BF16),
        "aR2": vm((CHIPS - 1, planes, rp, dm.wide), BF16),
        "aR3": vm((planes + 1, rp, dm.wide), BF16),
        "QS": vm((dm.micro, HEADS * dm.slots, LANES), BF16),
        "PF": vm((dm.micro, HEADS * dm.slots, dm.slots), F32),
        "hid": vm((tok, dm.d), F32),
        "fa": vm((rp, dm.wide), F32),
        "dhid": vm((tok, dm.d), F32),
        "npad": vm((tok, dm.dp), BF16),
        "mpad": vm((tok, dm.dp), BF16),
        "spr": vm((dm.d, dm.dp), BF16),
        "kd": vm((KV_HEADS, tok, LANES), BF16),
        "vd": vm((KV_HEADS, tok, LANES), BF16),
        "FQ": vm((tok, pairs), F32),
        "tabs": vm((2, tok, LANES), F32),
        "vec": vm((8, dm.d), F32),
        "ssem": sem((n_sends,)),
        "csem": sem((4,)),
        "osem": sem((CHIPS,)),
        "dsem": sem((CHIPS,)),
        "osem2": sem((CHIPS - 1,)),
        "dsem2": sem((CHIPS - 1,)),
        "rA": sem((n,)),
        "rGU": sem((PLANE,)),
        "rGZ0": sem((planes,)),
        "rGZ1": sem((planes,)),
        "rG": sem((PLANE,)),
        "rWD": sem((planes,)),
        "rNF": sem((PLANE,)),
        "rO1": sem((CHIPS,)),
        "rD1": sem((CHIPS,)),
        "rO2": sem((CHIPS - 1,)),
        "rD2": sem((CHIPS - 1,)),
        "rZ0": sem((planes + 1,)),
        "rZ1": sem((planes + 1,)),
        "rF0": sem((PLANE,)),
        "rF1": sem((PLANE,)),
        "rW": sem((planes + 1,)),
        "rA1": sem((planes,)),
        "rA2": sem((CHIPS - 1, planes)),
        "rA3": sem((planes + 1,)),
    }
    return pl.pallas_call(
        functools.partial(layer_kernel, dm, (*operands, *outs, *scratch)),
        name="layer",
        out_shape=list(outs.values()),
        in_specs=[pl.BlockSpec(memory_space=pltpu.VMEM)] * len(operands),
        out_specs=[pl.BlockSpec(memory_space=pltpu.VMEM)] * len(outs),
        scratch_shapes=list(scratch.values()),
        compiler_params=pltpu.CompilerParams(
            collective_id=0, has_side_effects=True, vmem_limit_bytes=67043328
        ),
    )(*operands.values())


def per_device(n, *args):
    (
        tokens,
        positions,
        cotangent,
        norm_attn,
        w_query,
        b_query,
        w_key,
        b_key,
        w_value,
        b_value,
        w_out,
        norm_ffn,
        w_gate,
        w_up,
        w_down,
    ) = args
    micro, slots, d = tokens.shape
    dm = Dims(n, d, w_gate.shape[0] * n // d, slots, micro)
    rows, rp = dm.rows, dm.rp

    def lanes(vector):
        return jnp.pad(vector, (0, FIELD - vector.shape[0]))

    spare = jnp.concatenate([lanes(v) for v in (norm_attn, b_query, norm_ffn, b_value)])
    spare = jnp.pad(spare, (0, dm.wide - spare.shape[0]))
    pack = jnp.concatenate(
        [w.reshape(rows, -1) for w in (w_query, w_key, w_value, w_out)], axis=1
    )
    pack = jnp.concatenate([pack, spare[None]], axis=0)
    pack = jnp.pad(pack, ((0, rp - rows - 1), (0, 0)))

    def columns(weight):
        weight = weight.reshape(rows, dm.planes, PLANE, dm.rf)
        weight = jnp.pad(weight, ((0, rp - rows), (0, 0), (0, 0), (0, dm.rfp - dm.rf)))
        return weight.transpose(2, 0, 1, 3).reshape(PLANE, rp, dm.ffr)

    both = jnp.stack([columns(w_gate), columns(w_up)], axis=1)
    down = jnp.pad(w_down.reshape(dm.rf, d), ((0, dm.rfp - dm.rf), (0, 0)))
    operands = {
        "x": tokens.reshape(dm.tok, d),
        "g": cotangent.reshape(dm.tok, d),
        "posr": positions,
        "bkey": b_key[None],
        "ap": pack,
        "gus": both,
        "wds": down,
    }
    out, gin, fq, fk, fv, fo, fs, fgu, fd = run_layer(dm, operands)

    def field(i, size):
        return fs[0, i * FIELD : i * FIELD + size]

    def gate_part(i):
        part = fgu[:, i, :rows].astype(F32)
        part = part.reshape(PLANE, rows, dm.planes, dm.rfp)[..., : dm.rf]
        return part.transpose(1, 2, 0, 3).reshape(-1)

    return (
        out.reshape(micro, slots, d),
        gin.reshape(micro, slots, d),
        field(0, rows),
        fq.reshape(-1),
        field(1, rows),
        fk.reshape(-1),
        fs[0, LANES : LANES + dm.kv],
        fv.reshape(-1),
        field(3, dm.rv),
        fo.reshape(-1),
        field(2, rows),
        gate_part(0),
        gate_part(1),
        fd.reshape(-1),
    )


def solution(mesh):
    n = mesh.shape["dp"]
    split, row = P("dp"), P(None, "dp", None)
    in_specs = (row, P(None, "dp"), row, *[split] * 4, P(), *[split] * 7)
    out_specs = (row, row, *[split] * 4, P(), *[split] * 7)
    return jax.shard_map(
        functools.partial(per_device, n),
        mesh=mesh,
        in_specs=in_specs,
        out_specs=out_specs,
        check_vma=False,
    )
```

```python
import functools
import math

import jax
import jax.numpy as jnp
from jax import lax
from jax.experimental import pallas as pl
from jax.experimental.pallas import tpu as pltpu
from jax.sharding import PartitionSpec as P

HEADS = 14
KV_HEADS = 2
HEAD_DIM = 64
GROUP = HEADS // KV_HEADS
PLANE = 8
CHIPS = 4
LANES = 128
ROTARY_LOG = math.log(1000000.0)
FIELD = 32
MESH = pl.DeviceIdType.MESH
F32 = jnp.float32
BF16 = jnp.bfloat16


def up(value, step):
    return -(-value // step) * step


def mm(left, right, dims=((1,), (0,))):
    return lax.dot_general(left, right, (dims, ((), ())), preferred_element_type=F32)


def mm_nt(left, right):
    return mm(left, right, ((1,), (1,)))


def mm_tn(left, right):
    return mm(left, right, ((0,), (0,)))


def split_mm(left, right, nt=False):
    high = left.astype(BF16)
    low = (left - high.astype(F32)).astype(BF16)
    dot = mm_nt if nt else mm
    return dot(high, right) + dot(low, right)


def iota(shape, dim):
    return lax.broadcasted_iota(jnp.int32, shape, dim)


class Dims:
    def __init__(self, n, d, ff, slots, micro):
        self.n, self.d, self.ff = n, d, ff
        self.planes = n // PLANE
        self.rows = d // n
        self.rp = 8
        while self.rp < self.rows + 1:
            self.rp *= 2
        self.dp = n * self.rp
        self.rf = ff // n
        self.ffr = up(ff // PLANE, LANES)
        self.rfp = self.ffr // self.planes
        self.slots, self.micro = slots, micro
        self.tok = slots * micro
        self.heads = HEADS * HEAD_DIM
        self.kv = KV_HEADS * HEAD_DIM
        self.qkv = self.heads + 2 * self.kv
        self.wide = self.qkv + d
        self.rv = self.kv // n
        self.unit = PLANE * self.rows
        self.gs = 16 if self.unit % 16 == 0 else 8
        self.groups = self.unit // self.gs
        blocks = self.ffr // LANES
        first = blocks // 2 * LANES
        self.parts = ((0, first), (first, self.ffr - first))


def spread_matrix(dm):
    shape = (dm.d, dm.dp)
    row, col = iota(shape, 0), iota(shape, 1)
    inner = col & (dm.rp - 1)
    hit = (row == (col // dm.rp) * dm.rows + inner) & (inner < dm.rows)
    return jnp.where(hit, 1.0, 0.0).astype(BF16)


def field_matrix(dm, offset):
    shape = (LANES, dm.dp)
    row, col = iota(shape, 0), iota(shape, 1)
    inner = col & (dm.rp - 1)
    return jnp.where((row == offset + inner) & (inner < dm.rows), 1.0, 0.0).astype(BF16)


def own_block(dm):
    shape = (dm.n, dm.dp)
    return iota(shape, 1) // dm.rp == iota(shape, 0)


def spare_rows(dm):
    shape = (dm.n, dm.dp)
    return jnp.where(iota(shape, 1) == iota(shape, 0) * dm.rp + dm.rows, 1.0, 0.0).astype(BF16)


def value_field(dm):
    shape = (LANES, LANES)
    return jnp.where(
        iota(shape, 0) == 3 * FIELD + (iota(shape, 1) & (dm.rv - 1)), 1.0, 0.0
    ).astype(BF16)


def value_block(dm):
    shape = (dm.n, LANES)
    return iota(shape, 1) // dm.rv == iota(shape, 0)


def half_turn(field):
    width = field.shape[-1]
    first = (iota(field.shape, 1) & (HEAD_DIM - 1)) < HEAD_DIM // 2
    ahead = pltpu.roll(field, width - HEAD_DIM // 2, 1)
    behind = pltpu.roll(field, HEAD_DIM // 2, 1)
    return first, ahead, behind


def twice(field):
    low = iota(field.shape, 1) < HEAD_DIM
    turned = pltpu.roll(field, HEAD_DIM, 1)
    return jnp.where(low, field, turned), jnp.where(low, turned, field)


class Refs:
    def __init__(self, names, refs):
        self.__dict__.update(zip(names, refs, strict=True))


def layer_kernel(dm, names, *refs):
    b = Refs(names, refs)
    n, planes, rp = dm.n, dm.planes, dm.rp
    me = lax.axis_index("dp")
    r, p = me // PLANE, me % PLANE
    q, c = p // 2, p % 2
    other = 1 - c
    partner = r * PLANE + q * 2 + other

    def dev(plane, place):
        return (plane * PLANE + place,)

    barrier = pltpu.get_barrier_semaphore()
    peers = [dev(r, (p + k) % PLANE) for k in range(1, PLANE)]
    peers += [dev((r + k) % planes, p) for k in range(1, planes)]
    for peer in peers:
        pl.semaphore_signal(barrier, inc=1, device_id=peer, device_id_type=MESH)
    pl.semaphore_wait(barrier, len(peers))

    pending = []
    count = [0]

    def prepare(src, dst, arrive, to, cond=None, tag=None):
        copy = pltpu.make_async_remote_copy(
            src_ref=src,
            dst_ref=dst,
            send_sem=b.ssem.at[count[0]],
            recv_sem=arrive,
            device_id=to,
            device_id_type=MESH,
        )
        count[0] += 1
        pending.append((copy, cond, tag))
        return copy

    def send(src, dst, arrive, to, cond=None, tag=None):
        copy = prepare(src, dst, arrive, to, cond, tag)
        if cond is None:
            copy.start()
        else:
            pl.when(cond)(copy.start)

    def drain(tag=None):
        now = [item for item in pending if tag in (None, item[2])]
        for copy, cond, _ in now:
            if cond is None:
                copy.wait_send()
            else:
                pl.when(cond)(copy.wait_send)
        pending[:] = [item for item in pending if tag not in (None, item[2])]

    upper = r // max(planes // 2, 1)
    mirror = r + upper * (planes - 1 - 2 * r)

    def origin_of(k):
        spot = k - (mirror + planes - k) // planes
        return spot + upper * (planes - 1 - 2 * spot)

    def relay_own(src, dst, arrive, tag=None):
        send(src, dst, arrive, dev(r + 1, p), r + 1 < planes, tag)
        send(src, dst, arrive, dev(r - 1, p), r >= 1, tag)

    def onward(part, sems, k, tag=None):
        origin = origin_of(k)
        to = r - 1 + 2 * ((r - origin - 1 + planes) // planes)
        cond = (to >= 0) & (to < planes)
        piece, arrive = part(origin), sems.at[origin]
        return piece, arrive, cond, prepare(piece, piece, arrive, dev(to, p), cond, tag)

    def pass_on(piece, arrive, cond, copy):
        @pl.when(cond)
        def _():
            arrived(piece, arrive)
            copy.start()

    def settle(piece, arrive, cond, copy):
        pl.when(jnp.logical_not(cond))(lambda: arrived(piece, arrive))

    def arrived(dst, arrive):
        pltpu.make_async_remote_copy(
            src_ref=dst,
            dst_ref=dst,
            send_sem=b.ssem.at[0],
            recv_sem=arrive,
            device_id=(partner,),
            device_id_type=MESH,
        ).wait_recv()

    def block(ref, index):
        return ref.at[index // 2, index % 2]

    def plane_rows(ref, plane):
        return ref.at[pl.ds(plane * dm.groups, dm.groups)]

    keep = [
        pltpu.make_async_copy(b.ap, block(b.W, me), b.csem.at[0]),
        pltpu.make_async_copy(b.gus.at[p], b.fgu.at[p], b.csem.at[1]),
        pltpu.make_async_copy(b.g, b.gA.at[p], b.csem.at[2]),
        pltpu.make_async_copy(b.wds, b.WD.at[r], b.csem.at[3]),
    ]
    for copy in keep:
        copy.start()

    relay_own(b.ap, block(b.W, me), b.rA.at[me])

    across, along = q + 1 - 2 * (q % 2), (q + 2) % CHIPS
    near = across * other + along * c
    next_to = along * other + across * c
    spots = (near, next_to, CHIPS - 1 - q)

    def fan(index, src):
        for where in (next_to, near):
            send(src, block(b.W, index), b.rA.at[index], dev(r, where * 2 + c))

    def spread_out(src, ref, arrive):
        for where in (next_to, near):
            send(src, ref.at[p], arrive.at[p], dev(r, where * 2 + c))
        send(src, ref.at[p], arrive.at[p], (partner,))

    def hand_on(ref, arrive, where):
        place = where * 2 + c
        arrived(ref.at[place], arrive.at[place])
        if where is near:
            send(ref.at[place], ref.at[place], arrive.at[place], dev(r, next_to * 2 + c))
        send(ref.at[place], ref.at[place], arrive.at[place], (partner,))

    fan(me, b.ap)
    send(b.ap, block(b.W, me), b.rA.at[me], (partner,))
    for k in range(1, PLANE):
        send(b.gus.at[(p + k) % PLANE], b.fgu.at[p], b.rGU.at[p], dev(r, (p + k) % PLANE))
    relay_own(b.wds, b.WD.at[r], b.rWD.at[r])

    tok = dm.tok
    xf = b.x[...].astype(F32)
    scale1 = lax.rsqrt(jnp.mean(xf * xf, axis=-1, keepdims=True) + 1e-06)
    diagonal = iota((dm.slots, dm.slots), 0) == iota((dm.slots, dm.slots), 1)
    posc = [
        jnp.sum(jnp.where(diagonal, b.posr[m : m + 1].astype(F32), 0.0), axis=1, keepdims=True)
        for m in range(dm.micro)
    ]
    power = (iota((1, LANES), 1) & (HEAD_DIM // 2 - 1)).astype(F32) * (-2.0 / HEAD_DIM * ROTARY_LOG)
    angle = jnp.concatenate(posc, axis=0) * jnp.exp(power)
    b.tabs[0] = jnp.cos(angle)
    b.tabs[1] = jnp.sin(angle)
    b.spr[...] = spread_matrix(dm)

    for k in range(1, planes):
        origin = origin_of(k)
        index = origin * PLANE + p
        arrived(block(b.W, index), b.rA.at[index])
        to = r - 1 + 2 * ((r - origin - 1 + planes) // planes)
        send(block(b.W, index), block(b.W, index), b.rA.at[index], dev(to, p), (to >= 0) & (to < planes))
        fan(index, block(b.W, index))
        send(block(b.W, index), block(b.W, index), b.rA.at[index], (partner,))
    for k in range(1, PLANE):
        origin = (p + PLANE - k) % PLANE
        arrived(b.fgu.at[origin], b.rGU.at[origin])
    keep[1].wait()
    GU = [ref.reshape(dm.d, ref.shape[-1]) for ref in (b.GU0, b.GU1)]
    my_rows = pl.ds(pl.multiple_of(r * dm.unit, dm.gs), dm.unit)
    squeeze = b.spr[: dm.unit, : PLANE * rp]
    for h, (start, width) in enumerate(dm.parts):
        for i in range(2):
            piece = b.fgu[:, i, :, start : start + width].reshape(PLANE * rp, width)
            GU[h][my_rows, i * width : (i + 1) * width] = mm(squeeze, piece).astype(BF16)

    def gate_part(h):
        ref = (b.GU0, b.GU1)[h]
        return lambda plane: plane_rows(ref, plane)

    def down_part(plane):
        return b.WD.at[plane]

    relay_own(gate_part(0)(r), gate_part(0)(r), b.rGZ0.at[r], "gate0")
    steps = range(1, planes)
    down_on = [onward(down_part, b.rWD, k, "down") for k in steps]
    gate_on = [[onward(gate_part(h), sems, k, f"gate{h}") for k in steps] for h, sems in ((0, b.rGZ0), (1, b.rGZ1))]
    pass_on(*down_on[0])
    origins = [r, *(origin_of(k) for k in steps)]
    for i, where in enumerate(spots):
        for origin in origins:
            index = origin * PLANE + where * 2 + c
            arrived(block(b.W, index), b.rA.at[index])
            if i == 0:
                send(block(b.W, index), block(b.W, index), b.rA.at[index], dev(r, next_to * 2 + c))
            send(block(b.W, index), block(b.W, index), b.rA.at[index], (partner,))
    spread_out(b.g, b.gA, b.rG)
    for item in down_on[1:]:
        pass_on(*item)

    keep[0].wait()
    for k in range(CHIPS):
        for shift in range(planes):
            index = ((r + planes - shift) % planes) * PLANE + ((q + CHIPS - k) % CHIPS) * 2 + other
            arrived(block(b.W, index), b.rA.at[index])

    W = b.W.reshape(dm.dp, dm.wide)
    small = mm(spare_rows(dm), W[:, :LANES]).astype(BF16)
    mine = own_block(dm)
    rows8 = iota((8, dm.dp), 0)
    padded = jnp.zeros((8, dm.dp), F32)
    for i in range(3):
        piece = mm(small, field_matrix(dm, i * FIELD))
        piece = jnp.sum(jnp.where(mine, piece, 0.0), axis=0, keepdims=True)
        padded = jnp.where(rows8 == i, piece, padded)
    b.vec[...] = mm_nt(padded.astype(BF16), b.spr[...])
    gain1, bias_q, gain2 = b.vec[0:1], b.vec[1:2], b.vec[2:3]
    bias_v = jnp.sum(
        jnp.where(value_block(dm), mm(small, value_field(dm)), 0.0), axis=0, keepdims=True
    )
    bias_k = b.bkey[...].astype(F32)

    normed = (xf * scale1 * gain1).astype(BF16)
    b.npad[...] = mm(normed, b.spr[...]).astype(BF16)
    lin = mm(b.npad[...], W[:, : dm.qkv])
    turn_in = jnp.concatenate([lin[:, : dm.heads] + bias_q, lin[:, dm.heads : dm.heads + dm.kv] + bias_k], axis=1)
    reps = (dm.heads + dm.kv) // LANES
    cosine = jnp.concatenate([b.tabs[0]] * reps, axis=1)
    sine = jnp.concatenate([b.tabs[1]] * reps, axis=1)
    first, ahead, behind = half_turn(turn_in)
    turned = turn_in * cosine + jnp.where(first, -ahead, behind) * sine
    values = lin[:, dm.heads + dm.kv :] + bias_v
    for i, piece in enumerate(twice(turned[:, dm.heads :])):
        b.kd[i] = piece.astype(BF16)
    for i, piece in enumerate(twice(values)):
        b.vd[i] = piece.astype(BF16)
    low = iota((dm.slots, LANES), 1) < HEAD_DIM

    def stack_heads(field, store):
        for h in range(HEADS):
            part = field[:, LANES * (h // 2) : LANES * (h // 2) + LANES]
            part = jnp.where(low if h % 2 == 0 else ~low, part, 0.0)
            store(h)[...] = part.astype(BF16)

    span = GROUP * dm.slots
    mix = b.oP.at[0, 0]
    BIG = b.BIG.reshape(dm.dp, 4 * dm.ffr)
    dms = [BIG.at[:span, dm.wide + kv * LANES : dm.wide + (kv + 1) * LANES] for kv in range(KV_HEADS)]

    def head_rows(h):
        return dms[h // GROUP].at[(h % GROUP) * dm.slots : (h % GROUP + 1) * dm.slots]

    for m in range(dm.micro):
        here = slice(m * dm.slots, (m + 1) * dm.slots)
        stack_heads(turned[here, : dm.heads], lambda h: b.QS.at[m, h * dm.slots : (h + 1) * dm.slots])
        grid = (dm.slots, dm.slots)
        start_row = iota((dm.slots, 1), 0).astype(F32) - posc[m]
        start_col = (iota((1, dm.slots), 1) - b.posr[m : m + 1]).astype(F32)
        allowed = (start_row == start_col) & (iota(grid, 1) <= iota(grid, 0))
        for kv in range(KV_HEADS):
            rows = slice(kv * span, (kv + 1) * span)
            score = mm_nt(b.QS[m, rows], b.kd[kv, here]) * 0.125
            score = jnp.where(allowed[None], score.reshape(GROUP, *grid), -1e30)
            top = jnp.max(score, axis=-1, keepdims=True)
            expo = jnp.exp(score - top)
            prob = expo / jnp.sum(expo, axis=-1, keepdims=True)
            prob = prob.reshape(span, dm.slots)
            b.PF[m, rows] = prob
            dms[kv][...] = mm(prob.astype(BF16), b.vd[kv, here]).astype(BF16)
        for t in range(HEADS // 2):
            even, odd = head_rows(2 * t)[...], head_rows(2 * t + 1)[...]
            mix[here, t * LANES : (t + 1) * LANES] = jnp.where(low, even, odd)
    b.mpad[...] = mm(mix[...], b.spr[...]).astype(BF16)
    hidden = xf + mm(b.mpad[...], W[:, dm.qkv :])
    b.hid[...] = hidden
    scale2 = lax.rsqrt(jnp.mean(hidden * hidden, axis=-1, keepdims=True) + 1e-06)
    nf = (hidden * scale2 * gain2).astype(BF16)
    b.nfA[p] = nf

    spread_out(b.nfA.at[p], b.nfA, b.rNF)
    pass_on(*gate_on[0][0])
    hand_on(b.gA, b.rG, near)
    for item in gate_on[0][1:]:
        pass_on(*item)
    relay_own(gate_part(1)(r), gate_part(1)(r), b.rGZ1.at[r], "gate1")
    hand_on(b.nfA, b.rNF, near)
    pass_on(*gate_on[1][0])
    for where in spots[1:]:
        hand_on(b.gA, b.rG, where)
    for where in spots[1:]:
        hand_on(b.nfA, b.rNF, where)
    for item in gate_on[1][1:]:
        pass_on(*item)
    for item in (*down_on, *gate_on[0]):
        settle(*item)
    keep[2].wait()
    keep[3].wait()
    for k in range(CHIPS):
        place = ((q + CHIPS - k) % CHIPS) * 2 + other
        arrived(b.gA.at[place], b.rG.at[place])
        arrived(b.nfA.at[place], b.rNF.at[place])

    ACT = b.act.reshape(PLANE * tok, dm.ffr)
    WD = b.WD.reshape(dm.ffr, dm.d)
    half = PLANE // 2

    base = (0, 4 * dm.parts[0][1])

    def feed(h, place_q, place_c):
        place = place_q * 2 + place_c
        start, width = dm.parts[h]
        nf_t, g_t = b.nfA[place], b.gA[place]
        down = WD[start : start + width]
        pre = mm(nf_t, GU[h][...])
        gate, upper = pre[:, :width], pre[:, width:]
        sigma = jax.nn.sigmoid(gate)
        silu = gate * sigma
        act = (silu * upper).astype(BF16)
        ACT[pl.ds(pl.multiple_of(place * tok, tok), tok), start : start + width] = act
        d_act = mm_nt(g_t, down)
        d_gate = (d_act * upper * (sigma + silu * (1.0 - sigma))).astype(BF16)
        d_up = (d_act * silu).astype(BF16)
        d_both = jnp.concatenate([d_gate, d_up], axis=1)
        rows = pl.ds(pl.multiple_of((place % half) * tok, tok), tok)
        cols = pl.ds(pl.multiple_of(base[h] + (place // half) * 2 * width, LANES), 2 * width)
        BIG[rows, cols] = d_both
        for ref, value in ((b.oP, mm(act, down)), (b.dP, mm_nt(d_both, GU[h][...]))):
            if h:
                value = value + ref[place_q, place_c].astype(F32)
            ref[place_q, place_c] = value.astype(BF16)

    def first_copy(where, part, landing, sems, arrive):
        return pltpu.make_async_remote_copy(
            src_ref=part.at[where, other],
            dst_ref=landing.at[where],
            send_sem=sems.at[where],
            recv_sem=arrive.at[where],
            device_id=(partner,),
            device_id_type=MESH,
        )

    diag = CHIPS - 1 - q
    routes = ((diag, near), (near, near), (next_to, next_to))

    def second_copy(slot, part, landing, sems, arrive):
        source, to = routes[slot]
        return pltpu.make_async_remote_copy(
            src_ref=part.at[source, c],
            dst_ref=landing.at[slot],
            send_sem=sems.at[slot],
            recv_sem=arrive.at[slot],
            device_id=dev(r, to * 2 + c),
            device_id_type=MESH,
        )

    def add_on(part, landing, sems, arrive):
        arrived(landing.at[0], arrive.at[0])
        part[next_to, c] = (part[next_to, c].astype(F32) + landing[0].astype(F32)).astype(BF16)
        second_copy(2, part, landing, sems, arrive).start()

    d_route = (b.dP, b.dR2, b.dsem2, b.rD2)
    o_route = (b.oP, b.oR2, b.osem2, b.rO2)

    def hop(part, landing, arrive, to, cond):
        ahead = (to - r - 1 + planes) // planes
        beyond = r - to - 1 + 2 * planes * ahead
        last = 1 - (beyond + 4 * planes - 1) // (4 * planes)
        slot = to + (planes - to) * last
        send(part(to), landing.at[slot], arrive.at[slot], dev(r - 1 + 2 * ahead, p), cond)

    def behind_of(to):
        ahead = (to - r - 1 + planes) // planes
        follows = r + 1 - 2 * ahead
        return (follows >= 0) & (follows < planes)

    far = [origin_of(planes - k) for k in range(1, planes)]

    def chain_start(part, landing, arrive):
        for to in far:
            hop(part, landing, arrive, to, jnp.logical_not(behind_of(to)))

    def chain_step(part, landing, arrive, k):
        to = far[k]
        has = behind_of(to)

        @pl.when(has)
        def _():
            arrived(landing.at[to], arrive.at[to])
            mine = part(to)
            mine[...] = (mine[...].astype(F32) + landing[to].astype(F32)).astype(BF16)

        hop(part, landing, arrive, to, has)

    def chain_end(total, landing, arrive):
        for slot, cond in ((r, r >= 1), (planes, r + 1 < planes)):

            @pl.when(cond)
            def _():
                arrived(landing.at[slot], arrive.at[slot])
                total[...] = (total[...].astype(F32) + landing[slot].astype(F32)).astype(total.dtype)

    nf_all = b.nfA.reshape(PLANE * tok, dm.d)
    g_all = b.gA.reshape(PLANE * tok, dm.d)
    wide_rows = half * tok
    chunk = 2 * LANES

    def gate_grad(h):
        width = dm.parts[h][1]

        def some(start, count):
            cols = pl.ds(start, count)
            total = mm_tn(nf_all[:wide_rows, cols], BIG[:, base[h] : base[h] + 2 * width])
            total = total + mm_tn(nf_all[wide_rows:, cols], BIG[:, base[h] + 2 * width : base[h] + 4 * width])
            GU[h][cols, :] = total.astype(BF16)

        @pl.loop(0, dm.d // chunk)
        def _(i):
            some(pl.multiple_of(i * chunk, chunk), chunk)

        if dm.d % chunk:
            some(dm.d - dm.d % chunk, dm.d % chunk)

    @pl.loop(0, PLANE)
    def _(turn):
        feed(0, turn // 2, turn % 2)

    drain("gate0")
    gate_grad(0)
    chain_start(gate_part(0), b.zR0, b.rZ0)
    for item in gate_on[1]:
        settle(*item)

    def join(where):
        for part, one, arrive in ((b.dP, b.dR1, b.rD1), (b.oP, b.oR1, b.rO1)):
            arrived(one.at[where], arrive.at[where])
            part[where, c] = (part[where, c].astype(F32) + one[where].astype(F32)).astype(BF16)

    @pl.loop(0, CHIPS)
    def _(step):
        one, two = (CHIPS - 1 - step) % 2, (CHIPS - 1 - step) // 2
        over_x, over_y = one * other + two * c, two * other + one * c
        where = 2 * ((q // 2 + over_y) % 2) + (q % 2 + over_x) % 2

        @pl.loop(0, 2)
        def _(turn):
            feed(1, where, (other + turn) % 2)

            @pl.when(turn == 0)
            def _():
                first_copy(where, b.dP, b.dR1, b.dsem, b.rD1).start()
                first_copy(where, b.oP, b.oR1, b.osem, b.rO1).start()

        for at, source in ((1, diag), (2, near)):

            @pl.when(step == at)
            def _():
                join(source)
                second_copy(at - 1, *d_route).start()

    join(next_to)
    add_on(*d_route)
    for slot in range(2):
        second_copy(slot, *o_route).start()
    join(q)

    def attn_part(plane):
        return b.aR2.at[0, plane]

    drain("down")
    WD[...] = mm_tn(ACT[...], g_all[...]).astype(BF16)
    chain_start(down_part, b.zD, b.rW)
    drain("gate1")
    gate_grad(1)
    chain_start(gate_part(1), b.zR1, b.rZ1)
    for k in range(planes - 1):
        chain_step(gate_part(0), b.zR0, b.rZ0, k)
    add_on(*o_route)
    d_nf = b.dP[q, c].astype(F32)
    for slot in (1, 2):
        arrived(b.dR2.at[slot], b.rD2.at[slot])
        d_nf = d_nf + b.dR2[slot].astype(F32)
    hidden = b.hid[...]
    scale2 = lax.rsqrt(jnp.mean(hidden * hidden, axis=-1, keepdims=True) + 1e-06)

    def norm_back(grad, field, scale, gain):
        weighted = grad * gain
        d_gain = jnp.sum(grad * field * scale, axis=0, keepdims=True)
        d_field = weighted * scale - field * (scale * scale * scale) * jnp.mean(
            weighted * field, axis=-1, keepdims=True
        )
        return d_gain, d_field

    d_gain2, d_part = norm_back(d_nf, hidden, scale2, b.vec[2:3])
    d_hidden = b.g[...].astype(F32) + d_part
    b.dhid[...] = d_hidden
    d_attn = d_hidden.astype(BF16)
    chain_step(down_part, b.zD, b.rW, 0)
    BIG[:, dm.qkv : dm.wide] = mm_tn(b.mpad[...], d_attn).astype(BF16)
    d_mixed = mm_nt(d_attn, W[:, dm.qkv :]).astype(BF16)
    d_mixed = mm_nt(d_mixed, b.spr[...])
    d_values = []
    for m in range(dm.micro):
        here = slice(m * dm.slots, (m + 1) * dm.slots)
        stack_heads(d_mixed[here], head_rows)
        d_v, d_k = [], []
        for kv in range(KV_HEADS):
            rows = slice(kv * span, (kv + 1) * span)
            d_mix, prob, qs = dms[kv][...], b.PF[m, rows], b.QS[m, rows]
            d_v.append(mm_tn(prob.astype(BF16), d_mix))
            d_prob = mm_nt(d_mix, b.vd[kv, here])
            delta = jnp.sum(d_prob * prob, axis=-1, keepdims=True)
            d_score = (prob * (d_prob - delta)).astype(BF16)
            d_k.append(0.125 * mm_tn(d_score, qs))
            b.PF[m, rows] = 0.125 * mm(d_score, b.kd[kv, here])
        for t in range(HEADS // 2):
            even = b.PF[m, 2 * t * dm.slots : (2 * t + 1) * dm.slots]
            odd = b.PF[m, (2 * t + 1) * dm.slots : (2 * t + 2) * dm.slots]
            b.FQ[here, t * LANES : (t + 1) * LANES] = jnp.where(low, even, odd)

        def joined(pair):
            zero, one = (piece + pltpu.roll(piece, HEAD_DIM, 1) for piece in pair)
            return jnp.where(low, zero, one)

        b.FQ[here, dm.heads : dm.heads + dm.kv] = joined(d_k)
        d_values.append(joined(d_v))
    d_turned = b.FQ[...]
    cosine = jnp.concatenate([b.tabs[0]] * reps, axis=1)
    sine = jnp.concatenate([b.tabs[1]] * reps, axis=1)
    first, ahead, behind = half_turn(d_turned * sine)
    d_lin = (d_turned * cosine + jnp.where(first, ahead, -behind)).astype(BF16)
    d_lin = jnp.concatenate([d_lin, jnp.concatenate(d_values, axis=0).astype(BF16)], axis=1)
    BIG[:, : dm.qkv] = mm_tn(b.npad[...], d_lin).astype(BF16)
    d_bias = jnp.sum(d_lin.astype(F32), axis=0, keepdims=True)
    d_normed = split_mm(mm_nt(d_lin, W[:, : dm.qkv]), b.spr[...], nt=True)
    xf = b.x[...].astype(F32)
    scale1 = lax.rsqrt(jnp.mean(xf * xf, axis=-1, keepdims=True) + 1e-06)
    d_gain1, d_part = norm_back(d_normed, xf, scale1, b.vec[0:1])
    b.gin[...] = (b.dhid[...] + d_part).astype(BF16)

    rows8 = iota((8, dm.d), 0)
    packed = jnp.zeros((8, dm.d), F32)
    for i, piece in enumerate((d_gain1, d_bias[:, : dm.heads], d_gain2)):
        packed = jnp.where(rows8 == i, piece, packed)
    packed = split_mm(packed, b.spr[...])
    mine = own_block(dm)
    spare = jnp.zeros((n, LANES), F32)
    for i in range(3):
        piece = jnp.where(mine, packed[i : i + 1], 0.0).astype(BF16)
        spare = spare + mm_nt(piece, field_matrix(dm, i * FIELD))
    piece = jnp.where(value_block(dm), d_bias[:, dm.heads + dm.kv :], 0.0).astype(BF16)
    spare = spare + mm_nt(piece, value_field(dm))
    key_bias = jnp.broadcast_to(d_bias[:, dm.heads : dm.heads + dm.kv], (n, LANES))
    spare = jnp.concatenate([spare, key_bias], axis=1).astype(BF16)
    BIG[:, : 2 * LANES] = (
        BIG[:, : 2 * LANES].astype(F32) + mm_tn(spare_rows(dm), spare)
    ).astype(BF16)

    cols = pl.ds(0, dm.wide)

    def quad(plane):
        return pl.ds(plane * CHIPS, CHIPS)

    for to in (*far, r):
        send(b.BIG.at[quad(to), other, :, cols], b.aR1.at[quad(to)], b.rA1.at[to], (partner,))
    for to in (*far, r):
        arrived(b.aR1.at[quad(to)], b.rA1.at[to])
        mine_now = b.BIG[quad(to), c, :, cols].astype(F32) + b.aR1[quad(to)].astype(F32)
        b.aR1[quad(to)] = mine_now.astype(BF16)
        send(b.aR1.at[to * CHIPS + diag], b.aR2.at[0, to], b.rA2.at[0, to], dev(r, near * 2 + c))
    for to in (*far, r):
        send(b.aR1.at[to * CHIPS + near], b.aR2.at[1, to], b.rA2.at[1, to], dev(r, near * 2 + c))
    for k in range(1, planes - 1):
        chain_step(down_part, b.zD, b.rW, k)
    chain_step(gate_part(1), b.zR1, b.rZ1, 0)
    for to in (*far, r):
        arrived(b.aR2.at[0, to], b.rA2.at[0, to])
        piece = b.aR1.at[to * CHIPS + next_to]
        piece[...] = (piece[...].astype(F32) + b.aR2[0, to].astype(F32)).astype(BF16)
        send(piece, b.aR2.at[2, to], b.rA2.at[2, to], dev(r, next_to * 2 + c))
    for k in range(1, planes - 2):
        chain_step(gate_part(1), b.zR1, b.rZ1, k)
    total = b.hid[...] + b.oP[q, c].astype(F32)
    for slot in (1, 2):
        arrived(b.oR2.at[slot], b.rO2.at[slot])
        total = total + b.oR2[slot].astype(F32)
    b.out[...] = total.astype(BF16)
    for to in (*far, r):
        total = b.aR1[to * CHIPS + q].astype(F32)
        for slot in (1, 2):
            arrived(b.aR2.at[slot, to], b.rA2.at[slot, to])
            total = total + b.aR2[slot, to].astype(F32)
        b.aR2[0, to] = total.astype(BF16)
    chain_start(attn_part, b.aR3, b.rA3)
    squeeze = b.spr[: dm.unit, : PLANE * rp]

    def home(h, landing, arrive, final):
        start, width = dm.parts[h]
        cols = pl.ds(start, width)
        chain_end(gate_part(h)(r), landing, arrive)
        for i in range(2):
            piece = mm_tn(squeeze, GU[h][my_rows, i * width : (i + 1) * width]).astype(BF16)
            piece = piece.reshape(PLANE, rp, width)
            for place in range(PLANE):
                b.act[2 * place + i, :, cols] = piece[place]
        for k in range(1, PLANE):
            to = (p + k) % PLANE
            send(b.act.at[pl.ds(2 * to, 2), :, cols], b.fgu.at[p, :, :, cols], final.at[p], dev(r, to))
        b.fgu[p, :, :, cols] = b.act[pl.ds(2 * p, 2), :, cols]

    home(0, b.zR0, b.rZ0, b.rF0)
    chain_step(gate_part(1), b.zR1, b.rZ1, planes - 2)
    home(1, b.zR1, b.rZ1, b.rF1)
    for k in range(planes - 1):
        chain_step(attn_part, b.aR3, b.rA3, k)
    sums = b.hid.at[: dm.rfp]
    sums[...] = b.WD[r].astype(F32)
    chain_end(sums, b.zD, b.rW)

    def lay_flat(flat, field):
        blocks = field.shape[1] // LANES
        for j in range(blocks):
            flat[pl.ds(j, field.shape[0], stride=blocks), :] = field[:, j * LANES : (j + 1) * LANES]

    lay_flat(b.fd, sums[: dm.rf])
    b.fa[...] = b.aR2[0, r].astype(F32)
    chain_end(b.fa, b.aR3, b.rA3)
    own_rows = b.fa[: dm.rows]
    h, kv = dm.heads, dm.kv
    lay_flat(b.fq, own_rows[:, :h])
    b.fk[...] = own_rows[:, h : h + kv]
    b.fv[...] = own_rows[:, h + kv : h + 2 * kv]
    lay_flat(b.fo, own_rows[:, h + 2 * kv :])
    b.fs[...] = b.fa[dm.rows : dm.rows + 1, : 2 * LANES]
    for k in range(1, PLANE):
        origin = (p + PLANE - k) % PLANE
        for (start, width), final in zip(dm.parts, (b.rF0, b.rF1)):
            arrived(b.fgu.at[origin, :, :, pl.ds(start, width)], final.at[origin])
    for where in range(CHIPS):
        first_copy(where, b.oP, b.oR1, b.osem, b.rO1).wait_send()
        first_copy(where, b.dP, b.dR1, b.dsem, b.rD1).wait_send()
    for slot in range(CHIPS - 1):
        second_copy(slot, *o_route).wait_send()
        second_copy(slot, *d_route).wait_send()
    drain()


def run_layer(dm, operands):
    n, planes, rp, tok = dm.n, dm.planes, dm.rp, dm.tok
    vm = pltpu.VMEM
    sem = pltpu.SemaphoreType.DMA
    quads = planes * CHIPS
    pairs = dm.heads + dm.kv
    outs = {
        "out": jax.ShapeDtypeStruct((tok, dm.d), BF16),
        "gin": jax.ShapeDtypeStruct((tok, dm.d), BF16),
        "fq": jax.ShapeDtypeStruct((dm.rows * dm.heads // LANES, LANES), F32),
        "fk": jax.ShapeDtypeStruct((dm.rows, LANES), F32),
        "fv": jax.ShapeDtypeStruct((dm.rows, LANES), F32),
        "fo": jax.ShapeDtypeStruct((dm.rows * dm.d // LANES, LANES), F32),
        "fs": jax.ShapeDtypeStruct((1, 2 * LANES), F32),
        "fgu": jax.ShapeDtypeStruct((PLANE, 2, rp, dm.ffr), BF16),
        "fd": jax.ShapeDtypeStruct((dm.rf * dm.d // LANES, LANES), F32),
    }
    n_sends = 1 + (planes - 1) * 16 + 16 * PLANE + 8 * quads + 64
    scratch = {
        "W": vm((quads, 2, rp, dm.wide), BF16),
        "GU0": vm((planes * dm.groups, dm.gs, 2 * dm.parts[0][1]), BF16),
        "GU1": vm((planes * dm.groups, dm.gs, 2 * dm.parts[1][1]), BF16),
        "WD": vm((planes, dm.rfp, dm.d), BF16),
        "nfA": vm((PLANE, tok, dm.d), BF16),
        "gA": vm((PLANE, tok, dm.d), BF16),
        "act": vm((PLANE * tok // rp, rp, dm.ffr), BF16),
        "BIG": vm((quads, 2, rp, 4 * dm.ffr), BF16),
        "oP": vm((CHIPS, 2, tok, dm.d), BF16),
        "dP": vm((CHIPS, 2, tok, dm.d), BF16),
        "oR1": vm((CHIPS, tok, dm.d), BF16),
        "dR1": vm((CHIPS, tok, dm.d), BF16),
        "oR2": vm((CHIPS - 1, tok, dm.d), BF16),
        "dR2": vm((CHIPS - 1, tok, dm.d), BF16),
        "zR0": vm((planes + 1, dm.groups, dm.gs, 2 * dm.parts[0][1]), BF16),
        "zR1": vm((planes + 1, dm.groups, dm.gs, 2 * dm.parts[1][1]), BF16),
        "zD": vm((planes + 1, dm.rfp, dm.d), BF16),
        "aR1": vm((quads, rp, dm.wide), BF16),
        "aR2": vm((CHIPS - 1, planes, rp, dm.wide), BF16),
        "aR3": vm((planes + 1, rp, dm.wide), BF16),
        "QS": vm((dm.micro, HEADS * dm.slots, LANES), BF16),
        "PF": vm((dm.micro, HEADS * dm.slots, dm.slots), F32),
        "hid": vm((tok, dm.d), F32),
        "fa": vm((rp, dm.wide), F32),
        "dhid": vm((tok, dm.d), F32),
        "npad": vm((tok, dm.dp), BF16),
        "mpad": vm((tok, dm.dp), BF16),
        "spr": vm((dm.d, dm.dp), BF16),
        "kd": vm((KV_HEADS, tok, LANES), BF16),
        "vd": vm((KV_HEADS, tok, LANES), BF16),
        "FQ": vm((tok, pairs), F32),
        "tabs": vm((2, tok, LANES), F32),
        "vec": vm((8, dm.d), F32),
        "ssem": sem((n_sends,)),
        "csem": sem((4,)),
        "osem": sem((CHIPS,)),
        "dsem": sem((CHIPS,)),
        "osem2": sem((CHIPS - 1,)),
        "dsem2": sem((CHIPS - 1,)),
        "rA": sem((n,)),
        "rGU": sem((PLANE,)),
        "rGZ0": sem((planes,)),
        "rGZ1": sem((planes,)),
        "rG": sem((PLANE,)),
        "rWD": sem((planes,)),
        "rNF": sem((PLANE,)),
        "rO1": sem((CHIPS,)),
        "rD1": sem((CHIPS,)),
        "rO2": sem((CHIPS - 1,)),
        "rD2": sem((CHIPS - 1,)),
        "rZ0": sem((planes + 1,)),
        "rZ1": sem((planes + 1,)),
        "rF0": sem((PLANE,)),
        "rF1": sem((PLANE,)),
        "rW": sem((planes + 1,)),
        "rA1": sem((planes,)),
        "rA2": sem((CHIPS - 1, planes)),
        "rA3": sem((planes + 1,)),
    }
    return pl.pallas_call(
        functools.partial(layer_kernel, dm, (*operands, *outs, *scratch)),
        name="layer",
        out_shape=list(outs.values()),
        in_specs=[pl.BlockSpec(memory_space=pltpu.VMEM)] * len(operands),
        out_specs=[pl.BlockSpec(memory_space=pltpu.VMEM)] * len(outs),
        scratch_shapes=list(scratch.values()),
        compiler_params=pltpu.CompilerParams(
            collective_id=0, has_side_effects=True, vmem_limit_bytes=67043328
        ),
    )(*operands.values())


def per_device(n, *args):
    (
        tokens,
        positions,
        cotangent,
        norm_attn,
        w_query,
        b_query,
        w_key,
        b_key,
        w_value,
        b_value,
        w_out,
        norm_ffn,
        w_gate,
        w_up,
        w_down,
    ) = args
    micro, slots, d = tokens.shape
    dm = Dims(n, d, w_gate.shape[0] * n // d, slots, micro)
    rows, rp = dm.rows, dm.rp

    def lanes(vector):
        return jnp.pad(vector, (0, FIELD - vector.shape[0]))

    spare = jnp.concatenate([lanes(v) for v in (norm_attn, b_query, norm_ffn, b_value)])
    spare = jnp.pad(spare, (0, dm.wide - spare.shape[0]))
    pack = jnp.concatenate(
        [w.reshape(rows, -1) for w in (w_query, w_key, w_value, w_out)], axis=1
    )
    pack = jnp.concatenate([pack, spare[None]], axis=0)
    pack = jnp.pad(pack, ((0, rp - rows - 1), (0, 0)))

    def columns(weight):
        weight = weight.reshape(rows, dm.planes, PLANE, dm.rf)
        weight = jnp.pad(weight, ((0, rp - rows), (0, 0), (0, 0), (0, dm.rfp - dm.rf)))
        return weight.transpose(2, 0, 1, 3).reshape(PLANE, rp, dm.ffr)

    both = jnp.stack([columns(w_gate), columns(w_up)], axis=1)
    down = jnp.pad(w_down.reshape(dm.rf, d), ((0, dm.rfp - dm.rf), (0, 0)))
    operands = {
        "x": tokens.reshape(dm.tok, d),
        "g": cotangent.reshape(dm.tok, d),
        "posr": positions,
        "bkey": b_key[None],
        "ap": pack,
        "gus": both,
        "wds": down,
    }
    out, gin, fq, fk, fv, fo, fs, fgu, fd = run_layer(dm, operands)

    def field(i, size):
        return fs[0, i * FIELD : i * FIELD + size]

    def gate_part(i):
        part = fgu[:, i, :rows].astype(F32)
        part = part.reshape(PLANE, rows, dm.planes, dm.rfp)[..., : dm.rf]
        return part.transpose(1, 2, 0, 3).reshape(-1)

    return (
        out.reshape(micro, slots, d),
        gin.reshape(micro, slots, d),
        field(0, rows),
        fq.reshape(-1),
        field(1, rows),
        fk.reshape(-1),
        fs[0, LANES : LANES + dm.kv],
        fv.reshape(-1),
        field(3, dm.rv),
        fo.reshape(-1),
        field(2, rows),
        gate_part(0),
        gate_part(1),
        fd.reshape(-1),
    )


def solution(mesh):
    n = mesh.shape["dp"]
    split, row = P("dp"), P(None, "dp", None)
    in_specs = (row, P(None, "dp"), row, *[split] * 4, P(), *[split] * 7)
    out_specs = (row, row, *[split] * 4, P(), *[split] * 7)
    return jax.shard_map(
        functools.partial(per_device, n),
        mesh=mesh,
        in_specs=in_specs,
        out_specs=out_specs,
        check_vma=False,
    )
```

```python
import functools
import math

import jax
import jax.numpy as jnp
from jax import lax
from jax.experimental import pallas as pl
from jax.experimental.pallas import tpu as pltpu
from jax.sharding import PartitionSpec as P

HEADS = 14
KV_HEADS = 2
HEAD_DIM = 64
GROUP = HEADS // KV_HEADS
PLANE = 8
CHIPS = 4
LANES = 128
ROTARY_LOG = math.log(1000000.0)
FIELD = 32
MESH = pl.DeviceIdType.MESH
F32 = jnp.float32
BF16 = jnp.bfloat16


def up(value, step):
    return -(-value // step) * step


def mm(left, right, dims=((1,), (0,))):
    return lax.dot_general(left, right, (dims, ((), ())), preferred_element_type=F32)


def mm_nt(left, right):
    return mm(left, right, ((1,), (1,)))


def mm_tn(left, right):
    return mm(left, right, ((0,), (0,)))


def split_mm(left, right, nt=False):
    high = left.astype(BF16)
    low = (left - high.astype(F32)).astype(BF16)
    dot = mm_nt if nt else mm
    return dot(high, right) + dot(low, right)


def iota(shape, dim):
    return lax.broadcasted_iota(jnp.int32, shape, dim)


class Dims:
    def __init__(self, n, d, ff, slots, micro):
        self.n, self.d, self.ff = n, d, ff
        self.planes = n // PLANE
        self.rows = d // n
        self.rp = 8
        while self.rp < self.rows + 1:
            self.rp *= 2
        self.dp = n * self.rp
        self.rf = ff // n
        self.ffr = up(ff // PLANE, LANES)
        self.rfp = self.ffr // self.planes
        self.slots, self.micro = slots, micro
        self.tok = slots * micro
        self.heads = HEADS * HEAD_DIM
        self.kv = KV_HEADS * HEAD_DIM
        self.qkv = self.heads + 2 * self.kv
        self.wide = self.qkv + d
        self.rv = self.kv // n
        self.unit = PLANE * self.rows
        self.gs = 16 if self.unit % 16 == 0 else 8
        self.groups = self.unit // self.gs
        blocks = self.ffr // LANES
        first = blocks // 2 * LANES
        self.parts = ((0, first), (first, self.ffr - first))


def spread_matrix(dm):
    shape = (dm.d, dm.dp)
    row, col = iota(shape, 0), iota(shape, 1)
    inner = col & (dm.rp - 1)
    hit = (row == (col // dm.rp) * dm.rows + inner) & (inner < dm.rows)
    return jnp.where(hit, 1.0, 0.0).astype(BF16)


def field_matrix(dm, offset):
    shape = (LANES, dm.dp)
    row, col = iota(shape, 0), iota(shape, 1)
    inner = col & (dm.rp - 1)
    return jnp.where((row == offset + inner) & (inner < dm.rows), 1.0, 0.0).astype(BF16)


def own_block(dm):
    shape = (dm.n, dm.dp)
    return iota(shape, 1) // dm.rp == iota(shape, 0)


def spare_rows(dm):
    shape = (dm.n, dm.dp)
    return jnp.where(iota(shape, 1) == iota(shape, 0) * dm.rp + dm.rows, 1.0, 0.0).astype(BF16)


def value_field(dm):
    shape = (LANES, LANES)
    return jnp.where(
        iota(shape, 0) == 3 * FIELD + (iota(shape, 1) & (dm.rv - 1)), 1.0, 0.0
    ).astype(BF16)


def value_block(dm):
    shape = (dm.n, LANES)
    return iota(shape, 1) // dm.rv == iota(shape, 0)


def half_turn(field):
    width = field.shape[-1]
    first = (iota(field.shape, 1) & (HEAD_DIM - 1)) < HEAD_DIM // 2
    ahead = pltpu.roll(field, width - HEAD_DIM // 2, 1)
    behind = pltpu.roll(field, HEAD_DIM // 2, 1)
    return first, ahead, behind


def twice(field):
    low = iota(field.shape, 1) < HEAD_DIM
    turned = pltpu.roll(field, HEAD_DIM, 1)
    return jnp.where(low, field, turned), jnp.where(low, turned, field)


class Refs:
    def __init__(self, names, refs):
        self.__dict__.update(zip(names, refs, strict=True))


def layer_kernel(dm, names, *refs):
    b = Refs(names, refs)
    n, planes, rp = dm.n, dm.planes, dm.rp
    me = lax.axis_index("dp")
    r, p = me // PLANE, me % PLANE
    q, c = p // 2, p % 2
    other = 1 - c
    partner = r * PLANE + q * 2 + other

    def dev(plane, place):
        return (plane * PLANE + place,)

    barrier = pltpu.get_barrier_semaphore()
    peers = [dev(r, (p + k) % PLANE) for k in range(1, PLANE)]
    peers += [dev((r + k) % planes, p) for k in range(1, planes)]
    for peer in peers:
        pl.semaphore_signal(barrier, inc=1, device_id=peer, device_id_type=MESH)
    pl.semaphore_wait(barrier, len(peers))

    pending = []
    count = [0]

    def prepare(src, dst, arrive, to, cond=None, tag=None):
        copy = pltpu.make_async_remote_copy(
            src_ref=src,
            dst_ref=dst,
            send_sem=b.ssem.at[count[0]],
            recv_sem=arrive,
            device_id=to,
            device_id_type=MESH,
        )
        count[0] += 1
        pending.append((copy, cond, tag))
        return copy

    def send(src, dst, arrive, to, cond=None, tag=None):
        copy = prepare(src, dst, arrive, to, cond, tag)
        if cond is None:
            copy.start()
        else:
            pl.when(cond)(copy.start)

    def drain(tag=None):
        now = [item for item in pending if tag in (None, item[2])]
        for copy, cond, _ in now:
            if cond is None:
                copy.wait_send()
            else:
                pl.when(cond)(copy.wait_send)
        pending[:] = [item for item in pending if tag not in (None, item[2])]

    upper = r // max(planes // 2, 1)
    mirror = r + upper * (planes - 1 - 2 * r)

    def origin_of(k):
        spot = k - (mirror + planes - k) // planes
        return spot + upper * (planes - 1 - 2 * spot)

    def relay_own(src, dst, arrive, tag=None):
        send(src, dst, arrive, dev(r + 1, p), r + 1 < planes, tag)
        send(src, dst, arrive, dev(r - 1, p), r >= 1, tag)

    def onward(part, sems, k, tag=None):
        origin = origin_of(k)
        to = r - 1 + 2 * ((r - origin - 1 + planes) // planes)
        cond = (to >= 0) & (to < planes)
        piece, arrive = part(origin), sems.at[origin]
        return piece, arrive, cond, prepare(piece, piece, arrive, dev(to, p), cond, tag)

    def pass_on(piece, arrive, cond, copy):
        @pl.when(cond)
        def _():
            arrived(piece, arrive)
            copy.start()

    def settle(piece, arrive, cond, copy):
        pl.when(jnp.logical_not(cond))(lambda: arrived(piece, arrive))

    def arrived(dst, arrive):
        pltpu.make_async_remote_copy(
            src_ref=dst,
            dst_ref=dst,
            send_sem=b.ssem.at[0],
            recv_sem=arrive,
            device_id=(partner,),
            device_id_type=MESH,
        ).wait_recv()

    def block(ref, index):
        return ref.at[index // 2, index % 2]

    def plane_rows(ref, plane):
        return ref.at[pl.ds(plane * dm.groups, dm.groups)]

    keep = [
        pltpu.make_async_copy(b.ap, block(b.W, me), b.csem.at[0]),
        pltpu.make_async_copy(b.gus.at[p], b.fgu.at[p], b.csem.at[1]),
        pltpu.make_async_copy(b.g, b.gA.at[p], b.csem.at[2]),
        pltpu.make_async_copy(b.wds, b.WD.at[r], b.csem.at[3]),
    ]
    for copy in keep:
        copy.start()

    relay_own(b.ap, block(b.W, me), b.rA.at[me])

    across, along = q + 1 - 2 * (q % 2), (q + 2) % CHIPS
    near = across * other + along * c
    next_to = along * other + across * c
    spots = (near, next_to, CHIPS - 1 - q)

    def fan(index, src):
        for where in (next_to, near):
            send(src, block(b.W, index), b.rA.at[index], dev(r, where * 2 + c))

    def spread_out(src, ref, arrive):
        for where in (next_to, near):
            send(src, ref.at[p], arrive.at[p], dev(r, where * 2 + c))
        send(src, ref.at[p], arrive.at[p], (partner,))

    def hand_on(ref, arrive, where):
        place = where * 2 + c
        arrived(ref.at[place], arrive.at[place])
        if where is near:
            send(ref.at[place], ref.at[place], arrive.at[place], dev(r, next_to * 2 + c))
        send(ref.at[place], ref.at[place], arrive.at[place], (partner,))

    fan(me, b.ap)
    send(b.ap, block(b.W, me), b.rA.at[me], (partner,))
    for k in range(1, PLANE):
        send(b.gus.at[(p + k) % PLANE], b.fgu.at[p], b.rGU.at[p], dev(r, (p + k) % PLANE))
    relay_own(b.wds, b.WD.at[r], b.rWD.at[r])

    tok = dm.tok
    xf = b.x[...].astype(F32)
    scale1 = lax.rsqrt(jnp.mean(xf * xf, axis=-1, keepdims=True) + 1e-06)
    diagonal = iota((dm.slots, dm.slots), 0) == iota((dm.slots, dm.slots), 1)
    posc = [
        jnp.sum(jnp.where(diagonal, b.posr[m : m + 1].astype(F32), 0.0), axis=1, keepdims=True)
        for m in range(dm.micro)
    ]
    power = (iota((1, LANES), 1) & (HEAD_DIM // 2 - 1)).astype(F32) * (-2.0 / HEAD_DIM * ROTARY_LOG)
    angle = jnp.concatenate(posc, axis=0) * jnp.exp(power)
    b.tabs[0] = jnp.cos(angle)
    b.tabs[1] = jnp.sin(angle)
    b.spr[...] = spread_matrix(dm)

    for k in range(1, planes):
        origin = origin_of(k)
        index = origin * PLANE + p
        arrived(block(b.W, index), b.rA.at[index])
        to = r - 1 + 2 * ((r - origin - 1 + planes) // planes)
        send(block(b.W, index), block(b.W, index), b.rA.at[index], dev(to, p), (to >= 0) & (to < planes))
        fan(index, block(b.W, index))
        send(block(b.W, index), block(b.W, index), b.rA.at[index], (partner,))
    for k in range(1, PLANE):
        origin = (p + PLANE - k) % PLANE
        arrived(b.fgu.at[origin], b.rGU.at[origin])
    keep[1].wait()
    GU = [ref.reshape(dm.d, ref.shape[-1]) for ref in (b.GU0, b.GU1)]
    my_rows = pl.ds(pl.multiple_of(r * dm.unit, dm.gs), dm.unit)
    squeeze = b.spr[: dm.unit, : PLANE * rp]
    for h, (start, width) in enumerate(dm.parts):
        for i in range(2):
            piece = b.fgu[:, i, :, start : start + width].reshape(PLANE * rp, width)
            GU[h][my_rows, i * width : (i + 1) * width] = mm(squeeze, piece).astype(BF16)

    def gate_part(h):
        ref = (b.GU0, b.GU1)[h]
        return lambda plane: plane_rows(ref, plane)

    def down_part(plane):
        return b.WD.at[plane]

    relay_own(gate_part(0)(r), gate_part(0)(r), b.rGZ0.at[r], "gate0")
    steps = range(1, planes)
    down_on = [onward(down_part, b.rWD, k, "down") for k in steps]
    gate_on = [[onward(gate_part(h), sems, k, f"gate{h}") for k in steps] for h, sems in ((0, b.rGZ0), (1, b.rGZ1))]
    pass_on(*down_on[0])
    origins = [r, *(origin_of(k) for k in steps)]
    for i, where in enumerate(spots):
        for origin in origins:
            index = origin * PLANE + where * 2 + c
            arrived(block(b.W, index), b.rA.at[index])
            if i == 0:
                send(block(b.W, index), block(b.W, index), b.rA.at[index], dev(r, next_to * 2 + c))
            send(block(b.W, index), block(b.W, index), b.rA.at[index], (partner,))
    spread_out(b.g, b.gA, b.rG)
    for item in down_on[1:]:
        pass_on(*item)

    keep[0].wait()
    for k in range(CHIPS):
        for shift in range(planes):
            index = ((r + planes - shift) % planes) * PLANE + ((q + CHIPS - k) % CHIPS) * 2 + other
            arrived(block(b.W, index), b.rA.at[index])

    W = b.W.reshape(dm.dp, dm.wide)
    small = mm(spare_rows(dm), W[:, :LANES]).astype(BF16)
    mine = own_block(dm)
    rows8 = iota((8, dm.dp), 0)
    padded = jnp.zeros((8, dm.dp), F32)
    for i in range(3):
        piece = mm(small, field_matrix(dm, i * FIELD))
        piece = jnp.sum(jnp.where(mine, piece, 0.0), axis=0, keepdims=True)
        padded = jnp.where(rows8 == i, piece, padded)
    b.vec[...] = mm_nt(padded.astype(BF16), b.spr[...])
    gain1, bias_q, gain2 = b.vec[0:1], b.vec[1:2], b.vec[2:3]
    bias_v = jnp.sum(
        jnp.where(value_block(dm), mm(small, value_field(dm)), 0.0), axis=0, keepdims=True
    )
    bias_k = b.bkey[...].astype(F32)

    normed = (xf * scale1 * gain1).astype(BF16)
    b.npad[...] = mm(normed, b.spr[...]).astype(BF16)
    lin = mm(b.npad[...], W[:, : dm.qkv])
    turn_in = jnp.concatenate([lin[:, : dm.heads] + bias_q, lin[:, dm.heads : dm.heads + dm.kv] + bias_k], axis=1)
    reps = (dm.heads + dm.kv) // LANES
    cosine = jnp.concatenate([b.tabs[0]] * reps, axis=1)
    sine = jnp.concatenate([b.tabs[1]] * reps, axis=1)
    first, ahead, behind = half_turn(turn_in)
    turned = turn_in * cosine + jnp.where(first, -ahead, behind) * sine
    values = lin[:, dm.heads + dm.kv :] + bias_v
    for i, piece in enumerate(twice(turned[:, dm.heads :])):
        b.kd[i] = piece.astype(BF16)
    for i, piece in enumerate(twice(values)):
        b.vd[i] = piece.astype(BF16)
    low = iota((dm.slots, LANES), 1) < HEAD_DIM

    def stack_heads(field, store):
        for h in range(HEADS):
            part = field[:, LANES * (h // 2) : LANES * (h // 2) + LANES]
            part = jnp.where(low if h % 2 == 0 else ~low, part, 0.0)
            store(h)[...] = part.astype(BF16)

    span = GROUP * dm.slots
    mix = b.oP.at[0, 0]
    BIG = b.BIG.reshape(dm.dp, 4 * dm.ffr)
    dms = [BIG.at[:span, dm.wide + kv * LANES : dm.wide + (kv + 1) * LANES] for kv in range(KV_HEADS)]

    def head_rows(h):
        return dms[h // GROUP].at[(h % GROUP) * dm.slots : (h % GROUP + 1) * dm.slots]

    for m in range(dm.micro):
        here = slice(m * dm.slots, (m + 1) * dm.slots)
        stack_heads(turned[here, : dm.heads], lambda h: b.QS.at[m, h * dm.slots : (h + 1) * dm.slots])
        grid = (dm.slots, dm.slots)
        start_row = iota((dm.slots, 1), 0).astype(F32) - posc[m]
        start_col = (iota((1, dm.slots), 1) - b.posr[m : m + 1]).astype(F32)
        allowed = (start_row == start_col) & (iota(grid, 1) <= iota(grid, 0))
        for kv in range(KV_HEADS):
            rows = slice(kv * span, (kv + 1) * span)
            score = mm_nt(b.QS[m, rows], b.kd[kv, here]) * 0.125
            score = jnp.where(allowed[None], score.reshape(GROUP, *grid), -1e30)
            top = jnp.max(score, axis=-1, keepdims=True)
            expo = jnp.exp(score - top)
            prob = expo / jnp.sum(expo, axis=-1, keepdims=True)
            prob = prob.reshape(span, dm.slots)
            b.PF[m, rows] = prob
            dms[kv][...] = mm(prob.astype(BF16), b.vd[kv, here]).astype(BF16)
        for t in range(HEADS // 2):
            even, odd = head_rows(2 * t)[...], head_rows(2 * t + 1)[...]
            mix[here, t * LANES : (t + 1) * LANES] = jnp.where(low, even, odd)
    b.mpad[...] = mm(mix[...], b.spr[...]).astype(BF16)
    hidden = xf + mm(b.mpad[...], W[:, dm.qkv :])
    b.hid[...] = hidden
    scale2 = lax.rsqrt(jnp.mean(hidden * hidden, axis=-1, keepdims=True) + 1e-06)
    nf = (hidden * scale2 * gain2).astype(BF16)
    b.nfA[p] = nf

    spread_out(b.nfA.at[p], b.nfA, b.rNF)
    pass_on(*gate_on[0][0])
    hand_on(b.gA, b.rG, near)
    for item in gate_on[0][1:]:
        pass_on(*item)
    relay_own(gate_part(1)(r), gate_part(1)(r), b.rGZ1.at[r], "gate1")
    hand_on(b.nfA, b.rNF, near)
    pass_on(*gate_on[1][0])
    for where in spots[1:]:
        hand_on(b.gA, b.rG, where)
    for where in spots[1:]:
        hand_on(b.nfA, b.rNF, where)
    for item in gate_on[1][1:]:
        pass_on(*item)
    for item in (*down_on, *gate_on[0]):
        settle(*item)
    keep[2].wait()
    keep[3].wait()
    for k in range(CHIPS):
        place = ((q + CHIPS - k) % CHIPS) * 2 + other
        arrived(b.gA.at[place], b.rG.at[place])
        arrived(b.nfA.at[place], b.rNF.at[place])

    ACT = b.act.reshape(PLANE * tok, dm.ffr)
    WD = b.WD.reshape(dm.ffr, dm.d)
    half = PLANE // 2

    base = (0, 4 * dm.parts[0][1])

    def feed(h, place_q, place_c):
        place = place_q * 2 + place_c
        start, width = dm.parts[h]
        nf_t, g_t = b.nfA[place], b.gA[place]
        down = WD[start : start + width]
        pre = mm(nf_t, GU[h][...])
        gate, upper = pre[:, :width], pre[:, width:]
        sigma = jax.nn.sigmoid(gate)
        silu = gate * sigma
        act = (silu * upper).astype(BF16)
        ACT[pl.ds(pl.multiple_of(place * tok, tok), tok), start : start + width] = act
        d_act = mm_nt(g_t, down)
        d_gate = (d_act * upper * (sigma + silu * (1.0 - sigma))).astype(BF16)
        d_up = (d_act * silu).astype(BF16)
        d_both = jnp.concatenate([d_gate, d_up], axis=1)
        rows = pl.ds(pl.multiple_of((place % half) * tok, tok), tok)
        cols = pl.ds(pl.multiple_of(base[h] + (place // half) * 2 * width, LANES), 2 * width)
        BIG[rows, cols] = d_both
        for ref, value in ((b.oP, mm(act, down)), (b.dP, mm_nt(d_both, GU[h][...]))):
            if h:
                value = value + ref[place_q, place_c].astype(F32)
            ref[place_q, place_c] = value.astype(BF16)

    def first_copy(where, part, landing, sems, arrive):
        return pltpu.make_async_remote_copy(
            src_ref=part.at[where, other],
            dst_ref=landing.at[where],
            send_sem=sems.at[where],
            recv_sem=arrive.at[where],
            device_id=(partner,),
            device_id_type=MESH,
        )

    diag = CHIPS - 1 - q
    routes = ((diag, near), (near, near), (next_to, next_to))

    def second_copy(slot, part, landing, sems, arrive):
        source, to = routes[slot]
        return pltpu.make_async_remote_copy(
            src_ref=part.at[source, c],
            dst_ref=landing.at[slot],
            send_sem=sems.at[slot],
            recv_sem=arrive.at[slot],
            device_id=dev(r, to * 2 + c),
            device_id_type=MESH,
        )

    def add_on(part, landing, sems, arrive):
        arrived(landing.at[0], arrive.at[0])
        part[next_to, c] = (part[next_to, c].astype(F32) + landing[0].astype(F32)).astype(BF16)
        second_copy(2, part, landing, sems, arrive).start()

    d_route = (b.dP, b.dR2, b.dsem2, b.rD2)
    o_route = (b.oP, b.oR2, b.osem2, b.rO2)

    def hop(part, landing, arrive, to, cond):
        ahead = (to - r - 1 + planes) // planes
        beyond = r - to - 1 + 2 * planes * ahead
        last = 1 - (beyond + 4 * planes - 1) // (4 * planes)
        slot = to + (planes - to) * last
        send(part(to), landing.at[slot], arrive.at[slot], dev(r - 1 + 2 * ahead, p), cond)

    def behind_of(to):
        ahead = (to - r - 1 + planes) // planes
        follows = r + 1 - 2 * ahead
        return (follows >= 0) & (follows < planes)

    far = [origin_of(planes - k) for k in range(1, planes)]

    def chain_start(part, landing, arrive):
        for to in far:
            hop(part, landing, arrive, to, jnp.logical_not(behind_of(to)))

    def chain_step(part, landing, arrive, k):
        to = far[k]
        has = behind_of(to)

        @pl.when(has)
        def _():
            arrived(landing.at[to], arrive.at[to])
            mine = part(to)
            mine[...] = (mine[...].astype(F32) + landing[to].astype(F32)).astype(BF16)

        hop(part, landing, arrive, to, has)

    def chain_end(total, landing, arrive):
        for slot, cond in ((r, r >= 1), (planes, r + 1 < planes)):

            @pl.when(cond)
            def _():
                arrived(landing.at[slot], arrive.at[slot])
                total[...] = (total[...].astype(F32) + landing[slot].astype(F32)).astype(total.dtype)

    nf_all = b.nfA.reshape(PLANE * tok, dm.d)
    g_all = b.gA.reshape(PLANE * tok, dm.d)
    wide_rows = half * tok
    chunk = 2 * LANES

    def gate_grad(h):
        width = dm.parts[h][1]

        def some(start, count):
            cols = pl.ds(start, count)
            total = mm_tn(nf_all[:wide_rows, cols], BIG[:, base[h] : base[h] + 2 * width])
            total = total + mm_tn(nf_all[wide_rows:, cols], BIG[:, base[h] + 2 * width : base[h] + 4 * width])
            GU[h][cols, :] = total.astype(BF16)

        @pl.loop(0, dm.d // chunk)
        def _(i):
            some(pl.multiple_of(i * chunk, chunk), chunk)

        if dm.d % chunk:
            some(dm.d - dm.d % chunk, dm.d % chunk)

    @pl.loop(0, PLANE)
    def _(turn):
        feed(0, turn // 2, turn % 2)

    drain("gate0")
    gate_grad(0)
    chain_start(gate_part(0), b.zR0, b.rZ0)
    for item in gate_on[1]:
        settle(*item)

    def join(where):
        for part, one, arrive in ((b.dP, b.dR1, b.rD1), (b.oP, b.oR1, b.rO1)):
            arrived(one.at[where], arrive.at[where])
            part[where, c] = (part[where, c].astype(F32) + one[where].astype(F32)).astype(BF16)

    @pl.loop(0, CHIPS)
    def _(step):
        one, two = (CHIPS - 1 - step) % 2, (CHIPS - 1 - step) // 2
        over_x, over_y = one * other + two * c, two * other + one * c
        where = 2 * ((q // 2 + over_y) % 2) + (q % 2 + over_x) % 2

        @pl.loop(0, 2)
        def _(turn):
            feed(1, where, (other + turn) % 2)

            @pl.when(turn == 0)
            def _():
                first_copy(where, b.dP, b.dR1, b.dsem, b.rD1).start()
                first_copy(where, b.oP, b.oR1, b.osem, b.rO1).start()

        for at, source in ((1, diag), (2, near)):

            @pl.when(step == at)
            def _():
                join(source)
                second_copy(at - 1, *d_route).start()

    join(next_to)
    add_on(*d_route)
    for slot in range(2):
        second_copy(slot, *o_route).start()
    join(q)

    def attn_part(plane):
        return b.aR2.at[0, plane]

    drain("down")
    WD[...] = mm_tn(ACT[...], g_all[...]).astype(BF16)
    chain_start(down_part, b.zD, b.rW)
    drain("gate1")
    gate_grad(1)
    chain_start(gate_part(1), b.zR1, b.rZ1)
    for k in range(planes - 1):
        chain_step(gate_part(0), b.zR0, b.rZ0, k)
    add_on(*o_route)
    d_nf = b.dP[q, c].astype(F32)
    for slot in (1, 2):
        arrived(b.dR2.at[slot], b.rD2.at[slot])
        d_nf = d_nf + b.dR2[slot].astype(F32)
    hidden = b.hid[...]
    scale2 = lax.rsqrt(jnp.mean(hidden * hidden, axis=-1, keepdims=True) + 1e-06)

    def norm_back(grad, field, scale, gain):
        weighted = grad * gain
        d_gain = jnp.sum(grad * field * scale, axis=0, keepdims=True)
        d_field = weighted * scale - field * (scale * scale * scale) * jnp.mean(
            weighted * field, axis=-1, keepdims=True
        )
        return d_gain, d_field

    d_gain2, d_part = norm_back(d_nf, hidden, scale2, b.vec[2:3])
    d_hidden = b.g[...].astype(F32) + d_part
    b.dhid[...] = d_hidden
    d_attn = d_hidden.astype(BF16)
    chain_step(down_part, b.zD, b.rW, 0)
    BIG[:, dm.qkv : dm.wide] = mm_tn(b.mpad[...], d_attn).astype(BF16)
    d_mixed = mm_nt(d_attn, W[:, dm.qkv :]).astype(BF16)
    d_mixed = mm_nt(d_mixed, b.spr[...])
    d_values = []
    for m in range(dm.micro):
        here = slice(m * dm.slots, (m + 1) * dm.slots)
        stack_heads(d_mixed[here], head_rows)
        d_v, d_k = [], []
        for kv in range(KV_HEADS):
            rows = slice(kv * span, (kv + 1) * span)
            d_mix, prob, qs = dms[kv][...], b.PF[m, rows], b.QS[m, rows]
            d_v.append(mm_tn(prob.astype(BF16), d_mix))
            d_prob = mm_nt(d_mix, b.vd[kv, here])
            delta = jnp.sum(d_prob * prob, axis=-1, keepdims=True)
            d_score = (prob * (d_prob - delta)).astype(BF16)
            d_k.append(0.125 * mm_tn(d_score, qs))
            b.PF[m, rows] = 0.125 * mm(d_score, b.kd[kv, here])
        for t in range(HEADS // 2):
            even = b.PF[m, 2 * t * dm.slots : (2 * t + 1) * dm.slots]
            odd = b.PF[m, (2 * t + 1) * dm.slots : (2 * t + 2) * dm.slots]
            b.FQ[here, t * LANES : (t + 1) * LANES] = jnp.where(low, even, odd)

        def joined(pair):
            zero, one = (piece + pltpu.roll(piece, HEAD_DIM, 1) for piece in pair)
            return jnp.where(low, zero, one)

        b.FQ[here, dm.heads : dm.heads + dm.kv] = joined(d_k)
        d_values.append(joined(d_v))
    d_turned = b.FQ[...]
    cosine = jnp.concatenate([b.tabs[0]] * reps, axis=1)
    sine = jnp.concatenate([b.tabs[1]] * reps, axis=1)
    first, ahead, behind = half_turn(d_turned * sine)
    d_lin = (d_turned * cosine + jnp.where(first, ahead, -behind)).astype(BF16)
    d_lin = jnp.concatenate([d_lin, jnp.concatenate(d_values, axis=0).astype(BF16)], axis=1)
    BIG[:, : dm.qkv] = mm_tn(b.npad[...], d_lin).astype(BF16)
    d_bias = jnp.sum(d_lin.astype(F32), axis=0, keepdims=True)
    d_normed = split_mm(mm_nt(d_lin, W[:, : dm.qkv]), b.spr[...], nt=True)
    xf = b.x[...].astype(F32)
    scale1 = lax.rsqrt(jnp.mean(xf * xf, axis=-1, keepdims=True) + 1e-06)
    d_gain1, d_part = norm_back(d_normed, xf, scale1, b.vec[0:1])
    b.gin[...] = (b.dhid[...] + d_part).astype(BF16)

    rows8 = iota((8, dm.d), 0)
    packed = jnp.zeros((8, dm.d), F32)
    for i, piece in enumerate((d_gain1, d_bias[:, : dm.heads], d_gain2)):
        packed = jnp.where(rows8 == i, piece, packed)
    packed = split_mm(packed, b.spr[...])
    mine = own_block(dm)
    spare = jnp.zeros((n, LANES), F32)
    for i in range(3):
        piece = jnp.where(mine, packed[i : i + 1], 0.0).astype(BF16)
        spare = spare + mm_nt(piece, field_matrix(dm, i * FIELD))
    piece = jnp.where(value_block(dm), d_bias[:, dm.heads + dm.kv :], 0.0).astype(BF16)
    spare = spare + mm_nt(piece, value_field(dm))
    key_bias = jnp.broadcast_to(d_bias[:, dm.heads : dm.heads + dm.kv], (n, LANES))
    spare = jnp.concatenate([spare, key_bias], axis=1).astype(BF16)
    BIG[:, : 2 * LANES] = (
        BIG[:, : 2 * LANES].astype(F32) + mm_tn(spare_rows(dm), spare)
    ).astype(BF16)

    cols = pl.ds(0, dm.wide)

    def quad(plane):
        return pl.ds(plane * CHIPS, CHIPS)

    for to in (*far, r):
        send(b.BIG.at[quad(to), other, :, cols], b.aR1.at[quad(to)], b.rA1.at[to], (partner,))
    for to in (*far, r):
        arrived(b.aR1.at[quad(to)], b.rA1.at[to])
        mine_now = b.BIG[quad(to), c, :, cols].astype(F32) + b.aR1[quad(to)].astype(F32)
        b.aR1[quad(to)] = mine_now.astype(BF16)
        send(b.aR1.at[to * CHIPS + diag], b.aR2.at[0, to], b.rA2.at[0, to], dev(r, near * 2 + c))
    for to in (*far, r):
        send(b.aR1.at[to * CHIPS + near], b.aR2.at[1, to], b.rA2.at[1, to], dev(r, near * 2 + c))
    for k in range(1, planes - 1):
        chain_step(down_part, b.zD, b.rW, k)
    chain_step(gate_part(1), b.zR1, b.rZ1, 0)
    for to in (*far, r):
        arrived(b.aR2.at[0, to], b.rA2.at[0, to])
        piece = b.aR1.at[to * CHIPS + next_to]
        piece[...] = (piece[...].astype(F32) + b.aR2[0, to].astype(F32)).astype(BF16)
        send(piece, b.aR2.at[2, to], b.rA2.at[2, to], dev(r, next_to * 2 + c))
    for k in range(1, planes - 2):
        chain_step(gate_part(1), b.zR1, b.rZ1, k)
    total = b.hid[...] + b.oP[q, c].astype(F32)
    for slot in (1, 2):
        arrived(b.oR2.at[slot], b.rO2.at[slot])
        total = total + b.oR2[slot].astype(F32)
    b.out[...] = total.astype(BF16)
    for to in (*far, r):
        total = b.aR1[to * CHIPS + q].astype(F32)
        for slot in (1, 2):
            arrived(b.aR2.at[slot, to], b.rA2.at[slot, to])
            total = total + b.aR2[slot, to].astype(F32)
        b.aR2[0, to] = total.astype(BF16)
    chain_start(attn_part, b.aR3, b.rA3)
    squeeze = b.spr[: dm.unit, : PLANE * rp]

    def home(h, landing, arrive, final):
        start, width = dm.parts[h]
        cols = pl.ds(start, width)
        chain_end(gate_part(h)(r), landing, arrive)
        for i in range(2):
            piece = mm_tn(squeeze, GU[h][my_rows, i * width : (i + 1) * width]).astype(BF16)
            piece = piece.reshape(PLANE, rp, width)
            for place in range(PLANE):
                b.act[2 * place + i, :, cols] = piece[place]
        for k in range(1, PLANE):
            to = (p + k) % PLANE
            send(b.act.at[pl.ds(2 * to, 2), :, cols], b.fgu.at[p, :, :, cols], final.at[p], dev(r, to))
        b.fgu[p, :, :, cols] = b.act[pl.ds(2 * p, 2), :, cols]

    home(0, b.zR0, b.rZ0, b.rF0)
    chain_step(gate_part(1), b.zR1, b.rZ1, planes - 2)
    home(1, b.zR1, b.rZ1, b.rF1)
    for k in range(planes - 1):
        chain_step(attn_part, b.aR3, b.rA3, k)
    sums = b.hid.at[: dm.rfp]
    sums[...] = b.WD[r].astype(F32)
    chain_end(sums, b.zD, b.rW)

    def lay_flat(flat, field):
        blocks = field.shape[1] // LANES
        for j in range(blocks):
            flat[pl.ds(j, field.shape[0], stride=blocks), :] = field[:, j * LANES : (j + 1) * LANES]

    lay_flat(b.fd, sums[: dm.rf])
    for k in range(1, PLANE):
        origin = (p + PLANE - k) % PLANE
        for (start, width), final in zip(dm.parts, (b.rF0, b.rF1)):
            arrived(b.fgu.at[origin, :, :, pl.ds(start, width)], final.at[origin])
    blocks = dm.ff // LANES

    def window(i, run, start):
        plane, place = run // PLANE, run % PLANE
        at = plane * dm.rfp + start
        low = at // LANES * LANES
        top = min(low + 2 * LANES, dm.ffr)
        field = b.fgu[place, i, :, low:top].astype(F32)
        if at > low:
            field = pltpu.roll(field, top - at, 1)
        return field[:, :LANES]

    lane = iota((rp, LANES), 1)
    for i, flat in enumerate((b.fg, b.fu)):
        for j in range(blocks):
            run, start = (j * LANES) // dm.rf, (j * LANES) % dm.rf
            field = window(i, run, start)
            left = dm.rf - start
            while left < LANES:
                run += 1
                nxt = window(i, run, 0)
                field = jnp.where(lane < left, field, pltpu.roll(nxt, left, 1))
                left += dm.rf
            flat[pl.ds(j, dm.rows, stride=blocks), :] = field[: dm.rows]

    b.fa[...] = b.aR2[0, r].astype(F32)
    chain_end(b.fa, b.aR3, b.rA3)
    own_rows = b.fa[: dm.rows]
    h, kv = dm.heads, dm.kv
    lay_flat(b.fq, own_rows[:, :h])
    b.fk[...] = own_rows[:, h : h + kv]
    b.fv[...] = own_rows[:, h + kv : h + 2 * kv]
    lay_flat(b.fo, own_rows[:, h + 2 * kv :])
    b.fs[...] = b.fa[dm.rows : dm.rows + 1, : 2 * LANES]
    for where in range(CHIPS):
        first_copy(where, b.oP, b.oR1, b.osem, b.rO1).wait_send()
        first_copy(where, b.dP, b.dR1, b.dsem, b.rD1).wait_send()
    for slot in range(CHIPS - 1):
        second_copy(slot, *o_route).wait_send()
        second_copy(slot, *d_route).wait_send()
    drain()


def run_layer(dm, operands):
    n, planes, rp, tok = dm.n, dm.planes, dm.rp, dm.tok
    vm = pltpu.VMEM
    sem = pltpu.SemaphoreType.DMA
    quads = planes * CHIPS
    pairs = dm.heads + dm.kv
    outs = {
        "out": jax.ShapeDtypeStruct((tok, dm.d), BF16),
        "gin": jax.ShapeDtypeStruct((tok, dm.d), BF16),
        "fq": jax.ShapeDtypeStruct((dm.rows * dm.heads // LANES, LANES), F32),
        "fk": jax.ShapeDtypeStruct((dm.rows, LANES), F32),
        "fv": jax.ShapeDtypeStruct((dm.rows, LANES), F32),
        "fo": jax.ShapeDtypeStruct((dm.rows * dm.d // LANES, LANES), F32),
        "fs": jax.ShapeDtypeStruct((1, 2 * LANES), F32),
        "fg": jax.ShapeDtypeStruct((dm.rows * dm.ff // LANES, LANES), F32),
        "fu": jax.ShapeDtypeStruct((dm.rows * dm.ff // LANES, LANES), F32),
        "fd": jax.ShapeDtypeStruct((dm.rf * dm.d // LANES, LANES), F32),
    }
    n_sends = 1 + (planes - 1) * 16 + 16 * PLANE + 8 * quads + 64
    scratch = {
        "W": vm((quads, 2, rp, dm.wide), BF16),
        "GU0": vm((planes * dm.groups, dm.gs, 2 * dm.parts[0][1]), BF16),
        "GU1": vm((planes * dm.groups, dm.gs, 2 * dm.parts[1][1]), BF16),
        "WD": vm((planes, dm.rfp, dm.d), BF16),
        "nfA": vm((PLANE, tok, dm.d), BF16),
        "gA": vm((PLANE, tok, dm.d), BF16),
        "act": vm((PLANE * tok // rp, rp, dm.ffr), BF16),
        "BIG": vm((quads, 2, rp, 4 * dm.ffr), BF16),
        "oP": vm((CHIPS, 2, tok, dm.d), BF16),
        "dP": vm((CHIPS, 2, tok, dm.d), BF16),
        "oR1": vm((CHIPS, tok, dm.d), BF16),
        "dR1": vm((CHIPS, tok, dm.d), BF16),
        "oR2": vm((CHIPS - 1, tok, dm.d), BF16),
        "dR2": vm((CHIPS - 1, tok, dm.d), BF16),
        "zR0": vm((planes + 1, dm.groups, dm.gs, 2 * dm.parts[0][1]), BF16),
        "zR1": vm((planes + 1, dm.groups, dm.gs, 2 * dm.parts[1][1]), BF16),
        "zD": vm((planes + 1, dm.rfp, dm.d), BF16),
        "aR1": vm((quads, rp, dm.wide), BF16),
        "aR2": vm((CHIPS - 1, planes, rp, dm.wide), BF16),
        "aR3": vm((planes + 1, rp, dm.wide), BF16),
        "QS": vm((dm.micro, HEADS * dm.slots, LANES), BF16),
        "PF": vm((dm.micro, HEADS * dm.slots, dm.slots), F32),
        "hid": vm((tok, dm.d), F32),
        "fa": vm((rp, dm.wide), F32),
        "fgu": vm((PLANE, 2, rp, dm.ffr), BF16),
        "dhid": vm((tok, dm.d), F32),
        "npad": vm((tok, dm.dp), BF16),
        "mpad": vm((tok, dm.dp), BF16),
        "spr": vm((dm.d, dm.dp), BF16),
        "kd": vm((KV_HEADS, tok, LANES), BF16),
        "vd": vm((KV_HEADS, tok, LANES), BF16),
        "FQ": vm((tok, pairs), F32),
        "tabs": vm((2, tok, LANES), F32),
        "vec": vm((8, dm.d), F32),
        "ssem": sem((n_sends,)),
        "csem": sem((4,)),
        "osem": sem((CHIPS,)),
        "dsem": sem((CHIPS,)),
        "osem2": sem((CHIPS - 1,)),
        "dsem2": sem((CHIPS - 1,)),
        "rA": sem((n,)),
        "rGU": sem((PLANE,)),
        "rGZ0": sem((planes,)),
        "rGZ1": sem((planes,)),
        "rG": sem((PLANE,)),
        "rWD": sem((planes,)),
        "rNF": sem((PLANE,)),
        "rO1": sem((CHIPS,)),
        "rD1": sem((CHIPS,)),
        "rO2": sem((CHIPS - 1,)),
        "rD2": sem((CHIPS - 1,)),
        "rZ0": sem((planes + 1,)),
        "rZ1": sem((planes + 1,)),
        "rF0": sem((PLANE,)),
        "rF1": sem((PLANE,)),
        "rW": sem((planes + 1,)),
        "rA1": sem((planes,)),
        "rA2": sem((CHIPS - 1, planes)),
        "rA3": sem((planes + 1,)),
    }
    return pl.pallas_call(
        functools.partial(layer_kernel, dm, (*operands, *outs, *scratch)),
        name="layer",
        out_shape=list(outs.values()),
        in_specs=[pl.BlockSpec(memory_space=pltpu.VMEM)] * len(operands),
        out_specs=[pl.BlockSpec(memory_space=pltpu.VMEM)] * len(outs),
        scratch_shapes=list(scratch.values()),
        compiler_params=pltpu.CompilerParams(
            collective_id=0, has_side_effects=True, vmem_limit_bytes=67043328
        ),
    )(*operands.values())


def per_device(n, *args):
    (
        tokens,
        positions,
        cotangent,
        norm_attn,
        w_query,
        b_query,
        w_key,
        b_key,
        w_value,
        b_value,
        w_out,
        norm_ffn,
        w_gate,
        w_up,
        w_down,
    ) = args
    micro, slots, d = tokens.shape
    dm = Dims(n, d, w_gate.shape[0] * n // d, slots, micro)
    rows, rp = dm.rows, dm.rp

    def lanes(vector):
        return jnp.pad(vector, (0, FIELD - vector.shape[0]))

    spare = jnp.concatenate([lanes(v) for v in (norm_attn, b_query, norm_ffn, b_value)])
    spare = jnp.pad(spare, (0, dm.wide - spare.shape[0]))
    pack = jnp.concatenate(
        [w.reshape(rows, -1) for w in (w_query, w_key, w_value, w_out)], axis=1
    )
    pack = jnp.concatenate([pack, spare[None]], axis=0)
    pack = jnp.pad(pack, ((0, rp - rows - 1), (0, 0)))

    def columns(weight):
        weight = weight.reshape(rows, dm.planes, PLANE, dm.rf)
        weight = jnp.pad(weight, ((0, rp - rows), (0, 0), (0, 0), (0, dm.rfp - dm.rf)))
        return weight.transpose(2, 0, 1, 3).reshape(PLANE, rp, dm.ffr)

    both = jnp.stack([columns(w_gate), columns(w_up)], axis=1)
    down = jnp.pad(w_down.reshape(dm.rf, d), ((0, dm.rfp - dm.rf), (0, 0)))
    operands = {
        "x": tokens.reshape(dm.tok, d),
        "g": cotangent.reshape(dm.tok, d),
        "posr": positions,
        "bkey": b_key[None],
        "ap": pack,
        "gus": both,
        "wds": down,
    }
    out, gin, fq, fk, fv, fo, fs, fg, fu, fd = run_layer(dm, operands)

    def field(i, size):
        return fs[0, i * FIELD : i * FIELD + size]

    return (
        out.reshape(micro, slots, d),
        gin.reshape(micro, slots, d),
        field(0, rows),
        fq.reshape(-1),
        field(1, rows),
        fk.reshape(-1),
        fs[0, LANES : LANES + dm.kv],
        fv.reshape(-1),
        field(3, dm.rv),
        fo.reshape(-1),
        field(2, rows),
        fg.reshape(-1),
        fu.reshape(-1),
        fd.reshape(-1),
    )


def solution(mesh):
    n = mesh.shape["dp"]
    split, row = P("dp"), P(None, "dp", None)
    in_specs = (row, P(None, "dp"), row, *[split] * 4, P(), *[split] * 7)
    out_specs = (row, row, *[split] * 4, P(), *[split] * 7)
    return jax.shard_map(
        functools.partial(per_device, n),
        mesh=mesh,
        in_specs=in_specs,
        out_specs=out_specs,
        check_vma=False,
    )
```

```python
import functools
import math

import jax
import jax.numpy as jnp
from jax import lax
from jax.experimental import pallas as pl
from jax.experimental.pallas import tpu as pltpu
from jax.sharding import PartitionSpec as P

HEADS = 14
KV_HEADS = 2
HEAD_DIM = 64
GROUP = HEADS // KV_HEADS
PLANE = 8
CHIPS = 4
LANES = 128
ROTARY_LOG = math.log(1000000.0)
FIELD = 32
MESH = pl.DeviceIdType.MESH
F32 = jnp.float32
BF16 = jnp.bfloat16


def up(value, step):
    return -(-value // step) * step


def mm(left, right, dims=((1,), (0,))):
    return lax.dot_general(left, right, (dims, ((), ())), preferred_element_type=F32)


def mm_nt(left, right):
    return mm(left, right, ((1,), (1,)))


def mm_tn(left, right):
    return mm(left, right, ((0,), (0,)))


def split_mm(left, right, nt=False):
    high = left.astype(BF16)
    low = (left - high.astype(F32)).astype(BF16)
    dot = mm_nt if nt else mm
    return dot(high, right) + dot(low, right)


def iota(shape, dim):
    return lax.broadcasted_iota(jnp.int32, shape, dim)


class Dims:
    def __init__(self, n, d, ff, slots, micro):
        self.n, self.d, self.ff = n, d, ff
        self.planes = n // PLANE
        self.rows = d // n
        self.rp = 8
        while self.rp < self.rows + 1:
            self.rp *= 2
        self.dp = n * self.rp
        self.rf = ff // n
        self.ffr = up(ff // PLANE, LANES)
        self.rfp = self.ffr // self.planes
        self.slots, self.micro = slots, micro
        self.tok = slots * micro
        self.heads = HEADS * HEAD_DIM
        self.kv = KV_HEADS * HEAD_DIM
        self.qkv = self.heads + 2 * self.kv
        self.wide = self.qkv + d
        self.rv = self.kv // n
        self.unit = PLANE * self.rows
        self.gs = 16 if self.unit % 16 == 0 else 8
        self.groups = self.unit // self.gs
        blocks = self.ffr // LANES
        first = blocks // 2 * LANES
        self.parts = ((0, first), (first, self.ffr - first))


def spread_matrix(dm):
    shape = (dm.d, dm.dp)
    row, col = iota(shape, 0), iota(shape, 1)
    inner = col & (dm.rp - 1)
    hit = (row == (col // dm.rp) * dm.rows + inner) & (inner < dm.rows)
    return jnp.where(hit, 1.0, 0.0).astype(BF16)


def field_matrix(dm, offset):
    shape = (LANES, dm.dp)
    row, col = iota(shape, 0), iota(shape, 1)
    inner = col & (dm.rp - 1)
    return jnp.where((row == offset + inner) & (inner < dm.rows), 1.0, 0.0).astype(BF16)


def own_block(dm):
    shape = (dm.n, dm.dp)
    return iota(shape, 1) // dm.rp == iota(shape, 0)


def spare_rows(dm):
    shape = (dm.n, dm.dp)
    return jnp.where(iota(shape, 1) == iota(shape, 0) * dm.rp + dm.rows, 1.0, 0.0).astype(BF16)


def value_field(dm):
    shape = (LANES, LANES)
    return jnp.where(
        iota(shape, 0) == 3 * FIELD + (iota(shape, 1) & (dm.rv - 1)), 1.0, 0.0
    ).astype(BF16)


def value_block(dm):
    shape = (dm.n, LANES)
    return iota(shape, 1) // dm.rv == iota(shape, 0)


def half_turn(field):
    width = field.shape[-1]
    first = (iota(field.shape, 1) & (HEAD_DIM - 1)) < HEAD_DIM // 2
    ahead = pltpu.roll(field, width - HEAD_DIM // 2, 1)
    behind = pltpu.roll(field, HEAD_DIM // 2, 1)
    return first, ahead, behind


def twice(field):
    low = iota(field.shape, 1) < HEAD_DIM
    turned = pltpu.roll(field, HEAD_DIM, 1)
    return jnp.where(low, field, turned), jnp.where(low, turned, field)


class Refs:
    def __init__(self, names, refs):
        self.__dict__.update(zip(names, refs, strict=True))


def layer_kernel(dm, names, *refs):
    b = Refs(names, refs)
    n, planes, rp = dm.n, dm.planes, dm.rp
    me = lax.axis_index("dp")
    r, p = me // PLANE, me % PLANE
    q, c = p // 2, p % 2
    other = 1 - c
    partner = r * PLANE + q * 2 + other

    def dev(plane, place):
        return (plane * PLANE + place,)

    barrier = pltpu.get_barrier_semaphore()
    peers = [dev(r, (p + k) % PLANE) for k in range(1, PLANE)]
    peers += [dev((r + k) % planes, p) for k in range(1, planes)]
    for peer in peers:
        pl.semaphore_signal(barrier, inc=1, device_id=peer, device_id_type=MESH)
    pl.semaphore_wait(barrier, len(peers))

    pending = []
    count = [0]

    def prepare(src, dst, arrive, to, cond=None, tag=None):
        copy = pltpu.make_async_remote_copy(
            src_ref=src,
            dst_ref=dst,
            send_sem=b.ssem.at[count[0]],
            recv_sem=arrive,
            device_id=to,
            device_id_type=MESH,
        )
        count[0] += 1
        pending.append((copy, cond, tag))
        return copy

    def send(src, dst, arrive, to, cond=None, tag=None):
        copy = prepare(src, dst, arrive, to, cond, tag)
        if cond is None:
            copy.start()
        else:
            pl.when(cond)(copy.start)

    def drain(tag=None):
        now = [item for item in pending if tag in (None, item[2])]
        for copy, cond, _ in now:
            if cond is None:
                copy.wait_send()
            else:
                pl.when(cond)(copy.wait_send)
        pending[:] = [item for item in pending if tag not in (None, item[2])]

    upper = r // max(planes // 2, 1)
    mirror = r + upper * (planes - 1 - 2 * r)

    def origin_of(k):
        spot = k - (mirror + planes - k) // planes
        return spot + upper * (planes - 1 - 2 * spot)

    def relay_own(src, dst, arrive, tag=None):
        send(src, dst, arrive, dev(r + 1, p), r + 1 < planes, tag)
        send(src, dst, arrive, dev(r - 1, p), r >= 1, tag)

    def onward(part, sems, k, tag=None):
        origin = origin_of(k)
        to = r - 1 + 2 * ((r - origin - 1 + planes) // planes)
        cond = (to >= 0) & (to < planes)
        piece, arrive = part(origin), sems.at[origin]
        return piece, arrive, cond, prepare(piece, piece, arrive, dev(to, p), cond, tag)

    def pass_on(piece, arrive, cond, copy):
        @pl.when(cond)
        def _():
            arrived(piece, arrive)
            copy.start()

    def settle(piece, arrive, cond, copy):
        pl.when(jnp.logical_not(cond))(lambda: arrived(piece, arrive))

    def arrived(dst, arrive):
        pltpu.make_async_remote_copy(
            src_ref=dst,
            dst_ref=dst,
            send_sem=b.ssem.at[0],
            recv_sem=arrive,
            device_id=(partner,),
            device_id_type=MESH,
        ).wait_recv()

    def block(ref, index):
        return ref.at[index // 2, index % 2]

    def plane_rows(ref, plane):
        return ref.at[pl.ds(plane * dm.groups, dm.groups)]

    keep = [
        pltpu.make_async_copy(b.ap, block(b.W, me), b.csem.at[0]),
        pltpu.make_async_copy(b.act.at[pl.ds(2 * p, 2)], b.fgu.at[p], b.csem.at[1]),
        pltpu.make_async_copy(b.g, b.gA.at[p], b.csem.at[2]),
        pltpu.make_async_copy(b.wds, b.WD.at[r], b.csem.at[3]),
    ]
    for i in (0, 2, 3):
        keep[i].start()

    relay_own(b.ap, block(b.W, me), b.rA.at[me])

    across, along = q + 1 - 2 * (q % 2), (q + 2) % CHIPS
    near = across * other + along * c
    next_to = along * other + across * c
    spots = (near, next_to, CHIPS - 1 - q)

    def fan(index, src):
        for where in (next_to, near):
            send(src, block(b.W, index), b.rA.at[index], dev(r, where * 2 + c))

    def spread_out(src, ref, arrive):
        for where in (next_to, near):
            send(src, ref.at[p], arrive.at[p], dev(r, where * 2 + c))
        send(src, ref.at[p], arrive.at[p], (partner,))

    def hand_on(ref, arrive, where):
        place = where * 2 + c
        arrived(ref.at[place], arrive.at[place])
        if where is near:
            send(ref.at[place], ref.at[place], arrive.at[place], dev(r, next_to * 2 + c))
        send(ref.at[place], ref.at[place], arrive.at[place], (partner,))

    fan(me, b.ap)
    send(b.ap, block(b.W, me), b.rA.at[me], (partner,))
    relay_own(b.wds, b.WD.at[r], b.rWD.at[r])

    lane = iota((dm.rows, LANES), 1)

    def shifted(read, at, width):
        low = at // LANES * LANES
        top = min(low + 2 * LANES, width)
        field = read(low, top).astype(F32)
        if at > low:
            field = pltpu.roll(field, top - at, 1)
        return field[:, :LANES]

    b.act[: 2 * PLANE] = jnp.zeros((2 * PLANE, rp, dm.ffr), BF16)
    for i, ref in enumerate((b.wg, b.wu)):
        for place in range(PLANE):
            for column in range(0, dm.ffr, LANES):
                plane, start = column // dm.rfp, column % dm.rfp
                filled, field = 0, jnp.zeros((dm.rows, LANES), F32)
                while filled < LANES:
                    real = dm.rf - start
                    if real > 0:
                        at = (plane * PLANE + place) * dm.rf + start
                        piece = shifted(lambda low, top: ref[:, low:top], at, dm.ff)
                        if filled:
                            piece = pltpu.roll(piece, filled, 1)
                        field = jnp.where((lane >= filled) & (lane < filled + real), piece, field)
                    filled += dm.rfp - start
                    plane, start = plane + 1, 0
                b.act[2 * place + i, : dm.rows, column : column + LANES] = field.astype(BF16)
    keep[1].start()
    for k in range(1, PLANE):
        to = (p + k) % PLANE
        send(b.act.at[pl.ds(2 * to, 2)], b.fgu.at[p], b.rGU.at[p], dev(r, to), tag="own")

    tok = dm.tok
    xf = b.x[...].astype(F32)
    scale1 = lax.rsqrt(jnp.mean(xf * xf, axis=-1, keepdims=True) + 1e-06)
    diagonal = iota((dm.slots, dm.slots), 0) == iota((dm.slots, dm.slots), 1)
    posc = [
        jnp.sum(jnp.where(diagonal, b.posr[m : m + 1].astype(F32), 0.0), axis=1, keepdims=True)
        for m in range(dm.micro)
    ]
    power = (iota((1, LANES), 1) & (HEAD_DIM // 2 - 1)).astype(F32) * (-2.0 / HEAD_DIM * ROTARY_LOG)
    angle = jnp.concatenate(posc, axis=0) * jnp.exp(power)
    b.tabs[0] = jnp.cos(angle)
    b.tabs[1] = jnp.sin(angle)
    b.spr[...] = spread_matrix(dm)

    for k in range(1, planes):
        origin = origin_of(k)
        index = origin * PLANE + p
        arrived(block(b.W, index), b.rA.at[index])
        to = r - 1 + 2 * ((r - origin - 1 + planes) // planes)
        send(block(b.W, index), block(b.W, index), b.rA.at[index], dev(to, p), (to >= 0) & (to < planes))
        fan(index, block(b.W, index))
        send(block(b.W, index), block(b.W, index), b.rA.at[index], (partner,))
    for k in range(1, PLANE):
        origin = (p + PLANE - k) % PLANE
        arrived(b.fgu.at[origin], b.rGU.at[origin])
    keep[1].wait()
    GU = [ref.reshape(dm.d, ref.shape[-1]) for ref in (b.GU0, b.GU1)]
    my_rows = pl.ds(pl.multiple_of(r * dm.unit, dm.gs), dm.unit)
    squeeze = b.spr[: dm.unit, : PLANE * rp]
    for h, (start, width) in enumerate(dm.parts):
        for i in range(2):
            piece = b.fgu[:, i, :, start : start + width].reshape(PLANE * rp, width)
            GU[h][my_rows, i * width : (i + 1) * width] = mm(squeeze, piece).astype(BF16)

    def gate_part(h):
        ref = (b.GU0, b.GU1)[h]
        return lambda plane: plane_rows(ref, plane)

    def down_part(plane):
        return b.WD.at[plane]

    relay_own(gate_part(0)(r), gate_part(0)(r), b.rGZ0.at[r], "gate0")
    steps = range(1, planes)
    down_on = [onward(down_part, b.rWD, k, "down") for k in steps]
    gate_on = [[onward(gate_part(h), sems, k, f"gate{h}") for k in steps] for h, sems in ((0, b.rGZ0), (1, b.rGZ1))]
    pass_on(*down_on[0])
    origins = [r, *(origin_of(k) for k in steps)]
    for i, where in enumerate(spots):
        for origin in origins:
            index = origin * PLANE + where * 2 + c
            arrived(block(b.W, index), b.rA.at[index])
            if i == 0:
                send(block(b.W, index), block(b.W, index), b.rA.at[index], dev(r, next_to * 2 + c))
            send(block(b.W, index), block(b.W, index), b.rA.at[index], (partner,))
    spread_out(b.g, b.gA, b.rG)
    for item in down_on[1:]:
        pass_on(*item)

    keep[0].wait()
    for k in range(CHIPS):
        for shift in range(planes):
            index = ((r + planes - shift) % planes) * PLANE + ((q + CHIPS - k) % CHIPS) * 2 + other
            arrived(block(b.W, index), b.rA.at[index])

    W = b.W.reshape(dm.dp, dm.wide)
    small = mm(spare_rows(dm), W[:, :LANES]).astype(BF16)
    mine = own_block(dm)
    rows8 = iota((8, dm.dp), 0)
    padded = jnp.zeros((8, dm.dp), F32)
    for i in range(3):
        piece = mm(small, field_matrix(dm, i * FIELD))
        piece = jnp.sum(jnp.where(mine, piece, 0.0), axis=0, keepdims=True)
        padded = jnp.where(rows8 == i, piece, padded)
    b.vec[...] = mm_nt(padded.astype(BF16), b.spr[...])
    gain1, bias_q, gain2 = b.vec[0:1], b.vec[1:2], b.vec[2:3]
    bias_v = jnp.sum(
        jnp.where(value_block(dm), mm(small, value_field(dm)), 0.0), axis=0, keepdims=True
    )
    bias_k = b.bkey[...].astype(F32)

    normed = (xf * scale1 * gain1).astype(BF16)
    b.npad[...] = mm(normed, b.spr[...]).astype(BF16)
    lin = mm(b.npad[...], W[:, : dm.qkv])
    turn_in = jnp.concatenate([lin[:, : dm.heads] + bias_q, lin[:, dm.heads : dm.heads + dm.kv] + bias_k], axis=1)
    reps = (dm.heads + dm.kv) // LANES
    cosine = jnp.concatenate([b.tabs[0]] * reps, axis=1)
    sine = jnp.concatenate([b.tabs[1]] * reps, axis=1)
    first, ahead, behind = half_turn(turn_in)
    turned = turn_in * cosine + jnp.where(first, -ahead, behind) * sine
    values = lin[:, dm.heads + dm.kv :] + bias_v
    for i, piece in enumerate(twice(turned[:, dm.heads :])):
        b.kd[i] = piece.astype(BF16)
    for i, piece in enumerate(twice(values)):
        b.vd[i] = piece.astype(BF16)
    low = iota((dm.slots, LANES), 1) < HEAD_DIM

    def stack_heads(field, store):
        for h in range(HEADS):
            part = field[:, LANES * (h // 2) : LANES * (h // 2) + LANES]
            part = jnp.where(low if h % 2 == 0 else ~low, part, 0.0)
            store(h)[...] = part.astype(BF16)

    span = GROUP * dm.slots
    mix = b.oP.at[0, 0]
    BIG = b.BIG.reshape(dm.dp, 4 * dm.ffr)
    dms = [BIG.at[:span, dm.wide + kv * LANES : dm.wide + (kv + 1) * LANES] for kv in range(KV_HEADS)]

    def head_rows(h):
        return dms[h // GROUP].at[(h % GROUP) * dm.slots : (h % GROUP + 1) * dm.slots]

    for m in range(dm.micro):
        here = slice(m * dm.slots, (m + 1) * dm.slots)
        stack_heads(turned[here, : dm.heads], lambda h: b.QS.at[m, h * dm.slots : (h + 1) * dm.slots])
        grid = (dm.slots, dm.slots)
        start_row = iota((dm.slots, 1), 0).astype(F32) - posc[m]
        start_col = (iota((1, dm.slots), 1) - b.posr[m : m + 1]).astype(F32)
        allowed = (start_row == start_col) & (iota(grid, 1) <= iota(grid, 0))
        for kv in range(KV_HEADS):
            rows = slice(kv * span, (kv + 1) * span)
            score = mm_nt(b.QS[m, rows], b.kd[kv, here]) * 0.125
            score = jnp.where(allowed[None], score.reshape(GROUP, *grid), -1e30)
            top = jnp.max(score, axis=-1, keepdims=True)
            expo = jnp.exp(score - top)
            prob = expo / jnp.sum(expo, axis=-1, keepdims=True)
            prob = prob.reshape(span, dm.slots)
            b.PF[m, rows] = prob
            dms[kv][...] = mm(prob.astype(BF16), b.vd[kv, here]).astype(BF16)
        for t in range(HEADS // 2):
            even, odd = head_rows(2 * t)[...], head_rows(2 * t + 1)[...]
            mix[here, t * LANES : (t + 1) * LANES] = jnp.where(low, even, odd)
    b.mpad[...] = mm(mix[...], b.spr[...]).astype(BF16)
    hidden = xf + mm(b.mpad[...], W[:, dm.qkv :])
    b.hid[...] = hidden
    scale2 = lax.rsqrt(jnp.mean(hidden * hidden, axis=-1, keepdims=True) + 1e-06)
    nf = (hidden * scale2 * gain2).astype(BF16)
    b.nfA[p] = nf

    spread_out(b.nfA.at[p], b.nfA, b.rNF)
    pass_on(*gate_on[0][0])
    hand_on(b.gA, b.rG, near)
    for item in gate_on[0][1:]:
        pass_on(*item)
    relay_own(gate_part(1)(r), gate_part(1)(r), b.rGZ1.at[r], "gate1")
    hand_on(b.nfA, b.rNF, near)
    pass_on(*gate_on[1][0])
    for where in spots[1:]:
        hand_on(b.gA, b.rG, where)
    for where in spots[1:]:
        hand_on(b.nfA, b.rNF, where)
    for item in gate_on[1][1:]:
        pass_on(*item)
    for item in (*down_on, *gate_on[0]):
        settle(*item)
    keep[2].wait()
    keep[3].wait()
    for k in range(CHIPS):
        place = ((q + CHIPS - k) % CHIPS) * 2 + other
        arrived(b.gA.at[place], b.rG.at[place])
        arrived(b.nfA.at[place], b.rNF.at[place])

    ACT = b.act.reshape(PLANE * tok, dm.ffr)
    WD = b.WD.reshape(dm.ffr, dm.d)
    half = PLANE // 2

    base = (0, 4 * dm.parts[0][1])

    def feed(h, place_q, place_c):
        place = place_q * 2 + place_c
        start, width = dm.parts[h]
        nf_t, g_t = b.nfA[place], b.gA[place]
        down = WD[start : start + width]
        pre = mm(nf_t, GU[h][...])
        gate, upper = pre[:, :width], pre[:, width:]
        sigma = jax.nn.sigmoid(gate)
        silu = gate * sigma
        act = (silu * upper).astype(BF16)
        ACT[pl.ds(pl.multiple_of(place * tok, tok), tok), start : start + width] = act
        d_act = mm_nt(g_t, down)
        d_gate = (d_act * upper * (sigma + silu * (1.0 - sigma))).astype(BF16)
        d_up = (d_act * silu).astype(BF16)
        d_both = jnp.concatenate([d_gate, d_up], axis=1)
        rows = pl.ds(pl.multiple_of((place % half) * tok, tok), tok)
        cols = pl.ds(pl.multiple_of(base[h] + (place // half) * 2 * width, LANES), 2 * width)
        BIG[rows, cols] = d_both
        for ref, value in ((b.oP, mm(act, down)), (b.dP, mm_nt(d_both, GU[h][...]))):
            if h:
                value = value + ref[place_q, place_c].astype(F32)
            ref[place_q, place_c] = value.astype(BF16)

    def first_copy(where, part, landing, sems, arrive):
        return pltpu.make_async_remote_copy(
            src_ref=part.at[where, other],
            dst_ref=landing.at[where],
            send_sem=sems.at[where],
            recv_sem=arrive.at[where],
            device_id=(partner,),
            device_id_type=MESH,
        )

    diag = CHIPS - 1 - q
    routes = ((diag, near), (near, near), (next_to, next_to))

    def second_copy(slot, part, landing, sems, arrive):
        source, to = routes[slot]
        return pltpu.make_async_remote_copy(
            src_ref=part.at[source, c],
            dst_ref=landing.at[slot],
            send_sem=sems.at[slot],
            recv_sem=arrive.at[slot],
            device_id=dev(r, to * 2 + c),
            device_id_type=MESH,
        )

    def add_on(part, landing, sems, arrive):
        arrived(landing.at[0], arrive.at[0])
        part[next_to, c] = (part[next_to, c].astype(F32) + landing[0].astype(F32)).astype(BF16)
        second_copy(2, part, landing, sems, arrive).start()

    d_route = (b.dP, b.dR2, b.dsem2, b.rD2)
    o_route = (b.oP, b.oR2, b.osem2, b.rO2)

    def hop(part, landing, arrive, to, cond):
        ahead = (to - r - 1 + planes) // planes
        beyond = r - to - 1 + 2 * planes * ahead
        last = 1 - (beyond + 4 * planes - 1) // (4 * planes)
        slot = to + (planes - to) * last
        send(part(to), landing.at[slot], arrive.at[slot], dev(r - 1 + 2 * ahead, p), cond)

    def behind_of(to):
        ahead = (to - r - 1 + planes) // planes
        follows = r + 1 - 2 * ahead
        return (follows >= 0) & (follows < planes)

    far = [origin_of(planes - k) for k in range(1, planes)]

    def chain_start(part, landing, arrive):
        for to in far:
            hop(part, landing, arrive, to, jnp.logical_not(behind_of(to)))

    def chain_step(part, landing, arrive, k):
        to = far[k]
        has = behind_of(to)

        @pl.when(has)
        def _():
            arrived(landing.at[to], arrive.at[to])
            mine = part(to)
            mine[...] = (mine[...].astype(F32) + landing[to].astype(F32)).astype(BF16)

        hop(part, landing, arrive, to, has)

    def chain_end(total, landing, arrive):
        for slot, cond in ((r, r >= 1), (planes, r + 1 < planes)):

            @pl.when(cond)
            def _():
                arrived(landing.at[slot], arrive.at[slot])
                total[...] = (total[...].astype(F32) + landing[slot].astype(F32)).astype(total.dtype)

    nf_all = b.nfA.reshape(PLANE * tok, dm.d)
    g_all = b.gA.reshape(PLANE * tok, dm.d)
    wide_rows = half * tok
    chunk = 2 * LANES

    def gate_grad(h):
        width = dm.parts[h][1]

        def some(start, count):
            cols = pl.ds(start, count)
            total = mm_tn(nf_all[:wide_rows, cols], BIG[:, base[h] : base[h] + 2 * width])
            total = total + mm_tn(nf_all[wide_rows:, cols], BIG[:, base[h] + 2 * width : base[h] + 4 * width])
            GU[h][cols, :] = total.astype(BF16)

        @pl.loop(0, dm.d // chunk)
        def _(i):
            some(pl.multiple_of(i * chunk, chunk), chunk)

        if dm.d % chunk:
            some(dm.d - dm.d % chunk, dm.d % chunk)

    drain("own")
    @pl.loop(0, PLANE)
    def _(turn):
        feed(0, turn // 2, turn % 2)

    drain("gate0")
    gate_grad(0)
    chain_start(gate_part(0), b.zR0, b.rZ0)
    for item in gate_on[1]:
        settle(*item)

    def join(where):
        for part, one, arrive in ((b.dP, b.dR1, b.rD1), (b.oP, b.oR1, b.rO1)):
            arrived(one.at[where], arrive.at[where])
            part[where, c] = (part[where, c].astype(F32) + one[where].astype(F32)).astype(BF16)

    @pl.loop(0, CHIPS)
    def _(step):
        one, two = (CHIPS - 1 - step) % 2, (CHIPS - 1 - step) // 2
        over_x, over_y = one * other + two * c, two * other + one * c
        where = 2 * ((q // 2 + over_y) % 2) + (q % 2 + over_x) % 2

        @pl.loop(0, 2)
        def _(turn):
            feed(1, where, (other + turn) % 2)

            @pl.when(turn == 0)
            def _():
                first_copy(where, b.dP, b.dR1, b.dsem, b.rD1).start()
                first_copy(where, b.oP, b.oR1, b.osem, b.rO1).start()

            for at, late, source in ((1, 0, diag), (2, 1, near)):

                @pl.when((step == at) & (turn == late))
                def _():
                    join(source)
                    second_copy(at - 1, *d_route).start()

    join(next_to)
    add_on(*d_route)
    for slot in range(2):
        second_copy(slot, *o_route).start()
    join(q)

    def attn_part(plane):
        return b.aR2.at[0, plane]

    drain("down")
    WD[...] = mm_tn(ACT[...], g_all[...]).astype(BF16)
    chain_start(down_part, b.zD, b.rW)
    drain("gate1")
    gate_grad(1)
    chain_start(gate_part(1), b.zR1, b.rZ1)
    for k in range(planes - 1):
        chain_step(gate_part(0), b.zR0, b.rZ0, k)
    add_on(*o_route)
    d_nf = b.dP[q, c].astype(F32)
    for slot in (1, 2):
        arrived(b.dR2.at[slot], b.rD2.at[slot])
        d_nf = d_nf + b.dR2[slot].astype(F32)
    hidden = b.hid[...]
    scale2 = lax.rsqrt(jnp.mean(hidden * hidden, axis=-1, keepdims=True) + 1e-06)

    def norm_back(grad, field, scale, gain):
        weighted = grad * gain
        d_gain = jnp.sum(grad * field * scale, axis=0, keepdims=True)
        d_field = weighted * scale - field * (scale * scale * scale) * jnp.mean(
            weighted * field, axis=-1, keepdims=True
        )
        return d_gain, d_field

    d_gain2, d_part = norm_back(d_nf, hidden, scale2, b.vec[2:3])
    d_hidden = b.g[...].astype(F32) + d_part
    b.dhid[...] = d_hidden
    d_attn = d_hidden.astype(BF16)
    chain_step(down_part, b.zD, b.rW, 0)
    BIG[:, dm.qkv : dm.wide] = mm_tn(b.mpad[...], d_attn).astype(BF16)
    d_mixed = mm_nt(d_attn, W[:, dm.qkv :]).astype(BF16)
    d_mixed = mm_nt(d_mixed, b.spr[...])
    d_values = []
    for m in range(dm.micro):
        here = slice(m * dm.slots, (m + 1) * dm.slots)
        stack_heads(d_mixed[here], head_rows)
        d_v, d_k = [], []
        for kv in range(KV_HEADS):
            rows = slice(kv * span, (kv + 1) * span)
            d_mix, prob, qs = dms[kv][...], b.PF[m, rows], b.QS[m, rows]
            d_v.append(mm_tn(prob.astype(BF16), d_mix))
            d_prob = mm_nt(d_mix, b.vd[kv, here])
            delta = jnp.sum(d_prob * prob, axis=-1, keepdims=True)
            d_score = (prob * (d_prob - delta)).astype(BF16)
            d_k.append(0.125 * mm_tn(d_score, qs))
            b.PF[m, rows] = 0.125 * mm(d_score, b.kd[kv, here])
        for t in range(HEADS // 2):
            even = b.PF[m, 2 * t * dm.slots : (2 * t + 1) * dm.slots]
            odd = b.PF[m, (2 * t + 1) * dm.slots : (2 * t + 2) * dm.slots]
            b.FQ[here, t * LANES : (t + 1) * LANES] = jnp.where(low, even, odd)

        def joined(pair):
            zero, one = (piece + pltpu.roll(piece, HEAD_DIM, 1) for piece in pair)
            return jnp.where(low, zero, one)

        b.FQ[here, dm.heads : dm.heads + dm.kv] = joined(d_k)
        d_values.append(joined(d_v))
    d_turned = b.FQ[...]
    cosine = jnp.concatenate([b.tabs[0]] * reps, axis=1)
    sine = jnp.concatenate([b.tabs[1]] * reps, axis=1)
    first, ahead, behind = half_turn(d_turned * sine)
    d_lin = (d_turned * cosine + jnp.where(first, ahead, -behind)).astype(BF16)
    d_lin = jnp.concatenate([d_lin, jnp.concatenate(d_values, axis=0).astype(BF16)], axis=1)
    BIG[:, : dm.qkv] = mm_tn(b.npad[...], d_lin).astype(BF16)
    d_bias = jnp.sum(d_lin.astype(F32), axis=0, keepdims=True)
    d_normed = split_mm(mm_nt(d_lin, W[:, : dm.qkv]), b.spr[...], nt=True)
    xf = b.x[...].astype(F32)
    scale1 = lax.rsqrt(jnp.mean(xf * xf, axis=-1, keepdims=True) + 1e-06)
    d_gain1, d_part = norm_back(d_normed, xf, scale1, b.vec[0:1])
    b.gin[...] = (b.dhid[...] + d_part).astype(BF16)

    rows8 = iota((8, dm.d), 0)
    packed = jnp.zeros((8, dm.d), F32)
    for i, piece in enumerate((d_gain1, d_bias[:, : dm.heads], d_gain2)):
        packed = jnp.where(rows8 == i, piece, packed)
    packed = split_mm(packed, b.spr[...])
    mine = own_block(dm)
    spare = jnp.zeros((n, LANES), F32)
    for i in range(3):
        piece = jnp.where(mine, packed[i : i + 1], 0.0).astype(BF16)
        spare = spare + mm_nt(piece, field_matrix(dm, i * FIELD))
    piece = jnp.where(value_block(dm), d_bias[:, dm.heads + dm.kv :], 0.0).astype(BF16)
    spare = spare + mm_nt(piece, value_field(dm))
    key_bias = jnp.broadcast_to(d_bias[:, dm.heads : dm.heads + dm.kv], (n, LANES))
    spare = jnp.concatenate([spare, key_bias], axis=1).astype(BF16)
    BIG[:, : 2 * LANES] = (
        BIG[:, : 2 * LANES].astype(F32) + mm_tn(spare_rows(dm), spare)
    ).astype(BF16)

    cols = pl.ds(0, dm.wide)

    def quad(plane):
        return pl.ds(plane * CHIPS, CHIPS)

    for to in (*far, r):
        send(b.BIG.at[quad(to), other, :, cols], b.aR1.at[quad(to)], b.rA1.at[to], (partner,))
    for to in (*far, r):
        arrived(b.aR1.at[quad(to)], b.rA1.at[to])
        mine_now = b.BIG[quad(to), c, :, cols].astype(F32) + b.aR1[quad(to)].astype(F32)
        b.aR1[quad(to)] = mine_now.astype(BF16)
        send(b.aR1.at[to * CHIPS + diag], b.aR2.at[0, to], b.rA2.at[0, to], dev(r, near * 2 + c))
    for to in (*far, r):
        send(b.aR1.at[to * CHIPS + near], b.aR2.at[1, to], b.rA2.at[1, to], dev(r, near * 2 + c))
    for k in range(1, planes - 1):
        chain_step(down_part, b.zD, b.rW, k)
    chain_step(gate_part(1), b.zR1, b.rZ1, 0)
    for to in (*far, r):
        arrived(b.aR2.at[0, to], b.rA2.at[0, to])
        piece = b.aR1.at[to * CHIPS + next_to]
        piece[...] = (piece[...].astype(F32) + b.aR2[0, to].astype(F32)).astype(BF16)
        send(piece, b.aR2.at[2, to], b.rA2.at[2, to], dev(r, next_to * 2 + c))
    for k in range(1, planes - 2):
        chain_step(gate_part(1), b.zR1, b.rZ1, k)
    total = b.hid[...] + b.oP[q, c].astype(F32)
    for slot in (1, 2):
        arrived(b.oR2.at[slot], b.rO2.at[slot])
        total = total + b.oR2[slot].astype(F32)
    b.out[...] = total.astype(BF16)
    for to in (*far, r):
        total = b.aR1[to * CHIPS + q].astype(F32)
        for slot in (1, 2):
            arrived(b.aR2.at[slot, to], b.rA2.at[slot, to])
            total = total + b.aR2[slot, to].astype(F32)
        b.aR2[0, to] = total.astype(BF16)
    chain_start(attn_part, b.aR3, b.rA3)
    squeeze = b.spr[: dm.unit, : PLANE * rp]

    def home(h, landing, arrive, final):
        start, width = dm.parts[h]
        cols = pl.ds(start, width)
        chain_end(gate_part(h)(r), landing, arrive)
        for i in range(2):
            piece = mm_tn(squeeze, GU[h][my_rows, i * width : (i + 1) * width]).astype(BF16)
            piece = piece.reshape(PLANE, rp, width)
            for place in range(PLANE):
                b.act[2 * place + i, :, cols] = piece[place]
        for k in range(1, PLANE):
            to = (p + k) % PLANE
            send(b.act.at[pl.ds(2 * to, 2), :, cols], b.fgu.at[p, :, :, cols], final.at[p], dev(r, to))
        b.fgu[p, :, :, cols] = b.act[pl.ds(2 * p, 2), :, cols]

    home(0, b.zR0, b.rZ0, b.rF0)
    chain_step(gate_part(1), b.zR1, b.rZ1, planes - 2)
    home(1, b.zR1, b.rZ1, b.rF1)
    for k in range(planes - 1):
        chain_step(attn_part, b.aR3, b.rA3, k)
    sums = b.hid.at[: dm.rfp]
    sums[...] = b.WD[r].astype(F32)
    chain_end(sums, b.zD, b.rW)

    def lay_flat(flat, field):
        blocks = field.shape[1] // LANES
        for j in range(blocks):
            flat[pl.ds(j, field.shape[0], stride=blocks), :] = field[:, j * LANES : (j + 1) * LANES]

    lay_flat(b.fd, sums[: dm.rf])
    for k in range(1, PLANE):
        origin = (p + PLANE - k) % PLANE
        for (start, width), final in zip(dm.parts, (b.rF0, b.rF1)):
            arrived(b.fgu.at[origin, :, :, pl.ds(start, width)], final.at[origin])
    blocks = dm.ff // LANES

    def window(i, run, start):
        place = run % PLANE
        return shifted(lambda low, top: b.fgu[place, i, :, low:top], run // PLANE * dm.rfp + start, dm.ffr)

    lane = iota((rp, LANES), 1)
    for i, flat in enumerate((b.fg, b.fu)):
        for j in range(blocks):
            run, start = (j * LANES) // dm.rf, (j * LANES) % dm.rf
            field = window(i, run, start)
            left = dm.rf - start
            while left < LANES:
                run += 1
                nxt = window(i, run, 0)
                field = jnp.where(lane < left, field, pltpu.roll(nxt, left, 1))
                left += dm.rf
            flat[pl.ds(j, dm.rows, stride=blocks), :] = field[: dm.rows]

    b.fa[...] = b.aR2[0, r].astype(F32)
    chain_end(b.fa, b.aR3, b.rA3)
    own_rows = b.fa[: dm.rows]
    h, kv = dm.heads, dm.kv
    lay_flat(b.fq, own_rows[:, :h])
    b.fk[...] = own_rows[:, h : h + kv]
    b.fv[...] = own_rows[:, h + kv : h + 2 * kv]
    lay_flat(b.fo, own_rows[:, h + 2 * kv :])
    b.fs[...] = b.fa[dm.rows : dm.rows + 1, : 2 * LANES]
    for where in range(CHIPS):
        first_copy(where, b.oP, b.oR1, b.osem, b.rO1).wait_send()
        first_copy(where, b.dP, b.dR1, b.dsem, b.rD1).wait_send()
    for slot in range(CHIPS - 1):
        second_copy(slot, *o_route).wait_send()
        second_copy(slot, *d_route).wait_send()
    drain()


def run_layer(dm, operands):
    n, planes, rp, tok = dm.n, dm.planes, dm.rp, dm.tok
    vm = pltpu.VMEM
    sem = pltpu.SemaphoreType.DMA
    quads = planes * CHIPS
    pairs = dm.heads + dm.kv
    outs = {
        "out": jax.ShapeDtypeStruct((tok, dm.d), BF16),
        "gin": jax.ShapeDtypeStruct((tok, dm.d), BF16),
        "fq": jax.ShapeDtypeStruct((dm.rows * dm.heads // LANES, LANES), F32),
        "fk": jax.ShapeDtypeStruct((dm.rows, LANES), F32),
        "fv": jax.ShapeDtypeStruct((dm.rows, LANES), F32),
        "fo": jax.ShapeDtypeStruct((dm.rows * dm.d // LANES, LANES), F32),
        "fs": jax.ShapeDtypeStruct((1, 2 * LANES), F32),
        "fg": jax.ShapeDtypeStruct((dm.rows * dm.ff // LANES, LANES), F32),
        "fu": jax.ShapeDtypeStruct((dm.rows * dm.ff // LANES, LANES), F32),
        "fd": jax.ShapeDtypeStruct((dm.rf * dm.d // LANES, LANES), F32),
    }
    n_sends = 1 + (planes - 1) * 16 + 16 * PLANE + 8 * quads + 64
    scratch = {
        "W": vm((quads, 2, rp, dm.wide), BF16),
        "GU0": vm((planes * dm.groups, dm.gs, 2 * dm.parts[0][1]), BF16),
        "GU1": vm((planes * dm.groups, dm.gs, 2 * dm.parts[1][1]), BF16),
        "WD": vm((planes, dm.rfp, dm.d), BF16),
        "nfA": vm((PLANE, tok, dm.d), BF16),
        "gA": vm((PLANE, tok, dm.d), BF16),
        "act": vm((PLANE * tok // rp, rp, dm.ffr), BF16),
        "BIG": vm((quads, 2, rp, 4 * dm.ffr), BF16),
        "oP": vm((CHIPS, 2, tok, dm.d), BF16),
        "dP": vm((CHIPS, 2, tok, dm.d), BF16),
        "oR1": vm((CHIPS, tok, dm.d), BF16),
        "dR1": vm((CHIPS, tok, dm.d), BF16),
        "oR2": vm((CHIPS - 1, tok, dm.d), BF16),
        "dR2": vm((CHIPS - 1, tok, dm.d), BF16),
        "zR0": vm((planes + 1, dm.groups, dm.gs, 2 * dm.parts[0][1]), BF16),
        "zR1": vm((planes + 1, dm.groups, dm.gs, 2 * dm.parts[1][1]), BF16),
        "zD": vm((planes + 1, dm.rfp, dm.d), BF16),
        "aR1": vm((quads, rp, dm.wide), BF16),
        "aR2": vm((CHIPS - 1, planes, rp, dm.wide), BF16),
        "aR3": vm((planes + 1, rp, dm.wide), BF16),
        "QS": vm((dm.micro, HEADS * dm.slots, LANES), BF16),
        "PF": vm((dm.micro, HEADS * dm.slots, dm.slots), F32),
        "hid": vm((tok, dm.d), F32),
        "fa": vm((rp, dm.wide), F32),
        "fgu": vm((PLANE, 2, rp, dm.ffr), BF16),
        "dhid": vm((tok, dm.d), F32),
        "npad": vm((tok, dm.dp), BF16),
        "mpad": vm((tok, dm.dp), BF16),
        "spr": vm((dm.d, dm.dp), BF16),
        "kd": vm((KV_HEADS, tok, LANES), BF16),
        "vd": vm((KV_HEADS, tok, LANES), BF16),
        "FQ": vm((tok, pairs), F32),
        "tabs": vm((2, tok, LANES), F32),
        "vec": vm((8, dm.d), F32),
        "ssem": sem((n_sends,)),
        "csem": sem((4,)),
        "osem": sem((CHIPS,)),
        "dsem": sem((CHIPS,)),
        "osem2": sem((CHIPS - 1,)),
        "dsem2": sem((CHIPS - 1,)),
        "rA": sem((n,)),
        "rGU": sem((PLANE,)),
        "rGZ0": sem((planes,)),
        "rGZ1": sem((planes,)),
        "rG": sem((PLANE,)),
        "rWD": sem((planes,)),
        "rNF": sem((PLANE,)),
        "rO1": sem((CHIPS,)),
        "rD1": sem((CHIPS,)),
        "rO2": sem((CHIPS - 1,)),
        "rD2": sem((CHIPS - 1,)),
        "rZ0": sem((planes + 1,)),
        "rZ1": sem((planes + 1,)),
        "rF0": sem((PLANE,)),
        "rF1": sem((PLANE,)),
        "rW": sem((planes + 1,)),
        "rA1": sem((planes,)),
        "rA2": sem((CHIPS - 1, planes)),
        "rA3": sem((planes + 1,)),
    }
    return pl.pallas_call(
        functools.partial(layer_kernel, dm, (*operands, *outs, *scratch)),
        name="layer",
        out_shape=list(outs.values()),
        in_specs=[pl.BlockSpec(memory_space=pltpu.VMEM)] * len(operands),
        out_specs=[pl.BlockSpec(memory_space=pltpu.VMEM)] * len(outs),
        scratch_shapes=list(scratch.values()),
        compiler_params=pltpu.CompilerParams(
            collective_id=0, has_side_effects=True, vmem_limit_bytes=67043328
        ),
    )(*operands.values())


def per_device(n, *args):
    (
        tokens,
        positions,
        cotangent,
        norm_attn,
        w_query,
        b_query,
        w_key,
        b_key,
        w_value,
        b_value,
        w_out,
        norm_ffn,
        w_gate,
        w_up,
        w_down,
    ) = args
    micro, slots, d = tokens.shape
    dm = Dims(n, d, w_gate.shape[0] * n // d, slots, micro)
    rows, rp = dm.rows, dm.rp

    def lanes(vector):
        return jnp.pad(vector, (0, FIELD - vector.shape[0]))

    spare = jnp.concatenate([lanes(v) for v in (norm_attn, b_query, norm_ffn, b_value)])
    spare = jnp.pad(spare, (0, dm.wide - spare.shape[0]))
    pack = jnp.concatenate(
        [w.reshape(rows, -1) for w in (w_query, w_key, w_value, w_out)], axis=1
    )
    pack = jnp.concatenate([pack, spare[None]], axis=0)
    pack = jnp.pad(pack, ((0, rp - rows - 1), (0, 0)))

    down = jnp.pad(w_down.reshape(dm.rf, d), ((0, dm.rfp - dm.rf), (0, 0)))
    operands = {
        "x": tokens.reshape(dm.tok, d),
        "g": cotangent.reshape(dm.tok, d),
        "posr": positions,
        "bkey": b_key[None],
        "ap": pack,
        "wg": w_gate.reshape(rows, dm.ff),
        "wu": w_up.reshape(rows, dm.ff),
        "wds": down,
    }
    out, gin, fq, fk, fv, fo, fs, fg, fu, fd = run_layer(dm, operands)

    def field(i, size):
        return fs[0, i * FIELD : i * FIELD + size]

    return (
        out.reshape(micro, slots, d),
        gin.reshape(micro, slots, d),
        field(0, rows),
        fq.reshape(-1),
        field(1, rows),
        fk.reshape(-1),
        fs[0, LANES : LANES + dm.kv],
        fv.reshape(-1),
        field(3, dm.rv),
        fo.reshape(-1),
        field(2, rows),
        fg.reshape(-1),
        fu.reshape(-1),
        fd.reshape(-1),
    )


def solution(mesh):
    n = mesh.shape["dp"]
    split, row = P("dp"), P(None, "dp", None)
    in_specs = (row, P(None, "dp"), row, *[split] * 4, P(), *[split] * 7)
    out_specs = (row, row, *[split] * 4, P(), *[split] * 7)
    return jax.shard_map(
        functools.partial(per_device, n),
        mesh=mesh,
        in_specs=in_specs,
        out_specs=out_specs,
        check_vma=False,
    )
```
